128 devices in a mesh: mem: 4 (over z_lo, core), lat: 8 (over y, z_hi), lon: 4 (over x).
Axes of the slice: x: 4, y: 4, z: 4 (z_hi: 2, z_lo: 2; z = z_hi * 2 + z_lo), core: 2. Of those that a mesh axis runs over, the one named last changes fastest.
Arguments:
- perturbations: bfloat16 [16, 8, 512, 1024], P('mem', None, 'lat', 'lon'), may hold values from -6 to 6
- increment: float32 [8, 512, 1024], P(None, 'lat', 'lon'), may hold values from -6 to 6
- taper_norm: float32 [8, 512, 1024], P(None, 'lat', 'lon'), may hold values from 1.5 to 6
- kappa: float32 [8], replicated, may hold values from 0.3 to 8
Outputs:
- covariance_product: float32 [8, 512, 1024], P('mem', 'lat', 'lon')
The draws below stay inside these ranges and needn't reach their ends.
All inputs are finite; a program needn't handle non-finite values.
Results may differ from the reference program's by a relative error of at most 0.0003.
Values may be sent and summed in bfloat16 or wider, within the bound.
No kernel may reach another device: no remote copies, remote signals or barrier semaphores. Data moves between devices by JAX's collectives and lax.ppermute only.
A program may use at most 64 MiB of HBM per device.

```python
import math
import jax
import jax.numpy as jnp
from jax import lax

LEV = 8
PASSES = 4
SWEEPS = 2
MEMBERS = 16
NLAT = 512
NLON = 1024


def steps_of(rng, extent, split, least, largest):
    def one(dim, blocks):
        draws = jax.random.uniform(jax.random.fold_in(jax.random.fold_in(rng, 6), dim), (blocks,), jnp.float32, least / len(split), largest / len(split))
        return jnp.repeat(jnp.exp(draws), extent[dim] // blocks).reshape((-1,) + (1,) * (len(extent) - dim - 1))

    factor_of = one(*split[0])
    for cut in split[1:]:
        factor_of = factor_of * one(*cut)
    return factor_of


def centred(own_key, dims, deviation, reach, pieces=(), dtype=jnp.bfloat16):
    array = deviation * jax.random.normal(own_key, dims, jnp.float32)
    if pieces:
        array = array * steps_of(own_key, dims, pieces, -0.22, 0.18)
    return jnp.clip(array, -reach, reach).astype(dtype)


def setup_inputs(seed: int = 0) -> dict:
    streams_of = jax.random.split(jax.random.key(seed), 5)
    return {
        "perturbations": centred(streams_of[0], (MEMBERS, LEV, NLAT, NLON), 1.0, 6.0, ((0, 4), (2, 8), (3, 4))),
        "increment": centred(streams_of[1], (LEV, NLAT, NLON), 1.0, 6.0, ((1, 8), (2, 4)), jnp.float32),
        "taper_norm": jnp.clip(jnp.exp(math.log(6.0) - 1.3862944 * jax.random.uniform(streams_of[2], (LEV, NLAT, NLON), jnp.float32) ** steps_of(streams_of[2], (LEV, NLAT, NLON), ((1, 8), (2, 4)), -0.2, 0.2)), 1.5, 6.0),
        "kappa": jnp.clip(jnp.exp(jax.random.uniform(streams_of[3], (LEV,), jnp.float32, math.log(0.3), math.log(8.0))), 0.3, 8.0),
    }


def relax_whole(source, field, weight):
    padded = jnp.pad(field, ((0, 0), (1, 1), (0, 0)))
    padded = jnp.concatenate([padded[:, :, -1:], padded, padded[:, :, :1]], axis=2)
    beside_all = padded[:, 2:, 1:-1] + padded[:, :-2, 1:-1] + padded[:, 1:-1, 2:] + padded[:, 1:-1, :-2]
    return (source + weight * beside_all) / (1.0 + 4.0 * weight)


def diffuse_whole(field, weight):
    for turn in range(2 * PASSES):
        result = field
        for sweep in range(SWEEPS):
            result = relax_whole(field, result, weight)
        field = result
    return field


def reference(perturbations, increment, taper_norm, kappa):
    weight = kappa[:, None, None]

    def add_member(total, member):
        values = member.astype(jnp.float32)
        spread = taper_norm * (values * increment)
        tapered = taper_norm * diffuse_whole(spread, weight)
        return total + values * tapered, None

    total, unused = lax.scan(add_member, jnp.zeros(increment.shape, jnp.float32), perturbations)
    return total / (MEMBERS - 1)
```

```python
import jax
import jax.numpy as jnp
from jax import lax
from jax.experimental import pallas as pl
from jax.experimental.pallas import tpu as pltpu
from jax.sharding import PartitionSpec as P

PASSES = 8
HALO = 16
LANES = 128
MEMBER_GROUP = 2
ROW_GROUP = 4


def roll(x, shift):
    shift = shift % LANES
    return pltpu.roll(x, shift, x.ndim - 1) if shift else x


def lane_of(shape):
    return lax.broadcasted_iota(jnp.int32, shape, len(shape) - 1)


def split_g(increment, taper):
    g = increment * taper
    hi = g.astype(jnp.bfloat16)
    return hi, (g - hi.astype(jnp.float32)).astype(jnp.bfloat16)


def pack_kernel(p, increment, taper, up, down, to_left, to_right):
    members, _, rows, cols = p.shape

    def edge(ref_rows, out):
        for m in range(members):
            out[m] = p[m, :, ref_rows, :]
        hi, lo = split_g(increment[:, ref_rows, :], taper[:, ref_rows, :])
        out[members] = hi
        out[members + 1] = lo

    edge(slice(0, HALO), up)
    edge(slice(rows - HALO, rows), down)

    def packed(pick, column, shift):
        fields = [p[m, :, pick, column].astype(jnp.float32) for m in range(members)]
        hi, lo = split_g(increment[:, pick, column], taper[:, pick, column])
        fields += [hi.astype(jnp.float32), lo.astype(jnp.float32)]
        lane = lane_of(fields[0].shape)
        total = jnp.zeros_like(fields[0])
        for e, field in enumerate(fields):
            inside = (lane >= HALO * e) & (lane < HALO * (e + 1))
            total = jnp.where(inside, roll(field, shift + HALO * e), total)
        return total.astype(jnp.bfloat16)

    def chunk(i, _):
        pick = pl.ds(pl.multiple_of(i * HALO, HALO), HALO)
        to_left[:, pick, :] = packed(pick, slice(0, LANES), 0)
        to_right[:, pick, :] = packed(pick, slice(cols - LANES, cols), HALO)
        return 0

    lax.fori_loop(0, rows // HALO, chunk, 0)


def windows(first, second, left, right):
    lane = lane_of(first.shape)
    return (
        jnp.where(lane < HALO, left, roll(first, HALO)),
        jnp.where(lane < 64, roll(first, 64), roll(second, 64)),
        jnp.where(lane >= LANES - HALO, right, roll(second, -HALO)),
    )


def turned(x):
    return jnp.swapaxes(x.astype(jnp.float32), 0, 1)


def main_kernel(
    place, p, increment, taper, top, bottom, left, right, top_side, bottom_side, coef,
    keep, send, x, values,
):
    members, levels, rows, cols = p.shape
    high = rows + 2 * HALO

    def fill(start, count, fields, g_of, sides, own):
        left_pack, right_pack = (turned(side) for side in sides)

        def shaped(pair, e):
            return windows(
                turned(pair[0]), turned(pair[1]),
                roll(left_pack, -HALO * e), roll(right_pack, -HALO * (e + 1)),
            )

        def side_only(pack, e, shift):
            return roll(pack, shift - HALO * e)

        g_first, g_second = g_of
        g_left = side_only(left_pack, members, 0) + side_only(left_pack, members + 1, 0)
        g_right = side_only(right_pack, members, -HALO) + side_only(right_pack, members + 1, -HALO)
        g = windows(turned(g_first), turned(g_second), g_left, g_right)
        for m in range(members):
            shaped_p = shaped(fields(m), m)
            for w in range(3):
                x[m, pl.ds(start, count), w] = shaped_p[w] * g[w]
                if own is not None:
                    values[m, pl.ds(own, count), w] = shaped_p[w]

    halves = (slice(0, LANES), slice(LANES, 2 * LANES))

    def own_chunk(i, _):
        first = pl.multiple_of(i * HALO, HALO)
        pick = pl.ds(first, HALO)
        fill(
            first + HALO, HALO,
            lambda m: [p[m, :, pick, half] for half in halves],
            [increment[:, pick, half] * taper[:, pick, half] for half in halves],
            (left[:, pick, :], right[:, pick, :]),
            first,
        )
        return 0

    lax.fori_loop(0, rows // HALO, own_chunk, 0)
    for start, strip, side in ((0, top, top_side), (rows + HALO, bottom, bottom_side)):
        fill(
            start, HALO,
            lambda m: [strip[m, :, :, half] for half in halves],
            [
                strip[members, :, :, half].astype(jnp.float32)
                + strip[members + 1, :, :, half].astype(jnp.float32)
                for half in halves
            ],
            (side[0], side[1]),
            None,
        )

    above = jnp.where(place[0] == 1, -1.0, 0.0).astype(jnp.float32)
    below = jnp.where(place[1] == 1, -1.0, 0.0).astype(jnp.float32)

    def reflect(m, _):
        for h in range(HALO - 1):
            for w in range(3):
                x[m, h, w] += above * x[m, 2 * HALO - 2 - h, w]
                x[m, high - 1 - h, w] += below * x[m, high - 1 - (2 * HALO - 2 - h), w]
        return 0

    lax.fori_loop(0, members, reflect, 0)

    linear = coef[0]
    constant = coef[1]

    def sweep_pair(turn):
        low = 2 * turn
        count = high - 4 * turn - 4

        def member_group(group, _):
            streams = [(group * MEMBER_GROUP + k, w) for k in range(MEMBER_GROUP) for w in range(3)]
            start = []
            for m, w in streams:
                x0, x1, x2, x3 = (x[m, low + k, w] for k in range(4))
                v0 = x0 + roll(x1, -1)
                v1 = x1 + roll(x2, -1)
                v2 = x2 + roll(x3, -1)
                u1 = linear * x1 + v0 + roll(v1, 1)
                u2 = linear * x2 + v1 + roll(v2, 1)
                start.append((x2, x3, v2, u2, u1 + roll(u2, -1)))

            def block(b, carry):
                carry = list(carry)
                first = low + 2 + b * ROW_GROUP
                for k in range(ROW_GROUP):
                    for s, (m, w) in enumerate(streams):
                        x0, x1, v, u, q = carry[s]
                        x2 = x[m, first + k + 2, w]
                        v_next = x1 + roll(x2, -1)
                        u_next = linear * x1 + v + roll(v_next, 1)
                        q_next = u + roll(u_next, -1)
                        x[m, first + k, w] = constant * x0 + q + roll(q_next, 1)
                        carry[s] = (x1, x2, v_next, u_next, q_next)
                return tuple(carry)

            lax.fori_loop(0, count // ROW_GROUP, block, tuple(start))
            return 0

        lax.fori_loop(0, members // MEMBER_GROUP, member_group, 0)

    for turn in range(PASSES):
        sweep_pair(turn)

    scale = coef[2]
    core, plane = place[2], place[3]

    def finish(i, _):
        first = pl.multiple_of(i * 8, 8)
        sums = []
        for w in range(3):
            total = x[0, pl.ds(first + HALO, 8), w] * values[0, pl.ds(first, 8), w]
            for m in range(1, members):
                total += x[m, pl.ds(first + HALO, 8), w] * values[m, pl.ds(first, 8), w]
            sums.append(total * scale)
        lane = lane_of(sums[0].shape)
        middle = roll(sums[1], 64)
        joined = (
            jnp.where(lane < 80, roll(sums[0], -HALO), middle),
            jnp.where(lane < 40, middle, roll(sums[2], HALO)),
        )
        for half, part in zip(halves, joined):
            natural = jnp.swapaxes(part, 0, 1) * taper[:, pl.ds(first, 8), half]
            for level in range(levels):
                owner_plane, owner_core, within = level // 4, level // 2 % 2, level % 2
                slot = jnp.where(plane == owner_plane, 0, 2) + within

                @pl.when(core == owner_core)
                def _():
                    keep[slot, pl.ds(first, 8), half] = natural[level]

                @pl.when(core != owner_core)
                def _():
                    send[slot, pl.ds(first, 8), half] = natural[level]

        return 0

    lax.fori_loop(0, rows // 8, finish, 0)


def shifted(value, axis, step, wrap):
    count = lax.axis_size(axis)
    pairs = [(i, (i + step) % count) for i in range(count) if wrap or 0 <= i + step < count]
    return lax.ppermute(value, axis, pairs)


def local(perturbations, increment, taper_norm, kappa):
    members, levels, rows, cols = perturbations.shape
    bf16 = jnp.bfloat16
    strip = jax.ShapeDtypeStruct((members + 2, levels, HALO, cols), bf16)
    pack = jax.ShapeDtypeStruct((levels, rows, LANES), bf16)
    big = pltpu.CompilerParams(vmem_limit_bytes=40 * 1024 * 1024)
    up, down, to_left, to_right = pl.pallas_call(
        pack_kernel, out_shape=(strip, strip, pack, pack), compiler_params=big, name="pack"
    )(perturbations, increment, taper_norm)

    left = shifted(to_right, "lon", 1, True)
    right = shifted(to_left, "lon", -1, True)
    top = shifted(down, "lat", 1, False)
    bottom = shifted(up, "lat", -1, False)
    top_side = shifted(jnp.stack([left[:, -HALO:], right[:, -HALO:]]), "lat", 1, False)
    bottom_side = shifted(jnp.stack([left[:, :HALO], right[:, :HALO]]), "lat", -1, False)

    denominator = 1.0 + 4.0 * kappa
    count = members * lax.axis_size("mem")
    coef = jnp.stack([
        1.0 / kappa,
        denominator / (kappa * kappa),
        (kappa / denominator) ** (2 * PASSES) / (count - 1),
    ])
    coef = jnp.broadcast_to(coef[:, :, None], (3, levels, LANES))
    lat, mem = lax.axis_index("lat"), lax.axis_index("mem")
    place = jnp.stack([
        (lat == 0).astype(jnp.int32),
        (lat == lax.axis_size("lat") - 1).astype(jnp.int32),
        mem % 2,
        mem // 2,
    ])
    vmem = pl.BlockSpec(memory_space=pltpu.VMEM)
    half = jax.ShapeDtypeStruct((levels // 2, rows, cols), jnp.float32)
    keep, send = pl.pallas_call(
        main_kernel,
        out_shape=(half, half),
        in_specs=[pl.BlockSpec(memory_space=pltpu.SMEM)] + [vmem] * 10,
        out_specs=(vmem, vmem),
        scratch_shapes=[
            pltpu.VMEM((members, rows + 2 * HALO, 3, levels, LANES), jnp.float32),
            pltpu.VMEM((members, rows, 3, levels, LANES), jnp.float32),
        ],
        compiler_params=big,
        name="diffuse",
    )(place, perturbations, increment, taper_norm, top, bottom, left, right, top_side, bottom_side, coef)

    got = lax.ppermute(send, "mem", [(i, i ^ 1) for i in range(4)])
    crossing = lax.ppermute(keep[2:] + got[2:], "mem", [(i, i ^ 2) for i in range(4)])
    return keep[:2] + got[:2] + crossing


def solution(mesh):
    return jax.shard_map(
        local,
        mesh=mesh,
        in_specs=(P("mem", None, "lat", "lon"), P(None, "lat", "lon"), P(None, "lat", "lon"), P()),
        out_specs=P("mem", "lat", "lon"),
        check_vma=False,
    )
```

```python
import numpy as np
import jax
import jax.numpy as jnp
from jax import lax
from jax.experimental import pallas as pl
from jax.experimental.pallas import tpu as pltpu
from jax.sharding import PartitionSpec as P

PASSES = 8
HALO = 2 * PASSES
LANES = 128
BLOCK = 8
BF16 = jnp.bfloat16
F32 = jnp.float32


def roll(x, shift):
    shift = shift % LANES
    return pltpu.roll(x, shift, x.ndim - 1) if shift else x


def lane_of(shape):
    return lax.broadcasted_iota(jnp.int32, shape, len(shape) - 1)


def split(value):
    hi = value.astype(BF16)
    return hi, (value - hi.astype(F32)).astype(BF16)


def selectors(members, cols):
    chunks = LANES // members
    fine = (cols + 2 * HALO) // chunks
    lane = np.arange(fine * LANES)
    member, chunk = lane % LANES // chunks, lane % chunks
    column = fine * chunk + lane // LANES - HALO
    before, after = column < 0, column >= cols

    def one_hot(count, target):
        return np.arange(count)[:, None] == target[None, :]

    packs = members * cols
    field = np.where(
        before, packs + HALO * member + column + HALO,
        np.where(after, packs + LANES + HALO * member + column - cols, cols * member + column),
    )
    to_fields = one_hot(packs + 2 * LANES, field)

    def weights(part):
        first = HALO * (members + part)
        return np.where(
            before, 2 * cols + first + column + HALO,
            np.where(after, 2 * cols + LANES + first + column - cols, part * cols + column),
        )

    count = 2 * cols + 2 * LANES
    to_weights = one_hot(count, weights(0)) | one_hot(count, weights(1))
    back = one_hot(cols, column).T
    return [m.astype(np.float32).astype(BF16) for m in (to_fields, to_weights, back)]


def pack_kernel(p, increment, taper, up, down, to_left, to_right):
    members, _, rows, cols = p.shape

    def edge(pick, out):
        for m in range(members):
            out[m] = p[m, :, pick, :]
        hi, lo = split(increment[:, pick, :] * taper[:, pick, :])
        out[members] = hi
        out[members + 1] = lo

    edge(slice(0, HALO), up)
    edge(slice(rows - HALO, rows), down)

    def packed(pick, column, shift):
        fields = [p[m, :, pick, column].astype(F32) for m in range(members)]
        hi, lo = split(increment[:, pick, column] * taper[:, pick, column])
        fields += [hi.astype(F32), lo.astype(F32)]
        lane = lane_of(fields[0].shape)
        total = jnp.zeros_like(fields[0])
        for e, field in enumerate(fields):
            inside = (lane >= HALO * e) & (lane < HALO * (e + 1))
            total = jnp.where(inside, roll(field, shift + HALO * e), total)
        return total.astype(BF16)

    def chunk(i, _):
        pick = pl.ds(pl.multiple_of(i * HALO, HALO), HALO)
        to_left[:, pick, :] = packed(pick, slice(0, LANES), 0)
        to_right[:, pick, :] = packed(pick, slice(cols - LANES, cols), HALO)
        return 0

    lax.fori_loop(0, rows // HALO, chunk, 0)


def turned(value):
    levels, rows, lanes = value.shape
    return jnp.swapaxes(value.astype(F32), 0, 1).reshape(rows * levels, lanes)


def row_of(ref, *where):
    return lambda c: ref[(*where, c + 2)]


def first_sweep(x, x_next, v, linear, fine):
    v_next = {c: x(c) + x_next(c + 1) for c in range(-2, fine + 1)}
    if v is None:
        return v_next, None
    u = {c: linear * x(c) + v[c] + v_next[c - 1] for c in range(-1, fine + 1)}
    return v_next, u


def second_sweep(x, u, u_next, q, constant, fine):
    q_next = {c: u[c] + u_next[c + 1] for c in range(-1, fine)}
    if q is None:
        return q_next, None
    return q_next, [constant * x(c) + q[c] + q_next[c - 1] for c in range(fine)]


def wrap_columns(source, target, fine):
    for c in (0, 1):
        target(fine + c, roll(source(c), -1))
        target(c - 2, roll(source(fine - 2 + c), 1))


def finish(sums, back, scale, taper_of, write, levels):
    hi, lo = split(sums)
    total = jnp.dot(hi, back, preferred_element_type=F32) + jnp.dot(lo, back, preferred_element_type=F32)
    count = total.shape[0] // levels
    for half in range(total.shape[1] // LANES):
        lanes = slice(half * LANES, (half + 1) * LANES)
        part = total[:, lanes].reshape(count, levels, LANES) * scale
        natural = jnp.swapaxes(part, 0, 1) * taper_of(lanes)
        write(natural, lanes)


def to_owner(place, natural, keep, send, pick, lanes, levels):
    core, plane = place[2], place[3]
    for level in range(levels):
        owner_plane, owner_core, within = level // 4, level // 2 % 2, level % 2
        slot = jnp.where(plane == owner_plane, 0, 2) + within

        @pl.when(core == owner_core)
        def _():
            keep[slot, pick, lanes] = natural[level]

        @pl.when(core != owner_core)
        def _():
            send[slot, pick, lanes] = natural[level]


def inner_kernel(
    place, p, increment, taper, left, right, to_fields, to_weights, back, coef,
    keep, send, edges, edge_values,
    x, values, fields, weights,
):
    members, levels, rows, cols = p.shape
    fine = x.shape[1] - 4

    def gather(i, _):
        pick = pl.ds(pl.multiple_of(i * HALO, HALO), HALO)
        out = pl.ds(pl.multiple_of(i * HALO * levels, HALO * levels), HALO * levels)
        for half in range(cols // LANES):
            lanes = slice(half * LANES, (half + 1) * LANES)
            for m in range(members):
                fields[out, m * cols + half * LANES : m * cols + (half + 1) * LANES] = turned(
                    p[m, :, pick, lanes]
                ).astype(BF16)
            hi, lo = split(turned(increment[:, pick, lanes] * taper[:, pick, lanes]))
            weights[out, lanes] = hi
            weights[out, cols + half * LANES : cols + (half + 1) * LANES] = lo
        for side, ref in enumerate((left, right)):
            value = turned(ref[:, pick, :]).astype(BF16)
            fields[out, members * cols + side * LANES : members * cols + (side + 1) * LANES] = value
            weights[out, 2 * cols + side * LANES : 2 * cols + (side + 1) * LANES] = value
        return 0

    lax.fori_loop(0, rows // HALO, gather, 0)
    for first in range(0, fine, 2):
        width = min(2, fine - first)
        lanes = slice(first * LANES, (first + width) * LANES)
        field = jnp.dot(fields[...], to_fields[:, lanes], preferred_element_type=F32)
        weight = jnp.dot(weights[...], to_weights[:, lanes], preferred_element_type=F32)
        for k in range(width):
            pick = slice(k * LANES, (k + 1) * LANES)
            value = field[:, pick].reshape(rows, levels, LANES)
            values[:, first + k] = value
            x[:, 2 + first + k] = value * weight[:, pick].reshape(rows, levels, LANES)
    for k in range(HALO):
        edge_values[0, k] = values[k]
        edge_values[1, k] = values[rows - 1 - k]

    linear, constant = coef[0], coef[1]

    def wrap(row):
        def target(c, value):
            x[row, c + 2] = value

        wrap_columns(row_of(x, row), target, fine)

    def wrap_first(row, _):
        wrap(row)
        return 0

    lax.fori_loop(0, rows, wrap_first, 0, unroll=BLOCK)

    for turn in range(PASSES):
        low = 2 * turn
        start, count = low + 2, rows - 4 * turn - 4
        for k in range(4):
            edges[0, turn, k] = x[low + k]
            edges[1, turn, k] = x[rows - 1 - low - k]

        v, _ = first_sweep(row_of(x, start - 2), row_of(x, start - 1), None, linear, fine)
        v, u = first_sweep(row_of(x, start - 1), row_of(x, start), v, linear, fine)
        v, u_next = first_sweep(row_of(x, start), row_of(x, start + 1), v, linear, fine)
        q, _ = second_sweep(None, u, u_next, None, constant, fine)
        u = u_next
        keys = tuple(list(part) for part in (v, u, q))

        def rows_at(first, number, carry):
            v, u, q = (dict(zip(k, part)) for k, part in zip(keys, carry))
            for k in range(number):
                i = first + k
                v, u_next = first_sweep(row_of(x, i + 1), row_of(x, i + 2), v, linear, fine)
                q, y = second_sweep(row_of(x, i), u, u_next, q, constant, fine)
                u = u_next
                for c in range(fine):
                    x[i, c + 2] = y[c]
            return tuple([part[c] for c in k] for k, part in zip(keys, (v, u, q)))

        def block(b, carry):
            first = start + b * BLOCK
            carry = rows_at(first, BLOCK, carry)
            @pl.when(b > 0)
            def _():
                for k in range(BLOCK):
                    wrap(first - BLOCK + k)
            return carry

        carry = tuple([part[c] for c in k] for k, part in zip(keys, (v, u, q)))
        whole = count // BLOCK
        carry = lax.fori_loop(0, whole, block, carry)
        rest = count - whole * BLOCK
        if rest:
            rows_at(start + whole * BLOCK, rest, carry)
        for row in range(start + (whole - 1) * BLOCK, start + count):
            wrap(row)

    scale = coef[2]

    def last(i, _):
        first = i * HALO
        from_row = first + HALO
        product = jnp.concatenate(
            [
                (x[pl.ds(from_row, HALO), c + 2] * values[pl.ds(from_row, HALO), c]).reshape(HALO * levels, LANES)
                for c in range(fine)
            ],
            axis=1,
        )
        pick = pl.ds(pl.multiple_of(first, HALO), HALO)
        finish(
            product, back[...], scale,
            lambda lanes: taper[:, pl.ds(pl.multiple_of(from_row, HALO), HALO), lanes],
            lambda natural, lanes: to_owner(place, natural, keep, send, pick, lanes, levels),
            levels,
        )
        return 0

    lax.fori_loop(0, (rows - 2 * HALO) // HALO, last, 0)


def outer_kernel(
    place, taper, top, bottom, top_side, bottom_side, edges, edge_values, to_fields, to_weights, back, coef,
    keep, send,
    x, fields, weights,
):
    _, levels, _, cols = top.shape
    members = top.shape[0] - 2
    fine = edge_values.shape[2]
    size = HALO * levels
    for edge, (strip, side) in enumerate(((top, top_side), (bottom, bottom_side))):
        out = slice(edge * size, (edge + 1) * size)
        for half in range(cols // LANES):
            lanes = slice(half * LANES, (half + 1) * LANES)
            for m in range(members + 2):
                value = turned(strip[m, :, :, lanes]).astype(BF16)
                ref, base = (fields, m * cols) if m < members else (weights, (m - members) * cols)
                ref[out, base + half * LANES : base + (half + 1) * LANES] = value
        for k in range(2):
            value = turned(side[k]).astype(BF16)
            fields[out, members * cols + k * LANES : members * cols + (k + 1) * LANES] = value
            weights[out, 2 * cols + k * LANES : 2 * cols + (k + 1) * LANES] = value
    for first in range(0, fine, 2):
        width = min(2, fine - first)
        lanes = slice(first * LANES, (first + width) * LANES)
        both = jnp.dot(fields[...], to_fields[:, lanes], preferred_element_type=F32) * jnp.dot(
            weights[...], to_weights[:, lanes], preferred_element_type=F32
        )
        for k in range(width):
            part = both[:, k * LANES : (k + 1) * LANES].reshape(2, HALO, levels, LANES)
            for row in range(HALO):
                x[0, row, 2 + first + k] = part[0, row]
                x[1, HALO - 1 - row, 2 + first + k] = part[1, row]

    linear, constant = coef[0], coef[1]
    inside = [jnp.where(place[edge] == 1, 0.0, 1.0).astype(F32) for edge in range(2)]

    def wrap(edge, row):
        def target(c, value):
            x[edge, row, c + 2] = value

        wrap_columns(row_of(x, edge, row), target, fine)

    for row in range(HALO):
        for edge in range(2):
            wrap(edge, row)

    for turn in range(PASSES):
        low = 2 * turn
        for edge in range(2):
            def row_at(row):
                if row < low + HALO:
                    return row_of(x, edge, row)
                return row_of(edges, edge, turn, row - low - HALO)

            v = u = q = None
            for i in range(low, low + HALO + 3):
                v, u_next = first_sweep(row_at(i), row_at(i + 1), v, linear, fine)
                if u_next is None:
                    continue
                if i == HALO - 1:
                    u_next = {c: part * inside[edge] for c, part in u_next.items()}
                if u is not None:
                    q, y = second_sweep(row_at(i - 1), u, u_next, q, constant, fine)
                    if y is not None:
                        for c in range(fine):
                            x[edge, i - 1, c + 2] = y[c] * inside[edge] if i == HALO else y[c]
                u = u_next
            if turn < PASSES - 1:
                for row in range(low + 2, low + HALO + 2):
                    wrap(edge, row)

    scale = coef[2]
    rows = taper.shape[1]
    for edge in range(2):
        order = range(HALO) if edge == 0 else range(HALO - 1, -1, -1)
        product = jnp.concatenate(
            [
                jnp.concatenate([x[edge, HALO + k, c + 2] * edge_values[edge, k, c] for k in order], axis=0)
                for c in range(fine)
            ],
            axis=1,
        )
        pick = slice(edge * HALO, (edge + 1) * HALO)
        own = slice(edge * (rows - HALO), edge * (rows - HALO) + HALO)
        finish(
            product, back[...], scale,
            lambda lanes: taper[:, own, lanes],
            lambda natural, lanes: to_owner(place, natural, keep, send, pick, lanes, levels),
            levels,
        )


def shifted(value, axis, step, wrap):
    count = lax.axis_size(axis)
    pairs = [(i, (i + step) % count) for i in range(count) if wrap or 0 <= i + step < count]
    return lax.ppermute(value, axis, pairs)


def total_over_members(keep, send):
    got = lax.ppermute(send, "mem", [(i, i ^ 1) for i in range(4)])
    crossing = lax.ppermute(keep[2:] + got[2:], "mem", [(i, i ^ 2) for i in range(4)])
    return keep[:2] + got[:2] + crossing


def local(perturbations, increment, taper_norm, kappa):
    members, levels, rows, cols = perturbations.shape
    fine = (cols + 2 * HALO) * members // LANES
    shape = jax.ShapeDtypeStruct
    strip = shape((members + 2, levels, HALO, cols), BF16)
    pack = shape((levels, rows, LANES), BF16)
    big = pltpu.CompilerParams(vmem_limit_bytes=40 * 1024 * 1024)
    vmem = pl.BlockSpec(memory_space=pltpu.VMEM)
    smem = pl.BlockSpec(memory_space=pltpu.SMEM)

    up, down, to_left, to_right = pl.pallas_call(
        pack_kernel, out_shape=(strip, strip, pack, pack), compiler_params=big, name="pack"
    )(perturbations, increment, taper_norm)

    left = shifted(to_right, "lon", 1, True)
    right = shifted(to_left, "lon", -1, True)
    top = shifted(down, "lat", 1, False)
    bottom = shifted(up, "lat", -1, False)
    top_side = shifted(jnp.stack([left[:, -HALO:], right[:, -HALO:]]), "lat", 1, False)
    bottom_side = shifted(jnp.stack([left[:, :HALO], right[:, :HALO]]), "lat", -1, False)

    denominator = 1.0 + 4.0 * kappa
    count = members * lax.axis_size("mem")
    coef = jnp.stack([
        1.0 / kappa,
        denominator / (kappa * kappa),
        (kappa / denominator) ** (2 * PASSES) / (count - 1),
    ])
    coef = jnp.broadcast_to(coef[:, :, None], (3, levels, LANES))
    lat, mem = lax.axis_index("lat"), lax.axis_index("mem")
    place = jnp.stack([
        (lat == 0).astype(jnp.int32),
        (lat == lax.axis_size("lat") - 1).astype(jnp.int32),
        mem % 2,
        mem // 2,
    ])
    to_fields, to_weights, back = (jnp.asarray(m) for m in selectors(members, cols))

    tile = (levels, LANES)
    inner_rows = rows - 2 * HALO
    keep, send, edges, edge_values = pl.pallas_call(
        inner_kernel,
        out_shape=(
            shape((levels // 2, inner_rows, cols), F32),
            shape((levels // 2, inner_rows, cols), F32),
            shape((2, PASSES, 4, fine + 4, *tile), F32),
            shape((2, HALO, fine, *tile), F32),
        ),
        in_specs=[smem] + [vmem] * 9,
        out_specs=(vmem,) * 4,
        scratch_shapes=[
            pltpu.VMEM((rows, fine + 4, *tile), F32),
            pltpu.VMEM((rows, fine, *tile), F32),
            pltpu.VMEM((rows * levels, members * cols + 2 * LANES), BF16),
            pltpu.VMEM((rows * levels, 2 * cols + 2 * LANES), BF16),
        ],
        compiler_params=big,
        name="inner",
    )(place, perturbations, increment, taper_norm, left, right, to_fields, to_weights, back, coef)
    middle = total_over_members(keep, send)

    keep, send = pl.pallas_call(
        outer_kernel,
        out_shape=(shape((levels // 2, 2 * HALO, cols), F32),) * 2,
        in_specs=[smem] + [vmem] * 11,
        out_specs=(vmem,) * 2,
        scratch_shapes=[
            pltpu.VMEM((2, 2 * HALO, fine + 4, *tile), F32),
            pltpu.VMEM((2 * HALO * levels, members * cols + 2 * LANES), BF16),
            pltpu.VMEM((2 * HALO * levels, 2 * cols + 2 * LANES), BF16),
        ],
        compiler_params=big,
        name="outer",
    )(place, taper_norm, top, bottom, top_side, bottom_side, edges, edge_values, to_fields, to_weights, back, coef)
    outside = total_over_members(keep, send)
    return jnp.concatenate([outside[:, :HALO], middle, outside[:, HALO:]], axis=1)


def solution(mesh):
    return jax.shard_map(
        local,
        mesh=mesh,
        in_specs=(P("mem", None, "lat", "lon"), P(None, "lat", "lon"), P(None, "lat", "lon"), P()),
        out_specs=P("mem", "lat", "lon"),
        check_vma=False,
    )
```

```python
import numpy as np
import jax
import jax.numpy as jnp
from jax import lax
from jax.experimental import pallas as pl
from jax.experimental.pallas import tpu as pltpu
from jax.sharding import PartitionSpec as P

PASSES = 8
HALO = 2 * PASSES
LANES = 128
NEAR = 4
BF16 = jnp.bfloat16
F32 = jnp.float32


def roll(x, shift):
    shift = shift % LANES
    return pltpu.roll(x, shift, x.ndim - 1) if shift else x


def lane_of(shape):
    return lax.broadcasted_iota(jnp.int32, shape, len(shape) - 1)


def split(value):
    hi = value.astype(BF16)
    return hi, (value - hi.astype(F32)).astype(BF16)


def selectors(members, cols):
    chunks = LANES // members
    fine = (cols + 2 * HALO) // chunks
    lane = np.arange(fine * LANES)
    member, chunk = lane % LANES // chunks, lane % chunks
    column = fine * chunk + lane // LANES - HALO
    before, after = column < 0, column >= cols

    def one_hot(count, target):
        return np.arange(count)[:, None] == target[None, :]

    packs = members * cols
    field = np.where(
        before, packs + HALO * member + column + HALO,
        np.where(after, packs + LANES + HALO * member + column - cols, cols * member + column),
    )
    to_fields = one_hot(packs + 2 * LANES, field)

    def weights(part):
        first = HALO * (members + part)
        return np.where(
            before, 2 * cols + first + column + HALO,
            np.where(after, 2 * cols + LANES + first + column - cols, part * cols + column),
        )

    count = 2 * cols + 2 * LANES
    to_weights = one_hot(count, weights(0)) | one_hot(count, weights(1))
    back = one_hot(cols, column).T
    return [m.astype(np.float32).astype(BF16) for m in (to_fields, to_weights, back)]


def sides_kernel(p_hbm, increment_hbm, taper_hbm, to_left, to_right, p, g, taper, increment, sems):
    members, _, rows, cols = p.shape
    copies = []
    for i in range(rows // HALO):
        pick = slice(i * HALO, (i + 1) * HALO)
        copies.append([
            pltpu.make_async_copy(p_hbm.at[:, :, pick, :], p.at[:, :, pick, :], sems.at[i, 0]),
            pltpu.make_async_copy(increment_hbm.at[:, pick, :], increment.at[:, pick, :], sems.at[i, 1]),
            pltpu.make_async_copy(taper_hbm.at[:, pick, :], taper.at[:, pick, :], sems.at[i, 2]),
        ])
    for group in copies:
        for copy in group:
            copy.start()

    def packed(pick, column, shift):
        fields = [p[m, :, pick, column].astype(F32) for m in range(members)]
        hi, lo = split(g[:, pick, column])
        fields += [hi.astype(F32), lo.astype(F32)]
        lane = lane_of(fields[0].shape)
        total = jnp.zeros_like(fields[0])
        for e, field in enumerate(fields):
            inside = (lane >= HALO * e) & (lane < HALO * (e + 1))
            total = jnp.where(inside, roll(field, shift + HALO * e), total)
        return total.astype(BF16)

    for i, group in enumerate(copies):
        pick = slice(i * HALO, (i + 1) * HALO)
        for copy in group:
            copy.wait()
        g[:, pick, :] = increment[:, pick, :] * taper[:, pick, :]
        to_left[:, pick, :] = packed(pick, slice(0, LANES), 0)
        to_right[:, pick, :] = packed(pick, slice(cols - LANES, cols), HALO)


def facing(value):
    return jnp.swapaxes(value.astype(F32), 0, 1)


def block_of(distance, members):
    near, far = 2 * (members + 2) + 2, 2 * members + 1
    return near * min(distance, NEAR) + far * max(distance - NEAR, 0)


def strips_kernel(p, g, left, right, up, down):
    members, _, rows, cols = p.shape
    for out, first, step in ((up, 0, 1), (down, rows - 1, -1)):
        low = min(first, first + step * (HALO - 1))
        pick = slice(low, low + HALO)
        at = [(distance, first + step * distance - low) for distance in range(HALO)]

        def put(distance, index, value):
            out[block_of(distance, members) + index] = value.astype(BF16)

        for half in range(2):
            lanes = slice(half * LANES, (half + 1) * LANES)
            weight = facing(g[:, pick, lanes])
            hi, lo = split(weight)
            for distance, row in at[:NEAR]:
                put(distance, 2 * members + half, hi[row])
                put(distance, 2 * members + 2 + half, lo[row])
            for m in range(members):
                field = facing(p[m, :, pick, lanes])
                for distance, row in at:
                    value = field[row] if distance < NEAR else field[row] * weight[row]
                    put(distance, 2 * m + half, value)
        packs = [facing(side[:, pick, :]) for side in (left, right)]
        lane = lane_of(packs[0].shape)
        products = []
        for pack in packs:
            weight = pack + roll(pack, -HALO)
            total = jnp.zeros_like(pack)
            for m in range(members):
                inside = (lane >= HALO * m) & (lane < HALO * (m + 1))
                total = jnp.where(inside, roll(weight, HALO * (m - members)), total)
            products.append(pack * total)
        both = jnp.where(lane < LANES // 2, products[0], roll(products[1], LANES // 2))
        for distance, row in at:
            if distance < NEAR:
                for k, pack in enumerate(packs):
                    put(distance, 2 * members + 4 + k, pack[row])
            else:
                put(distance, 2 * members, both[row])


def turned(value):
    levels, rows, lanes = value.shape
    return jnp.swapaxes(value.astype(F32), 0, 1).reshape(rows * levels, lanes)


def factors(kappa, count):
    denominator = 1.0 + 4.0 * kappa
    scale = kappa / denominator
    for _ in range(4):
        scale = scale * scale
    return 1.0 / kappa, denominator / (kappa * kappa), scale / (count - 1)


def row_of(ref, *where):
    return lambda c: ref[(*where, c + 2)]


def first_sweep(x, x_next, v, linear, fine):
    v_next = {c: x(c) + x_next(c + 1) for c in range(-2, fine + 1)}
    if v is None:
        return v_next, None
    u = {c: linear * x(c) + v[c] + v_next[c - 1] for c in range(-1, fine + 1)}
    return v_next, u


def second_sweep(x, u, u_next, q, constant, fine):
    q_next = {c: u[c] + u_next[c + 1] for c in range(-1, fine)}
    if q is None:
        return q_next, None
    return q_next, [constant * x(c) + q[c] + q_next[c - 1] for c in range(fine)]


def wrap_columns(source, target, fine):
    for c in (0, 1):
        target(fine + c, roll(source(c), -1))
        target(c - 2, roll(source(fine - 2 + c), 1))


def finish(sums, back, scale, taper_of, write, levels):
    hi, lo = split(sums)
    total = jnp.dot(hi, back, preferred_element_type=F32) + jnp.dot(lo, back, preferred_element_type=F32)
    count = total.shape[0] // levels
    for half in range(total.shape[1] // LANES):
        lanes = slice(half * LANES, (half + 1) * LANES)
        part = total[:, lanes].reshape(count, levels, LANES) * scale
        natural = jnp.swapaxes(part, 0, 1) * taper_of(lanes)
        write(natural, lanes)


def to_owner(place, natural, keep, send, pick, lanes, levels):
    core, plane = place[2], place[3]
    for level in range(levels):
        owner_plane, owner_core, within = level // 4, level // 2 % 2, level % 2
        slot = jnp.where(plane == owner_plane, 0, 2) + within

        @pl.when(core == owner_core)
        def _():
            keep[slot, pick, lanes] = natural[level]

        @pl.when(core != owner_core)
        def _():
            send[slot, pick, lanes] = natural[level]


def inner_kernel(
    place, p, g, taper, left, right, to_fields, to_weights, back, kappa,
    keep, send, edges, edge_values,
    x, values, fields, weights,
):
    members, levels, rows, cols = p.shape
    fine = x.shape[1] - 4

    def gather(i, _):
        pick = pl.ds(pl.multiple_of(i * HALO, HALO), HALO)
        out = pl.ds(pl.multiple_of(i * HALO * levels, HALO * levels), HALO * levels)
        for half in range(cols // LANES):
            lanes = slice(half * LANES, (half + 1) * LANES)
            for m in range(members):
                fields[out, m * cols + half * LANES : m * cols + (half + 1) * LANES] = turned(
                    p[m, :, pick, lanes]
                ).astype(BF16)
            hi, lo = split(turned(g[:, pick, lanes]))
            weights[out, lanes] = hi
            weights[out, cols + half * LANES : cols + (half + 1) * LANES] = lo
        for side, ref in enumerate((left, right)):
            value = turned(ref[:, pick, :]).astype(BF16)
            fields[out, members * cols + side * LANES : members * cols + (side + 1) * LANES] = value
            weights[out, 2 * cols + side * LANES : 2 * cols + (side + 1) * LANES] = value
        return 0

    lax.fori_loop(0, rows // HALO, gather, 0, unroll=True)
    for first in range(0, fine, 2):
        width = min(2, fine - first)
        lanes = slice(first * LANES, (first + width) * LANES)
        field = jnp.dot(fields[...], to_fields[:, lanes], preferred_element_type=F32)
        weight = jnp.dot(weights[...], to_weights[:, lanes], preferred_element_type=F32)
        for k in range(width):
            pick = slice(k * LANES, (k + 1) * LANES)
            value = field[:, pick].reshape(rows, levels, LANES)
            values[:, first + k] = value
            x[:, 2 + first + k] = value * weight[:, pick].reshape(rows, levels, LANES)
    for k in range(HALO):
        edge_values[0, k] = values[k]
        edge_values[1, k] = values[rows - 1 - k]

    linear, constant, scale = factors(kappa[...], 4 * members)

    def wrap(row):
        def target(c, value):
            x[row, c + 2] = value

        wrap_columns(row_of(x, row), target, fine)

    def wrap_first(row, _):
        wrap(row)
        return 0

    lax.fori_loop(0, rows, wrap_first, 0, unroll=True)

    for turn in range(PASSES):
        low = 2 * turn
        start, count = low + 2, rows - 4 * turn - 4
        for k in range(4):
            edges[0, turn, k] = x[low + k]
            edges[1, turn, k] = x[rows - 1 - low - k]

        v, _ = first_sweep(row_of(x, start - 2), row_of(x, start - 1), None, linear, fine)
        v, u = first_sweep(row_of(x, start - 1), row_of(x, start), v, linear, fine)
        v, u_next = first_sweep(row_of(x, start), row_of(x, start + 1), v, linear, fine)
        q, _ = second_sweep(None, u, u_next, None, constant, fine)
        u = u_next
        for i in range(start, start + count):
            v, u_next = first_sweep(row_of(x, i + 1), row_of(x, i + 2), v, linear, fine)
            q, y = second_sweep(row_of(x, i), u, u_next, q, constant, fine)
            u = u_next
            for c in range(fine):
                x[i, c + 2] = y[c]
            if turn < PASSES - 1:
                wrap(i)

    def last(i, _):
        first = i * HALO
        from_row = first + HALO
        product = jnp.concatenate(
            [
                (x[pl.ds(from_row, HALO), c + 2] * values[pl.ds(from_row, HALO), c]).reshape(HALO * levels, LANES)
                for c in range(fine)
            ],
            axis=1,
        )
        pick = pl.ds(pl.multiple_of(first, HALO), HALO)
        finish(
            product, back[...], scale,
            lambda lanes: taper[:, pl.ds(pl.multiple_of(from_row, HALO), HALO), lanes],
            lambda natural, lanes: to_owner(place, natural, keep, send, pick, lanes, levels),
            levels,
        )
        return 0

    lax.fori_loop(0, (rows - 2 * HALO) // HALO, last, 0)


def outer_kernel(
    place, taper, top, bottom, edges, edge_values, to_fields, to_weights, back, kappa,
    keep, send,
    x, fields, weights,
):
    levels, cols = taper.shape[0], taper.shape[2]
    fine = edge_values.shape[2]
    members = LANES * fine // (cols + 2 * HALO)
    for edge, strip in enumerate((top, bottom)):
        for distance in range(0, HALO, 2):
            is_near = distance < NEAR
            firsts = [block_of(distance + k, members) for k in range(2)]

            def pair(index):
                return jnp.concatenate([strip[first + index].astype(F32) for first in firsts], axis=0)

            out = slice((edge * HALO + distance) * levels, (edge * HALO + distance + 2) * levels)
            for k in range(2 * members):
                fields[out, k * LANES : (k + 1) * LANES] = pair(k).astype(BF16)
            sides = [2 * members + 4, 2 * members + 5] if is_near else [2 * members] * 2
            for k, index in enumerate(sides):
                value = pair(index)
                if k == 1 and not is_near:
                    value = roll(value, LANES // 2)
                value = value.astype(BF16)
                fields[out, members * cols + k * LANES : members * cols + (k + 1) * LANES] = value
                if is_near:
                    here = slice((edge * NEAR + distance) * levels, (edge * NEAR + distance + 2) * levels)
                    weights[here, 2 * cols + k * LANES : 2 * cols + (k + 1) * LANES] = value
            if is_near:
                for k in range(4):
                    weights[here, k * LANES : (k + 1) * LANES] = pair(2 * members + k).astype(BF16)
    for first in range(0, fine, 2):
        width = min(2, fine - first)
        lanes = slice(first * LANES, (first + width) * LANES)
        field = jnp.dot(fields[...], to_fields[:, lanes], preferred_element_type=F32)
        weight = jnp.dot(weights[...], to_weights[:, lanes], preferred_element_type=F32)
        for k in range(width):
            pick = slice(k * LANES, (k + 1) * LANES)
            part = field[:, pick].reshape(2, HALO, levels, LANES)
            near = weight[:, pick].reshape(2, NEAR, levels, LANES)
            for edge in range(2):
                for distance in range(HALO):
                    value = part[edge, distance]
                    if distance < NEAR:
                        value = value * near[edge, distance]
                    x[edge, HALO - 1 - distance, 2 + first + k] = value

    linear, constant, scale = factors(kappa[...], 4 * members)
    inside = [jnp.where(place[edge] == 1, 0.0, 1.0).astype(F32) for edge in range(2)]

    def wrap(edge, row):
        def target(c, value):
            x[edge, row, c + 2] = value

        wrap_columns(row_of(x, edge, row), target, fine)

    for row in range(HALO):
        for edge in range(2):
            wrap(edge, row)

    for turn in range(PASSES):
        low = 2 * turn
        for edge in range(2):
            def row_at(row):
                if row < low + HALO:
                    return row_of(x, edge, row)
                return row_of(edges, edge, turn, row - low - HALO)

            v = u = q = None
            for i in range(low, low + HALO + 3):
                v, u_next = first_sweep(row_at(i), row_at(i + 1), v, linear, fine)
                if u_next is None:
                    continue
                if i == HALO - 1:
                    u_next = {c: part * inside[edge] for c, part in u_next.items()}
                if u is not None:
                    q, y = second_sweep(row_at(i - 1), u, u_next, q, constant, fine)
                    if y is not None:
                        for c in range(fine):
                            x[edge, i - 1, c + 2] = y[c] * inside[edge] if i == HALO else y[c]
                u = u_next
            if turn < PASSES - 1:
                for row in range(low + 2, low + HALO + 2):
                    wrap(edge, row)

    rows = taper.shape[1]
    for edge in range(2):
        order = range(HALO) if edge == 0 else range(HALO - 1, -1, -1)
        product = jnp.concatenate(
            [
                jnp.concatenate([x[edge, HALO + k, c + 2] * edge_values[edge, k, c] for k in order], axis=0)
                for c in range(fine)
            ],
            axis=1,
        )
        pick = slice(edge * HALO, (edge + 1) * HALO)
        own = slice(edge * (rows - HALO), edge * (rows - HALO) + HALO)
        finish(
            product, back[...], scale,
            lambda lanes: taper[:, own, lanes],
            lambda natural, lanes: to_owner(place, natural, keep, send, pick, lanes, levels),
            levels,
        )


def shifted(value, axis, step, wrap):
    count = lax.axis_size(axis)
    pairs = [(i, (i + step) % count) for i in range(count) if wrap or 0 <= i + step < count]
    return lax.ppermute(value, axis, pairs)


def over_core(keep, send):
    got = lax.ppermute(send, "mem", [(i, i ^ 1) for i in range(4)])
    return keep[:2] + got[:2], keep[2:] + got[2:]


def over_plane(here, there):
    return here + lax.ppermute(there, "mem", [(i, i ^ 2) for i in range(4)])


def local(perturbations, increment, taper_norm, kappa):
    members, levels, rows, cols = perturbations.shape
    fine = (cols + 2 * HALO) * members // LANES
    shape = jax.ShapeDtypeStruct
    tile = (levels, LANES)
    big = pltpu.CompilerParams(vmem_limit_bytes=16 * 1024 * 1024)
    vmem = pl.BlockSpec(memory_space=pltpu.VMEM)
    smem = pl.BlockSpec(memory_space=pltpu.SMEM)
    hbm = pl.BlockSpec(memory_space=pltpu.HBM)

    pack = shape((levels, rows, LANES), BF16)
    whole = shape((levels, rows, cols), F32)
    to_left, to_right, p, g, taper = pl.pallas_call(
        sides_kernel,
        out_shape=(pack, pack, shape(perturbations.shape, BF16), whole, whole),
        in_specs=[hbm] * 3,
        out_specs=(vmem,) * 5,
        scratch_shapes=[pltpu.VMEM((levels, rows, cols), F32), pltpu.SemaphoreType.DMA((rows // HALO, 3))],
        compiler_params=big,
        name="sides",
    )(perturbations, increment, taper_norm)
    left = shifted(to_right, "lon", 1, True)
    right = shifted(to_left, "lon", -1, True)

    strip = shape((block_of(HALO, members), *tile), BF16)
    up, down = pl.pallas_call(
        strips_kernel,
        out_shape=(strip, strip),
        in_specs=[vmem] * 4,
        out_specs=(vmem,) * 2,
        compiler_params=big,
        name="strips",
    )(p, g, left, right)
    top = shifted(down, "lat", 1, False)
    bottom = shifted(up, "lat", -1, False)

    kappa = jnp.broadcast_to(kappa[:, None], tile)
    lat, mem = lax.axis_index("lat"), lax.axis_index("mem")
    place = jnp.stack([
        (lat == 0).astype(jnp.int32),
        (lat == lax.axis_size("lat") - 1).astype(jnp.int32),
        mem % 2,
        mem // 2,
    ])
    to_fields, to_weights, back = (jnp.asarray(m) for m in selectors(members, cols))

    part = shape((levels // 2, rows - 2 * HALO, cols), F32)
    keep, send, edges, edge_values = pl.pallas_call(
        inner_kernel,
        out_shape=(
            part,
            part,
            shape((2, PASSES, 4, fine + 4, *tile), F32),
            shape((2, HALO, fine, *tile), F32),
        ),
        in_specs=[smem] + [vmem] * 9,
        out_specs=(vmem,) * 4,
        scratch_shapes=[
            pltpu.VMEM((rows, fine + 4, *tile), F32),
            pltpu.VMEM((rows, fine, *tile), F32),
            pltpu.VMEM((rows * levels, members * cols + 2 * LANES), BF16),
            pltpu.VMEM((rows * levels, 2 * cols + 2 * LANES), BF16),
        ],
        compiler_params=big,
        name="inner",
    )(place, p, g, taper, left, right, to_fields, to_weights, back, kappa)
    here, there = over_core(keep, send)
    here, there, edges = lax.optimization_barrier((here, there, edges))
    middle = over_plane(here, there)

    part = shape((levels // 2, 2 * HALO, cols), F32)
    keep, send = pl.pallas_call(
        outer_kernel,
        out_shape=(part, part),
        in_specs=[smem] + [vmem] * 9,
        out_specs=(vmem,) * 2,
        scratch_shapes=[
            pltpu.VMEM((2, 2 * HALO, fine + 4, *tile), F32),
            pltpu.VMEM((2 * HALO * levels, members * cols + 2 * LANES), BF16),
            pltpu.VMEM((2 * NEAR * levels, 2 * cols + 2 * LANES), BF16),
        ],
        compiler_params=big,
        name="outer",
    )(place, taper, top, bottom, edges, edge_values, to_fields, to_weights, back, kappa)
    outside = over_plane(*over_core(keep, send))
    return jnp.concatenate([outside[:, :HALO], middle, outside[:, HALO:]], axis=1)


def solution(mesh):
    return jax.shard_map(
        local,
        mesh=mesh,
        in_specs=(P("mem", None, "lat", "lon"), P(None, "lat", "lon"), P(None, "lat", "lon"), P()),
        out_specs=P("mem", "lat", "lon"),
        check_vma=False,
    )
```

```python
import jax
import jax.numpy as jnp
from jax import lax
from jax.experimental import pallas as pl
from jax.experimental.pallas import tpu as pltpu
from jax.sharding import PartitionSpec as P

PASSES = 8
HALO = 2 * PASSES
LANES = 128
NEAR = 4
START_LIMIT = 50
BF16 = jnp.bfloat16
F32 = jnp.float32


def roll(x, shift):
    shift = shift % LANES
    return pltpu.roll(x, shift, x.ndim - 1) if shift else x


def lane_of(shape):
    return lax.broadcasted_iota(jnp.int32, shape, len(shape) - 1)


def split(value):
    hi = value.astype(BF16)
    return hi, (value - hi.astype(F32)).astype(BF16)


def target_column(shape, first, members, cols):
    chunks = LANES // members
    fine = (cols + 2 * HALO) // chunks
    lane = lax.broadcasted_iota(jnp.int32, shape, 1)
    return fine * (lane % chunks) + first - HALO, lane // chunks


def fill_selectors(to_fields, to_weights, back, members, cols):
    fine = back.shape[0] // LANES

    def mark(hit):
        return jnp.where(hit, 1.0, 0.0).astype(BF16)

    for first in range(fine):
        lanes = slice(first * LANES, (first + 1) * LANES)
        shape = (cols, LANES)
        column, member = target_column(shape, first, members, cols)
        row = lax.broadcasted_iota(jnp.int32, shape, 0)
        here = row == column
        for m in range(members):
            to_fields[m * cols : (m + 1) * cols, lanes] = mark(here & (member == m))
        for part in range(2):
            to_weights[part * cols : (part + 1) * cols, lanes] = mark(here)
        shape = (2 * LANES, LANES)
        column, member = target_column(shape, first, members, cols)
        row = lax.broadcasted_iota(jnp.int32, shape, 0)
        base = jnp.where(column < 0, column + HALO, jnp.where(column >= cols, column - cols + LANES, -4 * LANES))
        to_fields[members * cols :, lanes] = mark(row == base + HALO * member)
        hi = base + HALO * members
        to_weights[2 * cols :, lanes] = mark((row == hi) | (row == hi + HALO))
        shape = (LANES, cols)
        lane = lax.broadcasted_iota(jnp.int32, shape, 0)
        column = fine * (lane % (LANES // members)) + first - HALO
        back[lanes, :] = mark(lax.broadcasted_iota(jnp.int32, shape, 1) == column)


def facing(value):
    return jnp.swapaxes(value.astype(F32), 0, 1)


def start_kernel(p_hbm, increment_hbm, taper_hbm, up, down, to_left, to_right, p, g, taper, increment, sems):
    members, levels, rows, cols = p.shape
    copies = []
    for i in (0, rows // HALO - 1, *range(1, rows // HALO - 1)):
        pick = slice(i * HALO, (i + 1) * HALO)
        copies.append((pick, [
            pltpu.make_async_copy(p_hbm.at[:, :, pick, :], p.at[:, :, pick, :], sems.at[i, 0]),
            pltpu.make_async_copy(increment_hbm.at[:, pick, :], increment.at[:, pick, :], sems.at[i, 1]),
            pltpu.make_async_copy(taper_hbm.at[:, pick, :], taper.at[:, pick, :], sems.at[i, 2]),
        ]))
    for _, group in copies:
        for copy in group:
            copy.start()

    def strip(out, pick, order):
        def put(pair, lanes, field, first=0):
            rows_at = slice(first + 2 * pair * levels, first + 2 * (pair + 1) * levels)
            both = jnp.concatenate([field[order[2 * pair]], field[order[2 * pair + 1]]], axis=0)
            out[rows_at, lanes] = both.astype(BF16)

        for half in range(2):
            lanes = slice(half * LANES, (half + 1) * LANES)
            weight = facing(g[:, pick, lanes])
            hi = weight.astype(BF16).astype(F32)
            for k, part in enumerate((hi, weight - hi)):
                for pair in range(NEAR // 2):
                    put(pair, slice(members * cols, members * cols + LANES), part, (2 * k + half) * NEAR * levels)
            for m in range(members):
                to = slice(m * cols + half * LANES, m * cols + (half + 1) * LANES)
                field = facing(p[m, :, pick, lanes])
                for pair in range(HALO // 2):
                    put(pair, to, field if 2 * pair < NEAR else field * weight)

    def packed(pick, column, shift):
        fields = [p[m, :, pick, column].astype(F32) for m in range(members)]
        hi, lo = split(g[:, pick, column])
        fields += [hi.astype(F32), lo.astype(F32)]
        lane = lane_of(fields[0].shape)
        total = jnp.zeros_like(fields[0])
        for e, field in enumerate(fields):
            inside = (lane >= HALO * e) & (lane < HALO * (e + 1))
            total = jnp.where(inside, roll(field, shift + HALO * e), total)
        return total.astype(BF16)

    for k, (pick, group) in enumerate(copies):
        for copy in group:
            copy.wait()
        g[:, pick, :] = increment[:, pick, :] * taper[:, pick, :]
        if k == 0:
            strip(up, pick, range(HALO))
        if k == 1:
            strip(down, pick, range(HALO - 1, -1, -1))
        to_left[:, pick, :] = packed(pick, slice(0, LANES), 0)
        to_right[:, pick, :] = packed(pick, slice(cols - LANES, cols), HALO)


def corners_kernel(top, bottom, to_left, to_right):
    count = top.shape[0]
    pairs = count // 16
    for edge, strip in enumerate((top, bottom)):
        main = strip.shape[1] - LANES
        members = main // (2 * LANES)
        for pair in range(pairs):
            rows = slice(16 * pair, 16 * (pair + 1))
            out = slice(edge * count + 16 * pair, edge * count + 16 * (pair + 1))
            fields = [
                [strip[rows, (2 * m + half) * LANES : (2 * m + half + 1) * LANES].astype(F32) for m in range(members)]
                for half in range(2)
            ]
            if 2 * pair < NEAR:
                for half in range(2):
                    for k in range(2):
                        first = (2 * k + half) * (count // 4) + 16 * pair
                        fields[half].append(strip[first : first + 16, main:].astype(F32))
            lane = lane_of((16, LANES))
            for ref, half, shift in ((to_left, 0, 0), (to_right, 1, HALO)):
                total = jnp.zeros((16, LANES), F32)
                for e, field in enumerate(fields[half]):
                    inside = (lane >= HALO * e) & (lane < HALO * (e + 1))
                    total = jnp.where(inside, roll(field, shift + HALO * e), total)
                ref[out, :] = total.astype(BF16)


def turned(value):
    levels, rows, lanes = value.shape
    return jnp.swapaxes(value.astype(F32), 0, 1).reshape(rows * levels, lanes)


def factors(kappa, count):
    denominator = 1.0 + 4.0 * kappa
    scale = kappa / denominator
    for _ in range(4):
        scale = scale * scale
    return 1.0 / kappa, denominator / (kappa * kappa), scale / (count - 1)


def row_of(ref, *where):
    return lambda c: ref[(*where, c + 2)]


def first_sweep(x, x_next, v, linear, fine):
    v_next = {c: x(c) + x_next(c + 1) for c in range(-2, fine + 1)}
    if v is None:
        return v_next, None
    u = {c: linear * x(c) + v[c] + v_next[c - 1] for c in range(-1, fine + 1)}
    return v_next, u


def second_sweep(x, u, u_next, q, constant, fine):
    q_next = {c: u[c] + u_next[c + 1] for c in range(-1, fine)}
    if q is None:
        return q_next, None
    return q_next, [constant * x(c) + q[c] + q_next[c - 1] for c in range(fine)]


def wrap_columns(source, target, fine):
    for c in (0, 1):
        target(fine + c, roll(source(c), -1))
        target(c - 2, roll(source(fine - 2 + c), 1))


def finish(sums, back, scale, taper_of, write, levels):
    hi, lo = split(sums)
    total = jnp.dot(hi, back, preferred_element_type=F32) + jnp.dot(lo, back, preferred_element_type=F32)
    count = total.shape[0] // levels
    for half in range(total.shape[1] // LANES):
        lanes = slice(half * LANES, (half + 1) * LANES)
        part = total[:, lanes].reshape(count, levels, LANES) * scale
        natural = jnp.swapaxes(part, 0, 1) * taper_of(lanes)
        write(natural, lanes)


def to_owner(place, natural, keep, send, pick, lanes, levels):
    core, plane = place[2], place[3]
    for level in range(levels):
        owner_plane, owner_core, within = level // 4, level // 2 % 2, level % 2
        slot = jnp.where(plane == owner_plane, 0, 2) + within

        @pl.when(core == owner_core)
        def _():
            keep[slot, pick, lanes] = natural[level]

        @pl.when(core != owner_core)
        def _():
            send[slot, pick, lanes] = natural[level]


def dot(a, b):
    return jnp.dot(a, b, preferred_element_type=F32)


def prepare_kernel(p, g, own_values, own_weights, to_fields, to_weights, back, fields, weights):
    members, levels, rows, cols = p.shape
    fine = back.shape[0] // LANES
    fill_selectors(to_fields, to_weights, back, members, cols)
    for i in range(rows // HALO):
        pick = slice(i * HALO, (i + 1) * HALO)
        out = slice(i * HALO * levels, (i + 1) * HALO * levels)
        for half in range(cols // LANES):
            lanes = slice(half * LANES, (half + 1) * LANES)
            for m in range(members):
                to = slice(m * cols + half * LANES, m * cols + (half + 1) * LANES)
                fields[out, to] = turned(p[m, :, pick, lanes]).astype(BF16)
            hi, lo = split(turned(g[:, pick, lanes]))
            weights[out, lanes] = hi
            weights[out, cols + half * LANES : cols + (half + 1) * LANES] = lo
    for first in range(0, fine, 2):
        width = min(2, fine - first)
        lanes = slice(first * LANES, (first + width) * LANES)
        field = dot(fields[...], to_fields[: members * cols, lanes])
        weight = dot(weights[...], to_weights[: 2 * cols, lanes])
        for k in range(width):
            pick = slice(k * LANES, (k + 1) * LANES)
            own_values[:, first + k] = field[:, pick].reshape(rows, levels, LANES)
            own_weights[:, first + k] = weight[:, pick].reshape(rows, levels, LANES)


def inner_kernel(
    place, own_values, own_weights, taper, left, right, to_fields, to_weights, back, kappa,
    keep, send, edges, edge_values,
    x, values, packs,
):
    levels, rows, cols = taper.shape
    fine = x.shape[1] - 4
    members = LANES * fine // (cols + 2 * HALO)
    for i in range(rows // HALO):
        out = slice(i * HALO * levels, (i + 1) * HALO * levels)
        for side, ref in enumerate((left, right)):
            lanes = slice(side * LANES, (side + 1) * LANES)
            packs[out, lanes] = turned(ref[:, i * HALO : (i + 1) * HALO, :]).astype(BF16)
    for first in range(0, fine, 2):
        width = min(2, fine - first)
        lanes = slice(first * LANES, (first + width) * LANES)
        field = dot(packs[...], to_fields[members * cols :, lanes])
        weight = dot(packs[...], to_weights[2 * cols :, lanes])
        for k in range(width):
            pick = slice(k * LANES, (k + 1) * LANES)
            value = own_values[:, first + k] + field[:, pick].reshape(rows, levels, LANES)
            values[:, first + k] = value
            x[:, 2 + first + k] = value * (own_weights[:, first + k] + weight[:, pick].reshape(rows, levels, LANES))
    for k in range(HALO):
        edge_values[0, k] = values[k]
        edge_values[1, k] = values[rows - 1 - k]

    linear, constant, scale = factors(kappa[...], 4 * members)

    def wrap(row):
        def target(c, value):
            x[row, c + 2] = value

        wrap_columns(row_of(x, row), target, fine)

    def wrap_first(row, _):
        wrap(row)
        return 0

    lax.fori_loop(0, rows, wrap_first, 0, unroll=True)

    for turn in range(PASSES):
        low = 2 * turn
        start, count = low + 2, rows - 4 * turn - 4
        for k in range(4):
            edges[0, turn, k] = x[low + k]
            edges[1, turn, k] = x[rows - 1 - low - k]

        v, _ = first_sweep(row_of(x, start - 2), row_of(x, start - 1), None, linear, fine)
        v, u = first_sweep(row_of(x, start - 1), row_of(x, start), v, linear, fine)
        v, u_next = first_sweep(row_of(x, start), row_of(x, start + 1), v, linear, fine)
        q, _ = second_sweep(None, u, u_next, None, constant, fine)
        u = u_next
        for i in range(start, start + count):
            v, u_next = first_sweep(row_of(x, i + 1), row_of(x, i + 2), v, linear, fine)
            q, y = second_sweep(row_of(x, i), u, u_next, q, constant, fine)
            u = u_next
            for c in range(fine):
                x[i, c + 2] = y[c]
            if turn < PASSES - 1:
                wrap(i)

    def last(i, _):
        first = i * HALO
        from_row = first + HALO
        product = jnp.concatenate(
            [
                (x[pl.ds(from_row, HALO), c + 2] * values[pl.ds(from_row, HALO), c]).reshape(HALO * levels, LANES)
                for c in range(fine)
            ],
            axis=1,
        )
        pick = pl.ds(pl.multiple_of(first, HALO), HALO)
        finish(
            product, back[...], scale,
            lambda lanes: taper[:, pl.ds(pl.multiple_of(from_row, HALO), HALO), lanes],
            lambda natural, lanes: to_owner(place, natural, keep, send, pick, lanes, levels),
            levels,
        )
        return 0

    lax.fori_loop(0, (rows - 2 * HALO) // HALO, last, 0)


def lift_kernel(top, bottom, to_fields, to_weights, main_values, main_weights):
    fine, levels = main_values.shape[2:4]
    count = top.shape[0]
    main = top.shape[1] - LANES
    for first in range(0, fine, 2):
        width = min(2, fine - first)
        lanes = slice(first * LANES, (first + width) * LANES)
        for edge, strip in enumerate((top, bottom)):
            field = dot(strip[:, :main], to_fields[:main, lanes])
            part = count // 4
            near = jnp.concatenate([strip[k * part : (k + 1) * part, main:] for k in range(4)], axis=1)
            weight = dot(near, to_weights[: 4 * LANES, lanes])
            for k in range(width):
                pick = slice(k * LANES, (k + 1) * LANES)
                main_values[edge, :, first + k] = field[:, pick].reshape(HALO, levels, LANES)
                main_weights[edge, :, first + k] = weight[:, pick].reshape(NEAR, levels, LANES)


def outer_kernel(
    place, taper, left, right, main_values, main_weights, edges, edge_values, keep_inner, send_inner,
    to_fields, to_weights, back, kappa,
    keep, send,
    x,
):
    levels, rows, cols = taper.shape
    fine = edge_values.shape[2]
    members = LANES * fine // (cols + 2 * HALO)
    keep[:, HALO : rows - HALO, :] = keep_inner[...]
    send[:, HALO : rows - HALO, :] = send_inner[...]
    packs = jnp.concatenate([left[...], right[...]], axis=1)
    size = HALO * levels
    near_packs = jnp.concatenate([packs[edge * size : edge * size + NEAR * levels] for edge in range(2)], axis=0)
    for first in range(0, fine, 2):
        width = min(2, fine - first)
        lanes = slice(first * LANES, (first + width) * LANES)
        field = dot(packs, to_fields[members * cols :, lanes])
        weight = dot(near_packs, to_weights[2 * cols :, lanes])
        for k in range(width):
            pick = slice(k * LANES, (k + 1) * LANES)
            part = field[:, pick].reshape(2, HALO, levels, LANES)
            near = weight[:, pick].reshape(2, NEAR, levels, LANES)
            for edge in range(2):
                for distance in range(HALO):
                    value = main_values[edge, distance, first + k] + part[edge, distance]
                    if distance < NEAR:
                        value = value * (main_weights[edge, distance, first + k] + near[edge, distance])
                    x[edge, HALO - 1 - distance, 2 + first + k] = value

    linear, constant, scale = factors(kappa[...], 4 * members)
    inside = [jnp.where(place[edge] == 1, 0.0, 1.0).astype(F32) for edge in range(2)]

    def wrap(edge, row):
        def target(c, value):
            x[edge, row, c + 2] = value

        wrap_columns(row_of(x, edge, row), target, fine)

    for row in range(HALO):
        for edge in range(2):
            wrap(edge, row)

    for turn in range(PASSES):
        low = 2 * turn
        for edge in range(2):
            def row_at(row):
                if row < low + HALO:
                    return row_of(x, edge, row)
                return row_of(edges, edge, turn, row - low - HALO)

            v = u = q = None
            for i in range(low, low + HALO + 3):
                v, u_next = first_sweep(row_at(i), row_at(i + 1), v, linear, fine)
                if u_next is None:
                    continue
                if i == HALO - 1:
                    u_next = {c: part * inside[edge] for c, part in u_next.items()}
                if u is not None:
                    q, y = second_sweep(row_at(i - 1), u, u_next, q, constant, fine)
                    if y is not None:
                        for c in range(fine):
                            x[edge, i - 1, c + 2] = y[c] * inside[edge] if i == HALO else y[c]
                u = u_next
            if turn < PASSES - 1:
                for row in range(low + 2, low + HALO + 2):
                    wrap(edge, row)

    for edge in range(2):
        order = range(HALO) if edge == 0 else range(HALO - 1, -1, -1)
        product = jnp.concatenate(
            [
                jnp.concatenate([x[edge, HALO + k, c + 2] * edge_values[edge, k, c] for k in order], axis=0)
                for c in range(fine)
            ],
            axis=1,
        )
        own = slice(edge * (rows - HALO), edge * (rows - HALO) + HALO)
        finish(
            product, back[...], scale,
            lambda lanes: taper[:, own, lanes],
            lambda natural, lanes: to_owner(place, natural, keep, send, own, lanes, levels),
            levels,
        )


def shifted(value, axis, step, wrap):
    count = lax.axis_size(axis)
    pairs = [(i, (i + step) % count) for i in range(count) if wrap or 0 <= i + step < count]
    return lax.ppermute(value, axis, pairs)


def local(perturbations, increment, taper_norm, kappa):
    members, levels, rows, cols = perturbations.shape
    fine = (cols + 2 * HALO) * members // LANES
    shape = jax.ShapeDtypeStruct
    tile = (levels, LANES)
    vmem = pl.BlockSpec(memory_space=pltpu.VMEM)
    smem = pl.BlockSpec(memory_space=pltpu.SMEM)
    hbm = pl.BlockSpec(memory_space=pltpu.HBM)

    def call(kernel, name, outs, ins, scratch=(), specs=None, limit=16):
        return pl.pallas_call(
            kernel,
            out_shape=tuple(outs),
            in_specs=specs or [vmem] * len(ins),
            out_specs=(vmem,) * len(outs),
            scratch_shapes=list(scratch),
            compiler_params=pltpu.CompilerParams(vmem_limit_bytes=limit * 1024 * 1024),
            name=name,
        )(*ins)

    strip = shape((HALO * levels, members * cols + LANES), BF16)
    pack = shape((levels, rows, LANES), BF16)
    whole = shape((levels, rows, cols), F32)
    up, down, to_left, to_right, p, g = call(
        start_kernel, "start",
        (strip, strip, pack, pack, shape(perturbations.shape, BF16), whole),
        (perturbations, increment, taper_norm),
        (pltpu.VMEM(whole.shape, F32), pltpu.VMEM(whole.shape, F32), pltpu.SemaphoreType.DMA((rows // HALO, 3))),
        specs=[hbm] * 3, limit=START_LIMIT,
    )
    top = shifted(down, "lat", 1, False)
    bottom = shifted(up, "lat", -1, False)
    left = shifted(to_right, "lon", 1, True)
    right = shifted(to_left, "lon", -1, True)

    kappa = jnp.broadcast_to(kappa[:, None], tile)
    lat, mem = lax.axis_index("lat"), lax.axis_index("mem")
    place = jnp.stack([
        (lat == 0).astype(jnp.int32),
        (lat == lax.axis_size("lat") - 1).astype(jnp.int32),
        mem % 2,
        mem // 2,
    ])

    values = shape((rows, fine, *tile), F32)
    own_values, own_weights, to_fields, to_weights, back = call(
        prepare_kernel, "prepare",
        (
            values, values,
            shape((members * cols + 2 * LANES, fine * LANES), BF16),
            shape((2 * cols + 2 * LANES, fine * LANES), BF16),
            shape((fine * LANES, cols), BF16),
        ),
        (p, g),
        (pltpu.VMEM((rows * levels, members * cols), BF16), pltpu.VMEM((rows * levels, 2 * cols), BF16)),

    )

    part = shape((levels // 2, rows - 2 * HALO, cols), F32)
    keep, send, edges, edge_values = call(
        inner_kernel, "inner",
        (part, part, shape((2, PASSES, 4, fine + 4, *tile), F32), shape((2, HALO, fine, *tile), F32)),
        (place, own_values, own_weights, taper_norm, left, right, to_fields, to_weights, back, kappa),
        (
            pltpu.VMEM((rows, fine + 4, *tile), F32),
            pltpu.VMEM((rows, fine, *tile), F32),
            pltpu.VMEM((rows * levels, 2 * LANES), BF16),
        ),
        specs=[smem] + [vmem] * 9,
    )
    top, bottom, edges = lax.optimization_barrier((top, bottom, edges))

    side = shape((2 * HALO * levels, LANES), BF16)
    to_left, to_right = call(corners_kernel, "corners", (side, side), (top, bottom))
    left = shifted(to_right, "lon", 1, True)
    right = shifted(to_left, "lon", -1, True)
    top, bottom, _, _ = lax.optimization_barrier((top, bottom, to_left, to_right))
    main_values, main_weights = call(
        lift_kernel, "lift",
        (shape((2, HALO, fine, *tile), F32), shape((2, NEAR, fine, *tile), F32)),
        (top, bottom, to_fields, to_weights),

    )
    part = shape((levels // 2, rows, cols), F32)
    keep, send = call(
        outer_kernel, "outer",
        (part, part),
        (
            place, taper_norm, left, right, main_values, main_weights, edges, edge_values, keep, send,
            to_fields, to_weights, back, kappa,
        ),
        (pltpu.VMEM((2, 2 * HALO, fine + 4, *tile), F32),),
        specs=[smem] + [vmem] * 13,
    )
    got = lax.ppermute(send, "mem", [(i, i ^ 1) for i in range(4)])
    crossing = lax.ppermute(keep[2:] + got[2:], "mem", [(i, i ^ 2) for i in range(4)])
    return keep[:2] + got[:2] + crossing


def solution(mesh):
    return jax.shard_map(
        local,
        mesh=mesh,
        in_specs=(P("mem", None, "lat", "lon"), P(None, "lat", "lon"), P(None, "lat", "lon"), P()),
        out_specs=P("mem", "lat", "lon"),
        check_vma=False,
    )
```

```python
import jax
import jax.numpy as jnp
from jax import lax
from jax.experimental import pallas as pl
from jax.experimental.pallas import tpu as pltpu
from jax.sharding import PartitionSpec as P

PASSES = 8
HALO = 2 * PASSES
LANES = 128
NEAR = 4
BF16 = jnp.bfloat16
F32 = jnp.float32


def roll(x, shift):
    shift = shift % LANES
    return pltpu.roll(x, shift, x.ndim - 1) if shift else x


def lane_of(shape):
    return lax.broadcasted_iota(jnp.int32, shape, len(shape) - 1)


def split(value):
    hi = value.astype(BF16)
    return hi, (value - hi.astype(F32)).astype(BF16)


def target_column(shape, first, members, cols):
    chunks = LANES // members
    fine = (cols + 2 * HALO) // chunks
    lane = lax.broadcasted_iota(jnp.int32, shape, 1)
    return fine * (lane % chunks) + first - HALO, lane // chunks


def fill_selectors(to_fields, to_weights, back, members, cols):
    fine = back.shape[0] // LANES

    def mark(hit):
        return jnp.where(hit, 1.0, 0.0).astype(BF16)

    for first in range(fine):
        lanes = slice(first * LANES, (first + 1) * LANES)
        shape = (cols, LANES)
        column, member = target_column(shape, first, members, cols)
        row = lax.broadcasted_iota(jnp.int32, shape, 0)
        here = row == column
        for m in range(members):
            to_fields[m * cols : (m + 1) * cols, lanes] = mark(here & (member == m))
        for part in range(2):
            to_weights[part * cols : (part + 1) * cols, lanes] = mark(here)
        shape = (2 * LANES, LANES)
        column, member = target_column(shape, first, members, cols)
        row = lax.broadcasted_iota(jnp.int32, shape, 0)
        base = jnp.where(column < 0, column + HALO, jnp.where(column >= cols, column - cols + LANES, -4 * LANES))
        to_fields[members * cols :, lanes] = mark(row == base + HALO * member)
        hi = base + HALO * members
        to_weights[2 * cols :, lanes] = mark((row == hi) | (row == hi + HALO))
        shape = (LANES, cols)
        lane = lax.broadcasted_iota(jnp.int32, shape, 0)
        column = fine * (lane % (LANES // members)) + first - HALO
        back[lanes, :] = mark(lax.broadcasted_iota(jnp.int32, shape, 1) == column)


def facing(value):
    return jnp.swapaxes(value.astype(F32), 0, 1)


def start_kernel(place, p_hbm, increment_hbm, taper_hbm, to_near, to_far, to_left, to_right, p, g, taper, increment, sems):
    members, levels, rows, cols = p.shape
    copies = []
    for i in (0, rows // HALO - 1, *range(1, rows // HALO - 1)):
        pick = slice(i * HALO, (i + 1) * HALO)
        copies.append((pick, [
            pltpu.make_async_copy(p_hbm.at[:, :, pick, :], p.at[:, :, pick, :], sems.at[i, 0]),
            pltpu.make_async_copy(increment_hbm.at[:, pick, :], increment.at[:, pick, :], sems.at[i, 1]),
            pltpu.make_async_copy(taper_hbm.at[:, pick, :], taper.at[:, pick, :], sems.at[i, 2]),
        ]))
    for _, group in copies:
        for copy in group:
            copy.start()

    def strip(out, pick, order):
        def put(pair, lanes, field, first=0):
            rows_at = slice(first + 2 * pair * levels, first + 2 * (pair + 1) * levels)
            both = jnp.concatenate([field[order[2 * pair]], field[order[2 * pair + 1]]], axis=0)
            out[rows_at, lanes] = both.astype(BF16)

        for half in range(2):
            lanes = slice(half * LANES, (half + 1) * LANES)
            weight = facing(g[:, pick, lanes])
            hi = weight.astype(BF16).astype(F32)
            for k, part in enumerate((hi, weight - hi)):
                for pair in range(NEAR // 2):
                    put(pair, slice(members * cols, members * cols + LANES), part, (2 * k + half) * NEAR * levels)
            for m in range(members):
                to = slice(m * cols + half * LANES, m * cols + (half + 1) * LANES)
                field = facing(p[m, :, pick, lanes])
                for pair in range(HALO // 2):
                    put(pair, to, field if 2 * pair < NEAR else field * weight)

    def packed(pick, column, shift):
        fields = [p[m, :, pick, column].astype(F32) for m in range(members)]
        hi, lo = split(g[:, pick, column])
        fields += [hi.astype(F32), lo.astype(F32)]
        lane = lane_of(fields[0].shape)
        total = jnp.zeros_like(fields[0])
        for e, field in enumerate(fields):
            inside = (lane >= HALO * e) & (lane < HALO * (e + 1))
            total = jnp.where(inside, roll(field, shift + HALO * e), total)
        return total.astype(BF16)

    for k, (pick, group) in enumerate(copies):
        for copy in group:
            copy.wait()
        g[:, pick, :] = increment[:, pick, :] * taper[:, pick, :]
        if k < 2:
            order = range(HALO) if k == 0 else range(HALO - 1, -1, -1)

            @pl.when(place[1] == k)
            def _():
                strip(to_near, pick, order)

            @pl.when(place[1] != k)
            def _():
                strip(to_far, pick, order)
        to_left[:, pick, :] = packed(pick, slice(0, LANES), 0)
        to_right[:, pick, :] = packed(pick, slice(cols - LANES, cols), HALO)


def corners_kernel(top, bottom, to_left, to_right):
    count = top.shape[0]
    pairs = count // 16
    for edge, strip in enumerate((top, bottom)):
        main = strip.shape[1] - LANES
        members = main // (2 * LANES)
        for pair in range(pairs):
            rows = slice(16 * pair, 16 * (pair + 1))
            out = slice(edge * count + 16 * pair, edge * count + 16 * (pair + 1))
            fields = [
                [strip[rows, (2 * m + half) * LANES : (2 * m + half + 1) * LANES].astype(F32) for m in range(members)]
                for half in range(2)
            ]
            if 2 * pair < NEAR:
                for half in range(2):
                    for k in range(2):
                        first = (2 * k + half) * (count // 4) + 16 * pair
                        fields[half].append(strip[first : first + 16, main:].astype(F32))
            lane = lane_of((16, LANES))
            for ref, half, shift in ((to_left, 0, 0), (to_right, 1, HALO)):
                total = jnp.zeros((16, LANES), F32)
                for e, field in enumerate(fields[half]):
                    inside = (lane >= HALO * e) & (lane < HALO * (e + 1))
                    total = jnp.where(inside, roll(field, shift + HALO * e), total)
                ref[out, :] = total.astype(BF16)


def turned(value):
    levels, rows, lanes = value.shape
    return jnp.swapaxes(value.astype(F32), 0, 1).reshape(rows * levels, lanes)


def factors(kappa, count):
    denominator = 1.0 + 4.0 * kappa
    scale = kappa / denominator
    for _ in range(4):
        scale = scale * scale
    return 1.0 / kappa, denominator / (kappa * kappa), scale / (count - 1)


def row_of(ref, *where):
    return lambda c: ref[(*where, c + 2)]


def first_sweep(x, x_next, v, linear, fine):
    v_next = {c: x(c) + x_next(c + 1) for c in range(-2, fine + 1)}
    if v is None:
        return v_next, None
    u = {c: linear * x(c) + v[c] + v_next[c - 1] for c in range(-1, fine + 1)}
    return v_next, u


def second_sweep(x, u, u_next, q, constant, fine):
    q_next = {c: u[c] + u_next[c + 1] for c in range(-1, fine)}
    if q is None:
        return q_next, None
    return q_next, [constant * x(c) + q[c] + q_next[c - 1] for c in range(fine)]


def wrap_columns(source, target, fine):
    for c in (0, 1):
        target(fine + c, roll(source(c), -1))
        target(c - 2, roll(source(fine - 2 + c), 1))


def finish(sums, back, scale, taper_of, write, levels):
    hi, lo = split(sums)
    total = jnp.dot(hi, back, preferred_element_type=F32) + jnp.dot(lo, back, preferred_element_type=F32)
    count = total.shape[0] // levels
    for half in range(total.shape[1] // LANES):
        lanes = slice(half * LANES, (half + 1) * LANES)
        part = total[:, lanes].reshape(count, levels, LANES) * scale
        natural = jnp.swapaxes(part, 0, 1) * taper_of(lanes)
        write(natural, lanes)


def to_owner(place, natural, keep, send, pick, lanes, levels):
    core, plane = place[2], place[3]
    for level in range(levels):
        owner_plane, owner_core, within = level // 4, level // 2 % 2, level % 2
        slot = jnp.where(plane == owner_plane, 0, 2) + within

        @pl.when(core == owner_core)
        def _():
            keep[slot, pick, lanes] = natural[level]

        @pl.when(core != owner_core)
        def _():
            send[slot, pick, lanes] = natural[level]


def dot(a, b):
    return jnp.dot(a, b, preferred_element_type=F32)


def prepare_kernel(p, g, own_values, own_weights, to_fields, to_weights, back, fields, weights):
    members, levels, rows, cols = p.shape
    fine = back.shape[0] // LANES
    fill_selectors(to_fields, to_weights, back, members, cols)
    for i in range(rows // HALO):
        pick = slice(i * HALO, (i + 1) * HALO)
        out = slice(i * HALO * levels, (i + 1) * HALO * levels)
        for half in range(cols // LANES):
            lanes = slice(half * LANES, (half + 1) * LANES)
            for m in range(members):
                to = slice(m * cols + half * LANES, m * cols + (half + 1) * LANES)
                fields[out, to] = turned(p[m, :, pick, lanes]).astype(BF16)
            hi, lo = split(turned(g[:, pick, lanes]))
            weights[out, lanes] = hi
            weights[out, cols + half * LANES : cols + (half + 1) * LANES] = lo
    for first in range(0, fine, 2):
        width = min(2, fine - first)
        lanes = slice(first * LANES, (first + width) * LANES)
        field = dot(fields[...], to_fields[: members * cols, lanes])
        weight = dot(weights[...], to_weights[: 2 * cols, lanes])
        for k in range(width):
            pick = slice(k * LANES, (k + 1) * LANES)
            own_values[:, first + k] = field[:, pick].reshape(rows, levels, LANES)
            own_weights[:, first + k] = weight[:, pick].reshape(rows, levels, LANES)


def inner_kernel(
    place, own_values, own_weights, taper, left, right, to_fields, to_weights, back, kappa,
    keep, send, edges, edge_values,
    x, values, packs,
):
    levels, rows, cols = taper.shape
    fine = x.shape[1] - 4
    members = LANES * fine // (cols + 2 * HALO)
    for i in range(rows // HALO):
        out = slice(i * HALO * levels, (i + 1) * HALO * levels)
        for side, ref in enumerate((left, right)):
            lanes = slice(side * LANES, (side + 1) * LANES)
            packs[out, lanes] = turned(ref[:, i * HALO : (i + 1) * HALO, :]).astype(BF16)
    for first in range(0, fine, 2):
        width = min(2, fine - first)
        lanes = slice(first * LANES, (first + width) * LANES)
        field = dot(packs[...], to_fields[members * cols :, lanes])
        weight = dot(packs[...], to_weights[2 * cols :, lanes])
        for k in range(width):
            pick = slice(k * LANES, (k + 1) * LANES)
            value = own_values[:, first + k] + field[:, pick].reshape(rows, levels, LANES)
            values[:, first + k] = value
            x[:, 2 + first + k] = value * (own_weights[:, first + k] + weight[:, pick].reshape(rows, levels, LANES))
    upper, lower = place[1], 1 - place[1]
    for k in range(HALO):
        edge_values[upper, k] = values[k]
        edge_values[lower, k] = values[rows - 1 - k]

    linear, constant, scale = factors(kappa[...], 4 * members)

    def wrap(row):
        def target(c, value):
            x[row, c + 2] = value

        wrap_columns(row_of(x, row), target, fine)

    def wrap_first(row, _):
        wrap(row)
        return 0

    lax.fori_loop(0, rows, wrap_first, 0, unroll=True)

    for turn in range(PASSES):
        low = 2 * turn
        start, count = low + 2, rows - 4 * turn - 4
        for k in range(4):
            edges[upper, turn, k] = x[low + k]
            edges[lower, turn, k] = x[rows - 1 - low - k]

        v, _ = first_sweep(row_of(x, start - 2), row_of(x, start - 1), None, linear, fine)
        v, u = first_sweep(row_of(x, start - 1), row_of(x, start), v, linear, fine)
        v, u_next = first_sweep(row_of(x, start), row_of(x, start + 1), v, linear, fine)
        q, _ = second_sweep(None, u, u_next, None, constant, fine)
        u = u_next
        for i in range(start, start + count):
            v, u_next = first_sweep(row_of(x, i + 1), row_of(x, i + 2), v, linear, fine)
            q, y = second_sweep(row_of(x, i), u, u_next, q, constant, fine)
            u = u_next
            for c in range(fine):
                x[i, c + 2] = y[c]
            if turn < PASSES - 1:
                wrap(i)

    def last(i, _):
        first = i * HALO
        from_row = first + HALO
        product = jnp.concatenate(
            [
                (x[pl.ds(from_row, HALO), c + 2] * values[pl.ds(from_row, HALO), c]).reshape(HALO * levels, LANES)
                for c in range(fine)
            ],
            axis=1,
        )
        pick = pl.ds(pl.multiple_of(first, HALO), HALO)
        finish(
            product, back[...], scale,
            lambda lanes: taper[:, pl.ds(pl.multiple_of(from_row, HALO), HALO), lanes],
            lambda natural, lanes: to_owner(place, natural, keep, send, pick, lanes, levels),
            levels,
        )
        return 0

    lax.fori_loop(0, (rows - 2 * HALO) // HALO, last, 0)


def lift_kernel(top, bottom, to_fields, to_weights, main_values, main_weights):
    fine, levels = main_values.shape[2:4]
    count = top.shape[0]
    main = top.shape[1] - LANES
    for first in range(0, fine, 2):
        width = min(2, fine - first)
        lanes = slice(first * LANES, (first + width) * LANES)
        for edge, strip in enumerate((top, bottom)):
            field = dot(strip[:, :main], to_fields[:main, lanes])
            part = count // 4
            near = jnp.concatenate([strip[k * part : (k + 1) * part, main:] for k in range(4)], axis=1)
            weight = dot(near, to_weights[: 4 * LANES, lanes])
            for k in range(width):
                pick = slice(k * LANES, (k + 1) * LANES)
                main_values[edge, :, first + k] = field[:, pick].reshape(HALO, levels, LANES)
                main_weights[edge, :, first + k] = weight[:, pick].reshape(NEAR, levels, LANES)


def outer_kernel(
    place, taper, left, right, main_values, main_weights, edges, edge_values,
    to_fields, to_weights, back, kappa,
    keep, send,
    x,
):
    levels, rows, cols = taper.shape
    fine = edge_values.shape[2]
    members = LANES * fine // (cols + 2 * HALO)
    linear, constant, scale = factors(kappa[...], 4 * members)
    inside = jnp.where(place[0] == 1, 0.0, 1.0).astype(F32)
    packs = jnp.concatenate([left[...], right[...]], axis=1)
    size = HALO * levels
    near_packs = jnp.concatenate([packs[edge * size : edge * size + NEAR * levels] for edge in range(2)], axis=0)
    for first in range(0, fine, 2):
        width = min(2, fine - first)
        lanes = slice(first * LANES, (first + width) * LANES)
        field = dot(packs, to_fields[members * cols :, lanes])
        weight = dot(near_packs, to_weights[2 * cols :, lanes])
        for k in range(width):
            pick = slice(k * LANES, (k + 1) * LANES)
            part = field[:, pick].reshape(2, HALO, levels, LANES)
            near = weight[:, pick].reshape(2, NEAR, levels, LANES)
            for edge in range(2):
                for distance in range(HALO):
                    value = main_values[edge, distance, first + k] + part[edge, distance]
                    if distance < NEAR:
                        value = value * (main_weights[edge, distance, first + k] + near[edge, distance])
                    if edge == 1 and distance == 0:
                        value = value * inside
                    x[edge, HALO - 1 - distance, 2 + first + k] = value


    def wrap(edge, row):
        def target(c, value):
            x[edge, row, c + 2] = value

        wrap_columns(row_of(x, edge, row), target, fine)

    for row in range(HALO):
        for edge in range(2):
            wrap(edge, row)

    for turn in range(PASSES):
        low = 2 * turn
        for edge in range(2):
            def row_at(row):
                if row < low + HALO:
                    return row_of(x, edge, row)
                return row_of(edges, edge, turn, row - low - HALO)

            v = u = q = None
            for i in range(low, low + HALO + 3):
                v, u_next = first_sweep(row_at(i), row_at(i + 1), v, linear, fine)
                if u_next is None:
                    continue
                if edge == 1 and i == HALO - 1:
                    u_next = {c: part * inside for c, part in u_next.items()}
                if u is not None:
                    q, y = second_sweep(row_at(i - 1), u, u_next, q, constant, fine)
                    if y is not None:
                        for c in range(fine):
                            x[edge, i - 1, c + 2] = y[c] * inside if edge == 1 and i == HALO else y[c]
                u = u_next
            if turn < PASSES - 1:
                for row in range(low + 2, low + HALO + 2):
                    wrap(edge, row)

    for edge in range(2):
        order = range(HALO) if edge == 0 else range(HALO - 1, -1, -1)
        slot = place[1] if edge == 0 else 1 - place[1]
        product = jnp.concatenate(
            [
                jnp.concatenate([x[slot, HALO + k, c + 2] * edge_values[slot, k, c] for k in order], axis=0)
                for c in range(fine)
            ],
            axis=1,
        )
        own = slice(edge * (rows - HALO), edge * (rows - HALO) + HALO)
        pick = slice(edge * HALO, (edge + 1) * HALO)
        finish(
            product, back[...], scale,
            lambda lanes: taper[:, own, lanes],
            lambda natural, lanes: to_owner(place, natural, keep, send, pick, lanes, levels),
            levels,
        )


def shifted(value, axis, step, wrap):
    count = lax.axis_size(axis)
    pairs = [(i, (i + step) % count) for i in range(count) if wrap or 0 <= i + step < count]
    return lax.ppermute(value, axis, pairs)


def over_core(keep, send):
    got = lax.ppermute(send, "mem", [(i, i ^ 1) for i in range(4)])
    return keep[:2] + got[:2], keep[2:] + got[2:]


def over_plane(here, there):
    return here + lax.ppermute(there, "mem", [(i, i ^ 2) for i in range(4)])


def local(perturbations, increment, taper_norm, kappa):
    members, levels, rows, cols = perturbations.shape
    fine = (cols + 2 * HALO) * members // LANES
    shape = jax.ShapeDtypeStruct
    tile = (levels, LANES)
    vmem = pl.BlockSpec(memory_space=pltpu.VMEM)
    smem = pl.BlockSpec(memory_space=pltpu.SMEM)
    hbm = pl.BlockSpec(memory_space=pltpu.HBM)

    def call(kernel, name, outs, ins, scratch=(), specs=None):
        return pl.pallas_call(
            kernel,
            out_shape=tuple(outs),
            in_specs=specs or [vmem] * len(ins),
            out_specs=(vmem,) * len(outs),
            scratch_shapes=list(scratch),
            compiler_params=pltpu.CompilerParams(vmem_limit_bytes=20 * 1024 * 1024),
            name=name,
        )(*ins)

    strip = shape((HALO * levels, members * cols + LANES), BF16)
    pack = shape((levels, rows, LANES), BF16)
    whole = shape((levels, rows, cols), F32)
    kappa = jnp.broadcast_to(kappa[:, None], tile)
    lat, mem = lax.axis_index("lat"), lax.axis_index("mem")
    count = lax.axis_size("lat")
    place = jnp.stack([
        ((lat == 0) | (lat == count - 1)).astype(jnp.int32),
        1 - lat % 2,
        mem % 2,
        mem // 2,
    ])

    to_near, to_far, to_left, to_right, p, g = call(
        start_kernel, "start",
        (strip, strip, pack, pack, shape(perturbations.shape, BF16), whole),
        (place, *(pltpu.with_memory_space_constraint(a, pltpu.HBM) for a in (perturbations, increment, taper_norm))),
        (pltpu.VMEM(whole.shape, F32), pltpu.VMEM(whole.shape, F32), pltpu.SemaphoreType.DMA((rows // HALO, 3))),
        specs=[smem] + [hbm] * 3,
    )
    near = lax.ppermute(to_near, "lat", [(i, i ^ 1) for i in range(count)])
    far = lax.ppermute(to_far, "lat", [(i, (i + 1 - 2 * (1 - i % 2)) % count) for i in range(count)])
    left = shifted(to_right, "lon", 1, True)
    right = shifted(to_left, "lon", -1, True)

    values = shape((rows, fine, *tile), F32)
    own_values, own_weights, to_fields, to_weights, back = call(
        prepare_kernel, "prepare",
        (
            values, values,
            shape((members * cols + 2 * LANES, fine * LANES), BF16),
            shape((2 * cols + 2 * LANES, fine * LANES), BF16),
            shape((fine * LANES, cols), BF16),
        ),
        (p, g),
        (pltpu.VMEM((rows * levels, members * cols), BF16), pltpu.VMEM((rows * levels, 2 * cols), BF16)),
    )

    part = shape((levels // 2, rows - 2 * HALO, cols), F32)
    keep, send, edges, edge_values = call(
        inner_kernel, "inner",
        (part, part, shape((2, PASSES, 4, fine + 4, *tile), F32), shape((2, HALO, fine, *tile), F32)),
        (place, own_values, own_weights, taper_norm, left, right, to_fields, to_weights, back, kappa),
        (
            pltpu.VMEM((rows, fine + 4, *tile), F32),
            pltpu.VMEM((rows, fine, *tile), F32),
            pltpu.VMEM((rows * levels, 2 * LANES), BF16),
        ),
        specs=[smem] + [vmem] * 9,
    )
    near, far, edges = lax.optimization_barrier((near, far, edges))

    side = shape((2 * HALO * levels, LANES), BF16)
    to_left, to_right = call(corners_kernel, "corners", (side, side), (near, far))
    left = shifted(to_right, "lon", 1, True)
    right = shifted(to_left, "lon", -1, True)
    near, far, send, to_left, _ = lax.optimization_barrier((near, far, send, to_left, to_right))
    here, there = over_core(keep, send)
    main_values, main_weights = call(
        lift_kernel, "lift",
        (shape((2, HALO, fine, *tile), F32), shape((2, NEAR, fine, *tile), F32)),
        (near, far, to_fields, to_weights),
    )
    here, there, edges = lax.optimization_barrier((here, there, edges))
    middle = over_plane(here, there)
    part = shape((levels // 2, 2 * HALO, cols), F32)
    keep, send = call(
        outer_kernel, "outer",
        (part, part),
        (
            place, taper_norm, left, right, main_values, main_weights, edges, edge_values,
            to_fields, to_weights, back, kappa,
        ),
        (pltpu.VMEM((2, 2 * HALO, fine + 4, *tile), F32),),
        specs=[smem] + [vmem] * 11,
    )
    outside = over_plane(*over_core(keep, send))
    return jnp.concatenate([outside[:, :HALO], middle, outside[:, HALO:]], axis=1)


def solution(mesh):
    return jax.shard_map(
        local,
        mesh=mesh,
        in_specs=(P("mem", None, "lat", "lon"), P(None, "lat", "lon"), P(None, "lat", "lon"), P()),
        out_specs=P("mem", "lat", "lon"),
        check_vma=False,
    )
```

```python
import jax
import jax.numpy as jnp
from jax import lax
from jax.experimental import pallas as pl
from jax.experimental.pallas import tpu as pltpu
from jax.sharding import PartitionSpec as P

PASSES = 8
HALO = 2 * PASSES
LANES = 128
NEAR = 4
INNER_FLOPS = 4 * 10**9
BF16 = jnp.bfloat16
F32 = jnp.float32


def roll(x, shift):
    shift = shift % LANES
    return pltpu.roll(x, shift, x.ndim - 1) if shift else x


def lane_of(shape):
    return lax.broadcasted_iota(jnp.int32, shape, len(shape) - 1)


def split(value):
    hi = value.astype(BF16)
    return hi, (value - hi.astype(F32)).astype(BF16)


def target_column(shape, first, members, cols):
    chunks = LANES // members
    fine = (cols + 2 * HALO) // chunks
    lane = lax.broadcasted_iota(jnp.int32, shape, 1)
    return fine * (lane % chunks) + first - HALO, lane // chunks


def fill_selectors(to_fields, to_weights, back, members, cols):
    fine = back.shape[0] // LANES

    def mark(hit):
        return jnp.where(hit, 1.0, 0.0).astype(BF16)

    for first in range(fine):
        lanes = slice(first * LANES, (first + 1) * LANES)
        shape = (cols, LANES)
        column, member = target_column(shape, first, members, cols)
        row = lax.broadcasted_iota(jnp.int32, shape, 0)
        here = row == column
        for m in range(members):
            to_fields[m * cols : (m + 1) * cols, lanes] = mark(here & (member == m))
        for part in range(2):
            to_weights[part * cols : (part + 1) * cols, lanes] = mark(here)
        shape = (2 * LANES, LANES)
        column, member = target_column(shape, first, members, cols)
        row = lax.broadcasted_iota(jnp.int32, shape, 0)
        base = jnp.where(column < 0, column + HALO, jnp.where(column >= cols, column - cols + LANES, -4 * LANES))
        to_fields[members * cols :, lanes] = mark(row == base + HALO * member)
        hi = base + HALO * members
        to_weights[2 * cols :, lanes] = mark((row == hi) | (row == hi + HALO))
        shape = (LANES, cols)
        lane = lax.broadcasted_iota(jnp.int32, shape, 0)
        column = fine * (lane % (LANES // members)) + first - HALO
        back[lanes, :] = mark(lax.broadcasted_iota(jnp.int32, shape, 1) == column)


def facing(value):
    return jnp.swapaxes(value.astype(F32), 0, 1)


def write_strip(out, p, g, pick, order, packs=()):
    members, levels, _, cols = p.shape
    main = members * cols

    def put(pair, lanes, field, first=0):
        rows = slice(first + 2 * pair * levels, first + 2 * (pair + 1) * levels)
        both = jnp.concatenate([field[order[2 * pair]], field[order[2 * pair + 1]]], axis=0)
        out[rows, lanes] = both.astype(BF16)

    for half in range(2):
        lanes = slice(half * LANES, (half + 1) * LANES)
        weight = facing(g[:, pick, lanes])
        hi = weight.astype(BF16).astype(F32)
        for k, part in enumerate((hi, weight - hi)):
            for pair in range(NEAR // 2):
                put(pair, slice(main, main + LANES), part, (2 * k + half) * NEAR * levels)
        for m in range(members):
            to = slice(m * cols + half * LANES, m * cols + (half + 1) * LANES)
            field = facing(p[m, :, pick, lanes])
            product = field * weight
            for pair in range(HALO // 2):
                put(pair, to, field if 2 * pair < NEAR else product)
    for k, side in enumerate(packs):
        field = facing(side[:, pick, :])
        lane = lane_of(field.shape)
        weight = field + roll(field, -HALO)
        total = jnp.zeros_like(field)
        for m in range(members):
            inside = (lane >= HALO * m) & (lane < HALO * (m + 1))
            total = jnp.where(inside, roll(weight, HALO * (m - members)), total)
        product = field * total
        to = slice(main + (k + 1) * LANES, main + (k + 2) * LANES)
        for pair in range(HALO // 2):
            put(pair, to, field if 2 * pair < NEAR else product)


def start_kernel(place, p_hbm, increment_hbm, taper_hbm, to_near, to_left, to_right, p, g, taper, increment, sems):
    members, levels, rows, cols = p.shape
    copies = []
    for i in (0, rows // HALO - 1, *range(1, rows // HALO - 1)):
        pick = slice(i * HALO, (i + 1) * HALO)
        copies.append((pick, [
            pltpu.make_async_copy(p_hbm.at[:, :, pick, :], p.at[:, :, pick, :], sems.at[i, 0]),
            pltpu.make_async_copy(increment_hbm.at[:, pick, :], increment.at[:, pick, :], sems.at[i, 1]),
            pltpu.make_async_copy(taper_hbm.at[:, pick, :], taper.at[:, pick, :], sems.at[i, 2]),
        ]))
    for _, group in copies:
        for copy in group:
            copy.start()

    def packed(pick, column, shift):
        fields = [p[m, :, pick, column].astype(F32) for m in range(members)]
        hi, lo = split(g[:, pick, column])
        fields += [hi.astype(F32), lo.astype(F32)]
        lane = lane_of(fields[0].shape)
        total = jnp.zeros_like(fields[0])
        for e, field in enumerate(fields):
            inside = (lane >= HALO * e) & (lane < HALO * (e + 1))
            total = jnp.where(inside, roll(field, shift + HALO * e), total)
        return total.astype(BF16)

    for k, (pick, group) in enumerate(copies):
        for copy in group:
            copy.wait()
        g[:, pick, :] = increment[:, pick, :] * taper[:, pick, :]
        if k < 2:
            order = range(HALO) if k == 0 else range(HALO - 1, -1, -1)

            @pl.when(place[1] == k)
            def _():
                write_strip(to_near, p, g, pick, order)
        to_left[:, pick, :] = packed(pick, slice(0, LANES), 0)
        to_right[:, pick, :] = packed(pick, slice(cols - LANES, cols), HALO)


def far_kernel(place, p, g, left, right, to_far):
    rows = p.shape[2]
    for k in range(2):
        pick = slice(k * (rows - HALO), k * (rows - HALO) + HALO)
        order = range(HALO) if k == 0 else range(HALO - 1, -1, -1)

        @pl.when(place[1] != k)
        def _():
            write_strip(to_far, p, g, pick, order, (left, right))


def corners_kernel(strip, to_left, to_right):
    count = strip.shape[0]
    main = strip.shape[1] - LANES
    members = main // (2 * LANES)
    for pair in range(count // 16):
        rows = slice(16 * pair, 16 * (pair + 1))
        fields = [
            [strip[rows, (2 * m + half) * LANES : (2 * m + half + 1) * LANES].astype(F32) for m in range(members)]
            for half in range(2)
        ]
        if 2 * pair < NEAR:
            for half in range(2):
                for k in range(2):
                    first = (2 * k + half) * (count // 4) + 16 * pair
                    fields[half].append(strip[first : first + 16, main:].astype(F32))
        lane = lane_of((16, LANES))
        for ref, half, shift in ((to_left, 0, 0), (to_right, 1, HALO)):
            total = jnp.zeros((16, LANES), F32)
            for e, field in enumerate(fields[half]):
                inside = (lane >= HALO * e) & (lane < HALO * (e + 1))
                total = jnp.where(inside, roll(field, shift + HALO * e), total)
            ref[rows, :] = total.astype(BF16)


def turned(value):
    levels, rows, lanes = value.shape
    return jnp.swapaxes(value.astype(F32), 0, 1).reshape(rows * levels, lanes)


def factors(kappa, count):
    denominator = 1.0 + 4.0 * kappa
    scale = kappa / denominator
    for _ in range(4):
        scale = scale * scale
    return 1.0 / kappa, denominator / (kappa * kappa), scale / (count - 1)


def row_of(ref, *where):
    return lambda c: ref[(*where, c + 2)]


def first_sweep(x, x_next, v, linear, fine):
    v_next = {c: x(c) + x_next(c + 1) for c in range(-2, fine + 1)}
    if v is None:
        return v_next, None
    u = {c: linear * x(c) + v[c] + v_next[c - 1] for c in range(-1, fine + 1)}
    return v_next, u


def second_sweep(x, u, u_next, q, constant, fine):
    q_next = {c: u[c] + u_next[c + 1] for c in range(-1, fine)}
    if q is None:
        return q_next, None
    return q_next, [constant * x(c) + q[c] + q_next[c - 1] for c in range(fine)]


def wrap_columns(source, target, fine):
    for c in (0, 1):
        target(fine + c, roll(source(c), -1))
        target(c - 2, roll(source(fine - 2 + c), 1))


def finish(sums, back, scale, taper_of, write, levels):
    hi, lo = split(sums)
    total = jnp.dot(hi, back, preferred_element_type=F32) + jnp.dot(lo, back, preferred_element_type=F32)
    count = total.shape[0] // levels
    for half in range(total.shape[1] // LANES):
        lanes = slice(half * LANES, (half + 1) * LANES)
        part = total[:, lanes].reshape(count, levels, LANES) * scale
        natural = jnp.swapaxes(part, 0, 1) * taper_of(lanes)
        write(natural, lanes)


def to_owner(place, natural, keep, send, pick, lanes, levels):
    core, plane = place[2], place[3]
    for level in range(levels):
        owner_plane, owner_core, within = level // 4, level // 2 % 2, level % 2
        slot = jnp.where(plane == owner_plane, 0, 2) + within

        @pl.when(core == owner_core)
        def _():
            keep[slot, pick, lanes] = natural[level]

        @pl.when(core != owner_core)
        def _():
            send[slot, pick, lanes] = natural[level]


def dot(a, b):
    return jnp.dot(a, b, preferred_element_type=F32)


def prepare_kernel(p, g, own_values, own_weights, to_fields, to_weights, back, fields, weights):
    members, levels, rows, cols = p.shape
    fine = back.shape[0] // LANES
    fill_selectors(to_fields, to_weights, back, members, cols)
    for i in range(rows // HALO):
        pick = slice(i * HALO, (i + 1) * HALO)
        out = slice(i * HALO * levels, (i + 1) * HALO * levels)
        for half in range(cols // LANES):
            lanes = slice(half * LANES, (half + 1) * LANES)
            for m in range(members):
                to = slice(m * cols + half * LANES, m * cols + (half + 1) * LANES)
                fields[out, to] = turned(p[m, :, pick, lanes]).astype(BF16)
            hi, lo = split(turned(g[:, pick, lanes]))
            weights[out, lanes] = hi
            weights[out, cols + half * LANES : cols + (half + 1) * LANES] = lo
    for first in range(0, fine, 2):
        width = min(2, fine - first)
        lanes = slice(first * LANES, (first + width) * LANES)
        field = dot(fields[...], to_fields[: members * cols, lanes])
        weight = dot(weights[...], to_weights[: 2 * cols, lanes])
        for k in range(width):
            pick = slice(k * LANES, (k + 1) * LANES)
            own_values[:, first + k] = field[:, pick].reshape(rows, levels, LANES)
            own_weights[:, first + k] = weight[:, pick].reshape(rows, levels, LANES)


def inner_kernel(
    place, own_values, own_weights, taper, left, right, to_fields, to_weights, back, kappa,
    keep, send, edges, edge_values,
    x, values, packs,
):
    levels, rows, cols = taper.shape
    fine = x.shape[1] - 4
    members = LANES * fine // (cols + 2 * HALO)
    for i in range(rows // HALO):
        out = slice(i * HALO * levels, (i + 1) * HALO * levels)
        for side, ref in enumerate((left, right)):
            lanes = slice(side * LANES, (side + 1) * LANES)
            packs[out, lanes] = turned(ref[:, i * HALO : (i + 1) * HALO, :]).astype(BF16)
    for first in range(0, fine, 2):
        width = min(2, fine - first)
        lanes = slice(first * LANES, (first + width) * LANES)
        field = dot(packs[...], to_fields[members * cols :, lanes])
        weight = dot(packs[...], to_weights[2 * cols :, lanes])
        for k in range(width):
            pick = slice(k * LANES, (k + 1) * LANES)
            value = own_values[:, first + k] + field[:, pick].reshape(rows, levels, LANES)
            values[:, first + k] = value
            x[:, 2 + first + k] = value * (own_weights[:, first + k] + weight[:, pick].reshape(rows, levels, LANES))
    upper, lower = place[1], 1 - place[1]
    for k in range(HALO):
        edge_values[upper, k] = values[k]
        edge_values[lower, k] = values[rows - 1 - k]

    linear, constant, scale = factors(kappa[...], 4 * members)

    def wrap(row):
        def target(c, value):
            x[row, c + 2] = value

        wrap_columns(row_of(x, row), target, fine)

    def wrap_first(row, _):
        wrap(row)
        return 0

    lax.fori_loop(0, rows, wrap_first, 0, unroll=True)

    for turn in range(PASSES):
        low = 2 * turn
        start, count = low + 2, rows - 4 * turn - 4
        for k in range(4):
            edges[upper, turn, k] = x[low + k]
            edges[lower, turn, k] = x[rows - 1 - low - k]

        v, _ = first_sweep(row_of(x, start - 2), row_of(x, start - 1), None, linear, fine)
        v, u = first_sweep(row_of(x, start - 1), row_of(x, start), v, linear, fine)
        v, u_next = first_sweep(row_of(x, start), row_of(x, start + 1), v, linear, fine)
        q, _ = second_sweep(None, u, u_next, None, constant, fine)
        u = u_next
        for i in range(start, start + count):
            v, u_next = first_sweep(row_of(x, i + 1), row_of(x, i + 2), v, linear, fine)
            q, y = second_sweep(row_of(x, i), u, u_next, q, constant, fine)
            u = u_next
            for c in range(fine):
                x[i, c + 2] = y[c]
            if turn < PASSES - 1:
                wrap(i)

    def last(i, _):
        first = i * HALO
        from_row = first + HALO
        product = jnp.concatenate(
            [
                (x[pl.ds(from_row, HALO), c + 2] * values[pl.ds(from_row, HALO), c]).reshape(HALO * levels, LANES)
                for c in range(fine)
            ],
            axis=1,
        )
        pick = pl.ds(pl.multiple_of(first, HALO), HALO)
        finish(
            product, back[...], scale,
            lambda lanes: taper[:, pl.ds(pl.multiple_of(from_row, HALO), HALO), lanes],
            lambda natural, lanes: to_owner(place, natural, keep, send, pick, lanes, levels),
            levels,
        )
        return 0

    lax.fori_loop(0, (rows - 2 * HALO) // HALO, last, 0)


def outer_kernel(
    place, taper, near, far, left, right, edges, edge_values, keep_inner, send_inner,
    to_fields, to_weights, back, kappa,
    keep, send,
    x,
):
    levels, rows, cols = taper.shape
    keep[:, HALO : rows - HALO, :] = keep_inner[...]
    send[:, HALO : rows - HALO, :] = send_inner[...]
    fine = edge_values.shape[2]
    members = LANES * fine // (cols + 2 * HALO)
    linear, constant, scale = factors(kappa[...], 4 * members)
    inside = jnp.where(place[0] == 1, 0.0, 1.0).astype(F32)
    main = members * cols
    part = NEAR * levels
    sides = [jnp.concatenate([left[...], right[...]], axis=1), far[:, main + LANES :]]
    fields = jnp.concatenate(
        [jnp.concatenate([strip[:, :main], side], axis=1) for strip, side in zip((near, far), sides)], axis=0
    )
    weights = jnp.concatenate(
        [
            jnp.concatenate(
                [strip[k * part : (k + 1) * part, main : main + LANES] for k in range(4)] + [side[:part]], axis=1
            )
            for strip, side in zip((near, far), sides)
        ],
        axis=0,
    )
    for first in range(0, fine, 2):
        width = min(2, fine - first)
        lanes = slice(first * LANES, (first + width) * LANES)
        field = dot(fields, to_fields[:, lanes])
        weight = dot(weights, to_weights[:, lanes])
        for k in range(width):
            pick = slice(k * LANES, (k + 1) * LANES)
            value_of = field[:, pick].reshape(2, HALO, levels, LANES)
            weight_of = weight[:, pick].reshape(2, NEAR, levels, LANES)
            for edge in range(2):
                for distance in range(HALO):
                    value = value_of[edge, distance]
                    if distance < NEAR:
                        value = value * weight_of[edge, distance]
                    if edge == 1 and distance == 0:
                        value = value * inside
                    x[edge, HALO - 1 - distance, 2 + first + k] = value

    def wrap(edge, row):
        def target(c, value):
            x[edge, row, c + 2] = value

        wrap_columns(row_of(x, edge, row), target, fine)

    for row in range(HALO):
        for edge in range(2):
            wrap(edge, row)

    for turn in range(PASSES):
        low = 2 * turn
        for edge in range(2):
            def row_at(row):
                if row < low + HALO:
                    return row_of(x, edge, row)
                return row_of(edges, edge, turn, row - low - HALO)

            v = u = q = None
            for i in range(low, low + HALO + 3):
                v, u_next = first_sweep(row_at(i), row_at(i + 1), v, linear, fine)
                if u_next is None:
                    continue
                if edge == 1 and i == HALO - 1:
                    u_next = {c: part * inside for c, part in u_next.items()}
                if u is not None:
                    q, y = second_sweep(row_at(i - 1), u, u_next, q, constant, fine)
                    if y is not None:
                        for c in range(fine):
                            x[edge, i - 1, c + 2] = y[c] * inside if edge == 1 and i == HALO else y[c]
                u = u_next
            if turn < PASSES - 1:
                for row in range(low + 2, low + HALO + 2):
                    wrap(edge, row)

    for edge in range(2):
        order = range(HALO) if edge == 0 else range(HALO - 1, -1, -1)
        slot = place[1] if edge == 0 else 1 - place[1]
        product = jnp.concatenate(
            [
                jnp.concatenate([x[slot, HALO + k, c + 2] * edge_values[slot, k, c] for k in order], axis=0)
                for c in range(fine)
            ],
            axis=1,
        )
        own = slice(edge * (rows - HALO), edge * (rows - HALO) + HALO)
        finish(
            product, back[...], scale,
            lambda lanes: taper[:, own, lanes],
            lambda natural, lanes: to_owner(place, natural, keep, send, own, lanes, levels),
            levels,
        )


def shifted(value, axis, step, wrap):
    count = lax.axis_size(axis)
    pairs = [(i, (i + step) % count) for i in range(count) if wrap or 0 <= i + step < count]
    return lax.ppermute(value, axis, pairs)


def over_core(keep, send):
    got = lax.ppermute(send, "mem", [(i, i ^ 1) for i in range(4)])
    return keep[:2] + got[:2], keep[2:] + got[2:]


def over_plane(here, there):
    return here + lax.ppermute(there, "mem", [(i, i ^ 2) for i in range(4)])


def local(perturbations, increment, taper_norm, kappa):
    members, levels, rows, cols = perturbations.shape
    fine = (cols + 2 * HALO) * members // LANES
    shape = jax.ShapeDtypeStruct
    tile = (levels, LANES)
    vmem = pl.BlockSpec(memory_space=pltpu.VMEM)
    smem = pl.BlockSpec(memory_space=pltpu.SMEM)
    hbm = pl.BlockSpec(memory_space=pltpu.HBM)

    def call(kernel, name, outs, ins, scratch=(), specs=None, cost=None):
        return pl.pallas_call(
            kernel,
            out_shape=tuple(outs),
            in_specs=specs or [vmem] * len(ins),
            out_specs=(vmem,) * len(outs),
            scratch_shapes=list(scratch),
            compiler_params=pltpu.CompilerParams(vmem_limit_bytes=20 * 1024 * 1024),
            cost_estimate=cost,
            name=name,
        )(*ins)

    def strip(blocks):
        return shape((HALO * levels, members * cols + blocks * LANES), BF16)

    pack = shape((levels, rows, LANES), BF16)
    whole = shape((levels, rows, cols), F32)
    kappa = jnp.broadcast_to(kappa[:, None], tile)
    lat, mem = lax.axis_index("lat"), lax.axis_index("mem")
    count = lax.axis_size("lat")
    place = jnp.stack([
        ((lat == 0) | (lat == count - 1)).astype(jnp.int32),
        1 - lat % 2,
        mem % 2,
        mem // 2,
    ])

    to_near, to_left, to_right, p, g = call(
        start_kernel, "start",
        (strip(1), pack, pack, shape(perturbations.shape, BF16), whole),
        (place, *(pltpu.with_memory_space_constraint(a, pltpu.HBM) for a in (perturbations, increment, taper_norm))),
        (pltpu.VMEM(whole.shape, F32), pltpu.VMEM(whole.shape, F32), pltpu.SemaphoreType.DMA((rows // HALO, 3))),
        specs=[smem] + [hbm] * 3,
    )
    near = lax.ppermute(to_near, "lat", [(i, i ^ 1) for i in range(count)])
    left = shifted(to_right, "lon", 1, True)
    right = shifted(to_left, "lon", -1, True)

    values = shape((rows, fine, *tile), F32)
    own_values, own_weights, to_fields, to_weights, back = call(
        prepare_kernel, "prepare",
        (
            values, values,
            shape((members * cols + 2 * LANES, fine * LANES), BF16),
            shape((2 * cols + 2 * LANES, fine * LANES), BF16),
            shape((fine * LANES, cols), BF16),
        ),
        (p, g),
        (pltpu.VMEM((rows * levels, members * cols), BF16), pltpu.VMEM((rows * levels, 2 * cols), BF16)),
    )

    p, g, own_values = lax.optimization_barrier((p, g, own_values))
    (to_far,) = call(far_kernel, "far", (strip(3),), (place, p, g, left, right), specs=[smem] + [vmem] * 4)
    far = lax.ppermute(to_far, "lat", [(i, (i + 1 - 2 * (1 - i % 2)) % count) for i in range(count)])
    near, to_far = lax.optimization_barrier((near, to_far))
    side = shape((HALO * levels, LANES), BF16)
    to_left, to_right = call(corners_kernel, "corners", (side, side), (near,))
    near_left = shifted(to_right, "lon", 1, True)
    near_right = shifted(to_left, "lon", -1, True)
    own_values, to_left = lax.optimization_barrier((own_values, to_left))

    part = shape((levels // 2, rows - 2 * HALO, cols), F32)
    keep, send, edges, edge_values = call(
        inner_kernel, "inner",
        (part, part, shape((2, PASSES, 4, fine + 4, *tile), F32), shape((2, HALO, fine, *tile), F32)),
        (place, own_values, own_weights, taper_norm, left, right, to_fields, to_weights, back, kappa),
        (
            pltpu.VMEM((rows, fine + 4, *tile), F32),
            pltpu.VMEM((rows, fine, *tile), F32),
            pltpu.VMEM((rows * levels, 2 * LANES), BF16),
        ),
        specs=[smem] + [vmem] * 9,
        cost=pl.CostEstimate(flops=INNER_FLOPS, bytes_accessed=1 << 20, transcendentals=0),
    )
    part = shape((levels // 2, rows, cols), F32)
    keep, send = call(
        outer_kernel, "outer",
        (part, part),
        (
            place, taper_norm, near, far, near_left, near_right, edges, edge_values, keep, send,
            to_fields, to_weights, back, kappa,
        ),
        (pltpu.VMEM((2, 2 * HALO, fine + 4, *tile), F32),),
        specs=[smem] + [vmem] * 13,
    )
    return over_plane(*over_core(keep, send))


def solution(mesh):
    return jax.shard_map(
        local,
        mesh=mesh,
        in_specs=(P("mem", None, "lat", "lon"), P(None, "lat", "lon"), P(None, "lat", "lon"), P()),
        out_specs=P("mem", "lat", "lon"),
        check_vma=False,
    )
```

```python
import jax
import jax.numpy as jnp
from jax import lax
from jax.experimental import pallas as pl
from jax.experimental.pallas import tpu as pltpu
from jax.sharding import PartitionSpec as P

PASSES = 8
HALO = 2 * PASSES
LANES = 128
NEAR = 4
INNER_FLOPS = 4 * 10**9
OUTER_FLOPS = 4 * 10**9
BF16 = jnp.bfloat16
F32 = jnp.float32


def roll(x, shift):
    shift = shift % LANES
    return pltpu.roll(x, shift, x.ndim - 1) if shift else x


def lane_of(shape):
    return lax.broadcasted_iota(jnp.int32, shape, len(shape) - 1)


def split(value):
    hi = value.astype(BF16)
    return hi, (value - hi.astype(F32)).astype(BF16)


def target_column(shape, first, members, cols):
    chunks = LANES // members
    fine = (cols + 2 * HALO) // chunks
    lane = lax.broadcasted_iota(jnp.int32, shape, 1)
    return fine * (lane % chunks) + first - HALO, lane // chunks


def fill_selectors(to_fields, to_weights, to_sides, back, members, cols):
    fine = back.shape[0] // LANES
    nowhere = -4 * LANES

    def mark(hit):
        return jnp.where(hit, 1.0, 0.0).astype(BF16)

    for first in range(fine):
        lanes = slice(first * LANES, (first + 1) * LANES)
        shape = (cols, LANES)
        column, member = target_column(shape, first, members, cols)
        row = lax.broadcasted_iota(jnp.int32, shape, 0)
        here = row == column
        for m in range(members):
            to_fields[m * cols : (m + 1) * cols, lanes] = mark(here & (member == m))
        for part in range(2):
            to_weights[part * cols : (part + 1) * cols, lanes] = mark(here)
        for ref, base, count, offsets in (
            (to_fields, members * cols, LANES, (0,)), (to_sides, 0, 2 * LANES, (0, LANES // 2)),
        ):
            shape = (count, LANES)
            column, member = target_column(shape, first, members, cols)
            row = lax.broadcasted_iota(jnp.int32, shape, 0)
            after = column - cols + count // 2
            at = jnp.where(column < 0, column + HALO, jnp.where(column >= cols, after, nowhere)) + HALO * member
            hit = row == at
            for offset in offsets[1:]:
                hit = hit | (row == at + offset)
            ref[base : base + count, lanes] = mark(hit)
        shape = (LANES, cols)
        lane = lax.broadcasted_iota(jnp.int32, shape, 0)
        column = fine * (lane % (LANES // members)) + first - HALO
        back[lanes, :] = mark(lax.broadcasted_iota(jnp.int32, shape, 1) == column)


def facing(value):
    return jnp.swapaxes(value.astype(F32), 0, 1)


def write_strip(out, p, g, pick, order, sides=None):
    members, levels, _, cols = p.shape

    def put(pair, lanes, field, first=0):
        rows = slice((first + 2 * pair) * levels, (first + 2 * pair + 2) * levels)
        both = jnp.concatenate([field[order[2 * pair]], field[order[2 * pair + 1]]], axis=0)
        out[rows, lanes] = both.astype(BF16)

    for half in range(2):
        lanes = slice(half * LANES, (half + 1) * LANES)
        weight = g[:, pick, lanes]
        for m in range(members):
            to = slice(m * cols + half * LANES, m * cols + (half + 1) * LANES)
            product = facing(p[m, :, pick, lanes].astype(F32) * weight)
            rest = product - product.astype(BF16).astype(F32)
            for pair in range(HALO // 2):
                put(pair, to, product)
            for pair in range(NEAR // 2):
                put(pair, to, rest, HALO)
    if sides is not None:
        left, right = (facing(side[:, pick, :]) for side in sides)
        lane = lane_of(left.shape)
        half = LANES // 2
        to = slice(members * cols, members * cols + LANES)
        product = jnp.where(lane < half, left, roll(right, half))
        rest = jnp.where(lane < half, roll(left, half), right)
        for pair in range(HALO // 2):
            put(pair, to, product)
        for pair in range(NEAR // 2):
            put(pair, to, rest, HALO)


def start_kernel(place, p_hbm, increment_hbm, taper_hbm, to_near, to_left, to_right, p, g, taper, increment, sems):
    members, levels, rows, cols = p.shape
    copies = []
    for i in (0, rows // HALO - 1, *range(1, rows // HALO - 1)):
        pick = slice(i * HALO, (i + 1) * HALO)
        copies.append((pick, [
            pltpu.make_async_copy(p_hbm.at[:, :, pick, :], p.at[:, :, pick, :], sems.at[i, 0]),
            pltpu.make_async_copy(increment_hbm.at[:, pick, :], increment.at[:, pick, :], sems.at[i, 1]),
            pltpu.make_async_copy(taper_hbm.at[:, pick, :], taper.at[:, pick, :], sems.at[i, 2]),
        ]))
    for _, group in copies:
        for copy in group:
            copy.start()

    def packed(pick, column, shift):
        products = [p[m, :, pick, column].astype(F32) * g[:, pick, column] for m in range(members)]
        products += [product - product.astype(BF16).astype(F32) for product in products]
        lane = lane_of(products[0].shape)
        total = jnp.zeros_like(products[0])
        for e, product in enumerate(products):
            inside = (lane >= HALO * e) & (lane < HALO * (e + 1))
            total = jnp.where(inside, roll(product, shift + HALO * e), total)
        return total.astype(BF16)

    for k, (pick, group) in enumerate(copies):
        for copy in group:
            copy.wait()
        g[:, pick, :] = increment[:, pick, :] * taper[:, pick, :]
        if k < 2:
            order = range(HALO) if k == 0 else range(HALO - 1, -1, -1)

            @pl.when(place[1] == k)
            def _():
                write_strip(to_near, p, g, pick, order)
        to_left[:, pick, :] = packed(pick, slice(0, LANES), 0)
        to_right[:, pick, :] = packed(pick, slice(cols - LANES, cols), HALO)


def far_kernel(place, p, g, left, right, to_far):
    rows = p.shape[2]
    for k in range(2):
        pick = slice(k * (rows - HALO), k * (rows - HALO) + HALO)
        order = range(HALO) if k == 0 else range(HALO - 1, -1, -1)

        @pl.when(place[1] != k)
        def _():
            write_strip(to_far, p, g, pick, order, (left, right))


def corners_kernel(strip, to_left, to_right):
    count, main = strip.shape
    members = main // (2 * LANES)
    for first in range(0, count, 16):
        rows = slice(first, first + 16)
        lane = lane_of((16, LANES))
        for ref, half, base, shift in ((to_left, 0, LANES // 2, 0), (to_right, 1, 0, HALO)):
            total = jnp.zeros((16, LANES), F32)
            for m in range(members):
                field = strip[rows, (2 * m + half) * LANES : (2 * m + half + 1) * LANES].astype(F32)
                at = base + HALO * m
                total = jnp.where((lane >= at) & (lane < at + HALO), roll(field, shift + at), total)
            ref[rows, :] = total.astype(BF16)


def turned(value):
    levels, rows, lanes = value.shape
    return jnp.swapaxes(value.astype(F32), 0, 1).reshape(rows * levels, lanes)


def factors(kappa, count):
    denominator = 1.0 + 4.0 * kappa
    scale = kappa / denominator
    for _ in range(4):
        scale = scale * scale
    return 1.0 / kappa, denominator / (kappa * kappa), scale / (count - 1)


def row_of(ref, *where):
    return lambda c: ref[(*where, c + 2)]


def first_sweep(x, x_next, v, linear, fine):
    v_next = {c: x(c) + x_next(c + 1) for c in range(-2, fine + 1)}
    if v is None:
        return v_next, None
    u = {c: linear * x(c) + v[c] + v_next[c - 1] for c in range(-1, fine + 1)}
    return v_next, u


def second_sweep(x, u, u_next, q, constant, fine):
    q_next = {c: u[c] + u_next[c + 1] for c in range(-1, fine)}
    if q is None:
        return q_next, None
    return q_next, [constant * x(c) + q[c] + q_next[c - 1] for c in range(fine)]


def wrap_columns(source, target, fine):
    for c in (0, 1):
        target(fine + c, roll(source(c), -1))
        target(c - 2, roll(source(fine - 2 + c), 1))


def finish(sums, back, scale, taper_of, write, levels):
    hi, lo = split(sums)
    total = jnp.dot(hi, back, preferred_element_type=F32) + jnp.dot(lo, back, preferred_element_type=F32)
    count = total.shape[0] // levels
    for half in range(total.shape[1] // LANES):
        lanes = slice(half * LANES, (half + 1) * LANES)
        part = total[:, lanes].reshape(count, levels, LANES) * scale
        natural = jnp.swapaxes(part, 0, 1) * taper_of(lanes)
        write(natural, lanes)


def to_owner(place, natural, keep, send, pick, lanes, levels):
    core, plane = place[2], place[3]
    for level in range(levels):
        owner_plane, owner_core, within = level // 4, level // 2 % 2, level % 2
        slot = jnp.where(plane == owner_plane, 0, 2) + within

        @pl.when(core == owner_core)
        def _():
            keep[slot, pick, lanes] = natural[level]

        @pl.when(core != owner_core)
        def _():
            send[slot, pick, lanes] = natural[level]


def dot(a, b):
    return jnp.dot(a, b, preferred_element_type=F32)


def prepare_kernel(p, g, own_values, own_products, to_fields, to_sides, back, fields, weights, to_weights):
    members, levels, rows, cols = p.shape
    fine = back.shape[0] // LANES
    fill_selectors(to_fields, to_weights, to_sides, back, members, cols)
    for i in range(rows // HALO):
        pick = slice(i * HALO, (i + 1) * HALO)
        out = slice(i * HALO * levels, (i + 1) * HALO * levels)
        for half in range(cols // LANES):
            lanes = slice(half * LANES, (half + 1) * LANES)
            for m in range(members):
                to = slice(m * cols + half * LANES, m * cols + (half + 1) * LANES)
                fields[out, to] = turned(p[m, :, pick, lanes]).astype(BF16)
            hi, lo = split(turned(g[:, pick, lanes]))
            weights[out, lanes] = hi
            weights[out, cols + half * LANES : cols + (half + 1) * LANES] = lo
    for first in range(0, fine, 2):
        width = min(2, fine - first)
        lanes = slice(first * LANES, (first + width) * LANES)
        field = dot(fields[...], to_fields[: members * cols, lanes])
        weight = dot(weights[...], to_weights[:, lanes])
        product = field * weight
        for k in range(width):
            pick = slice(k * LANES, (k + 1) * LANES)
            own_values[:, first + k] = field[:, pick].reshape(rows, levels, LANES)
            own_products[:, first + k] = product[:, pick].reshape(rows, levels, LANES)


def inner_kernel(
    place, values, own_products, taper, left, right, to_sides, back, kappa,
    keep, send, edges, edge_values,
    x, packs,
):
    levels, rows, cols = taper.shape
    fine = x.shape[1] - 4
    members = LANES * fine // (cols + 2 * HALO)
    for i in range(rows // HALO):
        out = slice(i * HALO * levels, (i + 1) * HALO * levels)
        for side, ref in enumerate((left, right)):
            lanes = slice(side * LANES, (side + 1) * LANES)
            packs[out, lanes] = turned(ref[:, i * HALO : (i + 1) * HALO, :]).astype(BF16)
    for first in range(0, fine, 2):
        width = min(2, fine - first)
        beside = dot(packs[...], to_sides[:, first * LANES : (first + width) * LANES])
        for k in range(width):
            pick = slice(k * LANES, (k + 1) * LANES)
            x[:, 2 + first + k] = own_products[:, first + k] + beside[:, pick].reshape(rows, levels, LANES)
    upper, lower = place[1], 1 - place[1]
    for k in range(HALO):
        edge_values[upper, k] = values[k]
        edge_values[lower, k] = values[rows - 1 - k]

    linear, constant, scale = factors(kappa[...], 4 * members)

    def wrap(row):
        def target(c, value):
            x[row, c + 2] = value

        wrap_columns(row_of(x, row), target, fine)

    def wrap_first(row, _):
        wrap(row)
        return 0

    lax.fori_loop(0, rows, wrap_first, 0, unroll=True)

    for turn in range(PASSES):
        low = 2 * turn
        start, count = low + 2, rows - 4 * turn - 4
        for k in range(4):
            edges[upper, turn, k] = x[low + k]
            edges[lower, turn, k] = x[rows - 1 - low - k]

        v, _ = first_sweep(row_of(x, start - 2), row_of(x, start - 1), None, linear, fine)
        v, u = first_sweep(row_of(x, start - 1), row_of(x, start), v, linear, fine)
        v, u_next = first_sweep(row_of(x, start), row_of(x, start + 1), v, linear, fine)
        q, _ = second_sweep(None, u, u_next, None, constant, fine)
        u = u_next
        for i in range(start, start + count):
            v, u_next = first_sweep(row_of(x, i + 1), row_of(x, i + 2), v, linear, fine)
            q, y = second_sweep(row_of(x, i), u, u_next, q, constant, fine)
            u = u_next
            for c in range(fine):
                x[i, c + 2] = y[c]
            if turn < PASSES - 1:
                wrap(i)

    def last(i, _):
        first = i * HALO
        from_row = first + HALO
        product = jnp.concatenate(
            [
                (x[pl.ds(from_row, HALO), c + 2] * values[pl.ds(from_row, HALO), c]).reshape(HALO * levels, LANES)
                for c in range(fine)
            ],
            axis=1,
        )
        pick = pl.ds(pl.multiple_of(first, HALO), HALO)
        finish(
            product, back[...], scale,
            lambda lanes: taper[:, pl.ds(pl.multiple_of(from_row, HALO), HALO), lanes],
            lambda natural, lanes: to_owner(place, natural, keep, send, pick, lanes, levels),
            levels,
        )
        return 0

    lax.fori_loop(0, (rows - 2 * HALO) // HALO, last, 0)


def outer_kernel(
    place, taper, near, far, left, right, edges, edge_values, to_fields, back, kappa,
    keep, send,
    x, fields,
):
    levels, rows, cols = taper.shape
    fine = edge_values.shape[2]
    members = LANES * fine // (cols + 2 * HALO)
    linear, constant, scale = factors(kappa[...], 4 * members)
    inside = jnp.where(place[0] == 1, 0.0, 1.0).astype(F32)
    count, main = near.shape
    fields[:count, :main] = near[...]
    fields[:count, main:] = left[...] + right[...]
    fields[count:, :] = far[...]
    for first in range(0, fine, 2):
        width = min(2, fine - first)
        field = dot(fields[...], to_fields[:, first * LANES : (first + width) * LANES])
        for k in range(width):
            part = field[:, k * LANES : (k + 1) * LANES].reshape(2, HALO + NEAR, levels, LANES)
            for edge in range(2):
                for distance in range(HALO):
                    value = part[edge, distance]
                    if distance < NEAR:
                        value = value + part[edge, HALO + distance]
                    if edge == 1 and distance == 0:
                        value = value * inside
                    x[edge, HALO - 1 - distance, 2 + first + k] = value

    def wrap(edge, row):
        def target(c, value):
            x[edge, row, c + 2] = value

        wrap_columns(row_of(x, edge, row), target, fine)

    for row in range(HALO):
        for edge in range(2):
            wrap(edge, row)

    for turn in range(PASSES):
        low = 2 * turn
        for edge in range(2):
            def row_at(row):
                if row < low + HALO:
                    return row_of(x, edge, row)
                return row_of(edges, edge, turn, row - low - HALO)

            v = u = q = None
            for i in range(low, low + HALO + 3):
                v, u_next = first_sweep(row_at(i), row_at(i + 1), v, linear, fine)
                if u_next is None:
                    continue
                if edge == 1 and i == HALO - 1:
                    u_next = {c: part * inside for c, part in u_next.items()}
                if u is not None:
                    q, y = second_sweep(row_at(i - 1), u, u_next, q, constant, fine)
                    if y is not None:
                        for c in range(fine):
                            x[edge, i - 1, c + 2] = y[c] * inside if edge == 1 and i == HALO else y[c]
                u = u_next
            if turn < PASSES - 1:
                for row in range(low + 2, low + HALO + 2):
                    wrap(edge, row)

    for edge in range(2):
        order = range(HALO) if edge == 0 else range(HALO - 1, -1, -1)
        slot = place[1] if edge == 0 else 1 - place[1]
        product = jnp.concatenate(
            [
                jnp.concatenate([x[slot, HALO + k, c + 2] * edge_values[slot, k, c] for k in order], axis=0)
                for c in range(fine)
            ],
            axis=1,
        )
        own = slice(edge * (rows - HALO), edge * (rows - HALO) + HALO)
        pick = slice(edge * HALO, (edge + 1) * HALO)
        finish(
            product, back[...], scale,
            lambda lanes: taper[:, own, lanes],
            lambda natural, lanes: to_owner(place, natural, keep, send, pick, lanes, levels),
            levels,
        )


def shifted(value, axis, step, wrap):
    count = lax.axis_size(axis)
    pairs = [(i, (i + step) % count) for i in range(count) if wrap or 0 <= i + step < count]
    return lax.ppermute(value, axis, pairs)


def over_core(keep, send):
    got = lax.ppermute(send, "mem", [(i, i ^ 1) for i in range(4)])
    return keep[:2] + got[:2], keep[2:] + got[2:]


def over_plane(here, there):
    return here + lax.ppermute(there, "mem", [(i, i ^ 2) for i in range(4)])


def local(perturbations, increment, taper_norm, kappa):
    members, levels, rows, cols = perturbations.shape
    fine = (cols + 2 * HALO) * members // LANES
    shape = jax.ShapeDtypeStruct
    tile = (levels, LANES)
    vmem = pl.BlockSpec(memory_space=pltpu.VMEM)
    smem = pl.BlockSpec(memory_space=pltpu.SMEM)
    hbm = pl.BlockSpec(memory_space=pltpu.HBM)

    def call(kernel, name, outs, ins, scratch=(), specs=None, cost=None):
        return pl.pallas_call(
            kernel,
            out_shape=tuple(outs),
            in_specs=specs or [vmem] * len(ins),
            out_specs=(vmem,) * len(outs),
            scratch_shapes=list(scratch),
            compiler_params=pltpu.CompilerParams(vmem_limit_bytes=20 * 1024 * 1024),
            cost_estimate=cost,
            name=name,
        )(*ins)

    def strip(blocks):
        return shape(((HALO + NEAR) * levels, members * cols + blocks * LANES), BF16)

    pack = shape((levels, rows, LANES), BF16)
    whole = shape((levels, rows, cols), F32)
    kappa = jnp.broadcast_to(kappa[:, None], tile)
    lat, mem = lax.axis_index("lat"), lax.axis_index("mem")
    count = lax.axis_size("lat")
    place = jnp.stack([
        ((lat == 0) | (lat == count - 1)).astype(jnp.int32),
        1 - lat % 2,
        mem % 2,
        mem // 2,
    ])

    to_near, to_left, to_right, p, g = call(
        start_kernel, "start",
        (strip(0), pack, pack, shape(perturbations.shape, BF16), whole),
        (place, *(pltpu.with_memory_space_constraint(a, pltpu.HBM) for a in (perturbations, increment, taper_norm))),
        (pltpu.VMEM(whole.shape, F32), pltpu.VMEM(whole.shape, F32), pltpu.SemaphoreType.DMA((rows // HALO, 3))),
        specs=[smem] + [hbm] * 3,
    )
    near = lax.ppermute(to_near, "lat", [(i, i ^ 1) for i in range(count)])
    left = shifted(to_right, "lon", 1, True)
    right = shifted(to_left, "lon", -1, True)

    values = shape((rows, fine, *tile), F32)
    own_values, own_products, to_fields, to_sides, back = call(
        prepare_kernel, "prepare",
        (
            values, values,
            shape((members * cols + LANES, fine * LANES), BF16),
            shape((2 * LANES, fine * LANES), BF16),
            shape((fine * LANES, cols), BF16),
        ),
        (p, g),
        (
            pltpu.VMEM((rows * levels, members * cols), BF16),
            pltpu.VMEM((rows * levels, 2 * cols), BF16),
            pltpu.VMEM((2 * cols, fine * LANES), BF16),
        ),
    )

    p, g, own_values = lax.optimization_barrier((p, g, own_values))
    (to_far,) = call(far_kernel, "far", (strip(1),), (place, p, g, left, right), specs=[smem] + [vmem] * 4)
    far = lax.ppermute(to_far, "lat", [(i, (i + 1 - 2 * (1 - i % 2)) % count) for i in range(count)])
    near, to_far = lax.optimization_barrier((near, to_far))
    side = shape(((HALO + NEAR) * levels, LANES), BF16)
    to_left, to_right = call(corners_kernel, "corners", (side, side), (near,))
    near_left = shifted(to_right, "lon", 1, True)
    near_right = shifted(to_left, "lon", -1, True)
    own_values, to_left = lax.optimization_barrier((own_values, to_left))

    part = shape((levels // 2, rows - 2 * HALO, cols), F32)
    keep, send, edges, edge_values = call(
        inner_kernel, "inner",
        (part, part, shape((2, PASSES, 4, fine + 4, *tile), F32), shape((2, HALO, fine, *tile), F32)),
        (place, own_values, own_products, taper_norm, left, right, to_sides, back, kappa),
        (
            pltpu.VMEM((rows, fine + 4, *tile), F32),
            pltpu.VMEM((rows * levels, 2 * LANES), BF16),
        ),
        specs=[smem] + [vmem] * 8,
        cost=pl.CostEstimate(flops=INNER_FLOPS, bytes_accessed=1 << 20, transcendentals=0),
    )
    middle = over_plane(*over_core(keep, send))
    part = shape((levels // 2, 2 * HALO, cols), F32)
    keep, send = call(
        outer_kernel, "outer",
        (part, part),
        (
            place, taper_norm, near, far, near_left, near_right, edges, edge_values,
            to_fields, back, kappa,
        ),
        (
            pltpu.VMEM((2, 2 * HALO, fine + 4, *tile), F32),
            pltpu.VMEM((2 * (HALO + NEAR) * levels, members * cols + LANES), BF16),
        ),
        specs=[smem] + [vmem] * 10,
        cost=pl.CostEstimate(flops=OUTER_FLOPS, bytes_accessed=1 << 20, transcendentals=0),
    )
    outside = over_plane(*over_core(keep, send))
    return jnp.concatenate([outside[:, :HALO], middle, outside[:, HALO:]], axis=1)


def solution(mesh):
    return jax.shard_map(
        local,
        mesh=mesh,
        in_specs=(P("mem", None, "lat", "lon"), P(None, "lat", "lon"), P(None, "lat", "lon"), P()),
        out_specs=P("mem", "lat", "lon"),
        check_vma=False,
    )
```

```python
import jax
import jax.numpy as jnp
from jax import lax
from jax.experimental import pallas as pl
from jax.experimental.pallas import tpu as pltpu
from jax.sharding import PartitionSpec as P

PASSES = 8
HALO = 2 * PASSES
LANES = 128
NEAR = 4
INNER_FLOPS = 4 * 10**9
OUTER_FLOPS = 4 * 10**9
BF16 = jnp.bfloat16
F32 = jnp.float32


def roll(x, shift):
    shift = shift % LANES
    return pltpu.roll(x, shift, x.ndim - 1) if shift else x


def lane_of(shape):
    return lax.broadcasted_iota(jnp.int32, shape, len(shape) - 1)


def split(value):
    hi = value.astype(BF16)
    return hi, (value - hi.astype(F32)).astype(BF16)


def target_column(shape, first, members, cols):
    chunks = LANES // members
    fine = (cols + 2 * HALO) // chunks
    lane = lax.broadcasted_iota(jnp.int32, shape, 1)
    return fine * (lane % chunks) + first - HALO, lane // chunks


def fill_selectors(to_fields, to_weights, to_sides, back, members, cols):
    fine = back.shape[0] // LANES
    nowhere = -4 * LANES

    def mark(hit):
        return jnp.where(hit, 1.0, 0.0).astype(BF16)

    for first in range(fine):
        lanes = slice(first * LANES, (first + 1) * LANES)
        shape = (cols, LANES)
        column, member = target_column(shape, first, members, cols)
        row = lax.broadcasted_iota(jnp.int32, shape, 0)
        here = row == column
        for m in range(members):
            to_fields[m * cols : (m + 1) * cols, lanes] = mark(here & (member == m))
        for part in range(2):
            to_weights[part * cols : (part + 1) * cols, lanes] = mark(here)
        for ref, base, count, offsets in (
            (to_fields, members * cols, LANES, (0,)), (to_sides, 0, 2 * LANES, (0, LANES // 2)),
        ):
            shape = (count, LANES)
            column, member = target_column(shape, first, members, cols)
            row = lax.broadcasted_iota(jnp.int32, shape, 0)
            after = column - cols + count // 2
            at = jnp.where(column < 0, column + HALO, jnp.where(column >= cols, after, nowhere)) + HALO * member
            hit = row == at
            for offset in offsets[1:]:
                hit = hit | (row == at + offset)
            ref[base : base + count, lanes] = mark(hit)
        shape = (LANES, cols)
        lane = lax.broadcasted_iota(jnp.int32, shape, 0)
        column = fine * (lane % (LANES // members)) + first - HALO
        back[lanes, :] = mark(lax.broadcasted_iota(jnp.int32, shape, 1) == column)


def facing(value):
    return jnp.swapaxes(value.astype(F32), 0, 1)


def write_strip(out, p, g, pick, order, sides=None):
    members, levels, _, cols = p.shape

    def put(pair, lanes, field, first=0):
        rows = slice((first + 2 * pair) * levels, (first + 2 * pair + 2) * levels)
        both = jnp.concatenate([field[order[2 * pair]], field[order[2 * pair + 1]]], axis=0)
        out[rows, lanes] = both.astype(BF16)

    for half in range(2):
        lanes = slice(half * LANES, (half + 1) * LANES)
        weight = g[:, pick, lanes]
        for m in range(members):
            to = slice(m * cols + half * LANES, m * cols + (half + 1) * LANES)
            product = facing(p[m, :, pick, lanes].astype(F32) * weight)
            rest = product - product.astype(BF16).astype(F32)
            for pair in range(HALO // 2):
                put(pair, to, product)
            for pair in range(NEAR // 2):
                put(pair, to, rest, HALO)
    if sides is not None:
        left, right = (facing(side[:, pick, :]) for side in sides)
        lane = lane_of(left.shape)
        half = LANES // 2
        to = slice(members * cols, members * cols + LANES)
        product = jnp.where(lane < half, left, roll(right, half))
        rest = jnp.where(lane < half, roll(left, half), right)
        for pair in range(HALO // 2):
            put(pair, to, product)
        for pair in range(NEAR // 2):
            put(pair, to, rest, HALO)


def start_kernel(place, p_hbm, increment_hbm, taper_hbm, to_near, to_left, to_right, p, g, taper, increment, sems):
    members, levels, rows, cols = p.shape
    copies = []
    for i in (0, rows // HALO - 1, *range(1, rows // HALO - 1)):
        pick = slice(i * HALO, (i + 1) * HALO)
        copies.append((pick, [
            pltpu.make_async_copy(p_hbm.at[:, :, pick, :], p.at[:, :, pick, :], sems.at[i, 0]),
            pltpu.make_async_copy(increment_hbm.at[:, pick, :], increment.at[:, pick, :], sems.at[i, 1]),
            pltpu.make_async_copy(taper_hbm.at[:, pick, :], taper.at[:, pick, :], sems.at[i, 2]),
        ]))
    for _, group in copies:
        for copy in group:
            copy.start()

    def packed(pick, column, shift):
        products = [p[m, :, pick, column].astype(F32) * g[:, pick, column] for m in range(members)]
        products += [product - product.astype(BF16).astype(F32) for product in products]
        lane = lane_of(products[0].shape)
        total = jnp.zeros_like(products[0])
        for e, product in enumerate(products):
            inside = (lane >= HALO * e) & (lane < HALO * (e + 1))
            total = jnp.where(inside, roll(product, shift + HALO * e), total)
        return total.astype(BF16)

    for k, (pick, group) in enumerate(copies):
        for copy in group:
            copy.wait()
        g[:, pick, :] = increment[:, pick, :] * taper[:, pick, :]
        if k < 2:
            order = range(HALO) if k == 0 else range(HALO - 1, -1, -1)

            @pl.when(place[1] == k)
            def _():
                write_strip(to_near, p, g, pick, order)
        to_left[:, pick, :] = packed(pick, slice(0, LANES), 0)
        to_right[:, pick, :] = packed(pick, slice(cols - LANES, cols), HALO)


def far_kernel(place, p, g, left, right, to_far):
    rows = p.shape[2]
    for k in range(2):
        pick = slice(k * (rows - HALO), k * (rows - HALO) + HALO)
        order = range(HALO) if k == 0 else range(HALO - 1, -1, -1)

        @pl.when(place[1] != k)
        def _():
            write_strip(to_far, p, g, pick, order, (left, right))


def corners_kernel(strip, to_left, to_right):
    count, main = strip.shape
    members = main // (2 * LANES)
    for first in range(0, count, 16):
        rows = slice(first, first + 16)
        lane = lane_of((16, LANES))
        for ref, half, base, shift in ((to_left, 0, LANES // 2, 0), (to_right, 1, 0, HALO)):
            total = jnp.zeros((16, LANES), F32)
            for m in range(members):
                field = strip[rows, (2 * m + half) * LANES : (2 * m + half + 1) * LANES].astype(F32)
                at = base + HALO * m
                total = jnp.where((lane >= at) & (lane < at + HALO), roll(field, shift + at), total)
            ref[rows, :] = total.astype(BF16)


def turned(value):
    levels, rows, lanes = value.shape
    return jnp.swapaxes(value.astype(F32), 0, 1).reshape(rows * levels, lanes)


def factors(kappa, count):
    denominator = 1.0 + 4.0 * kappa
    scale = kappa / denominator
    for _ in range(4):
        scale = scale * scale
    return 1.0 / kappa, denominator / (kappa * kappa), scale / (count - 1)


def row_of(ref, *where):
    return lambda c: ref[(*where, c + 2)]


def first_sweep(x, x_next, v, linear, fine):
    v_next = {c: x(c) + x_next(c + 1) for c in range(-2, fine + 1)}
    if v is None:
        return v_next, None
    u = {c: linear * x(c) + v[c] + v_next[c - 1] for c in range(-1, fine + 1)}
    return v_next, u


def second_sweep(x, u, u_next, q, constant, fine):
    q_next = {c: u[c] + u_next[c + 1] for c in range(-1, fine)}
    if q is None:
        return q_next, None
    return q_next, [constant * x(c) + q[c] + q_next[c - 1] for c in range(fine)]


def wrap_columns(source, target, fine):
    for c in (0, 1):
        target(fine + c, roll(source(c), -1))
        target(c - 2, roll(source(fine - 2 + c), 1))


def finish(sums, back, scale, taper_of, write, levels):
    hi, lo = split(sums)
    total = jnp.dot(hi, back, preferred_element_type=F32) + jnp.dot(lo, back, preferred_element_type=F32)
    count = total.shape[0] // levels
    for half in range(total.shape[1] // LANES):
        lanes = slice(half * LANES, (half + 1) * LANES)
        part = total[:, lanes].reshape(count, levels, LANES) * scale
        natural = jnp.swapaxes(part, 0, 1) * taper_of(lanes)
        write(natural, lanes)


def to_owner(place, natural, ordered, pick, lanes, levels):
    core, plane = place[2], place[3]
    for level in range(levels):
        other_core = jnp.where(core == level // 2 % 2, 0, 1)
        other_plane = jnp.where(plane == level // 4, 0, 1)
        ordered[levels // 2 * other_core + 2 * other_plane + level % 2, pick, lanes] = natural[level]


def dot(a, b):
    return jnp.dot(a, b, preferred_element_type=F32)


def prepare_kernel(p, g, own_values, own_products, to_fields, to_sides, back, fields, weights, to_weights):
    members, levels, rows, cols = p.shape
    fine = back.shape[0] // LANES
    fill_selectors(to_fields, to_weights, to_sides, back, members, cols)
    for i in range(rows // HALO):
        pick = slice(i * HALO, (i + 1) * HALO)
        out = slice(i * HALO * levels, (i + 1) * HALO * levels)
        for half in range(cols // LANES):
            lanes = slice(half * LANES, (half + 1) * LANES)
            for m in range(members):
                to = slice(m * cols + half * LANES, m * cols + (half + 1) * LANES)
                fields[out, to] = turned(p[m, :, pick, lanes]).astype(BF16)
            hi, lo = split(turned(g[:, pick, lanes]))
            weights[out, lanes] = hi
            weights[out, cols + half * LANES : cols + (half + 1) * LANES] = lo
    for first in range(0, fine, 2):
        width = min(2, fine - first)
        lanes = slice(first * LANES, (first + width) * LANES)
        field = dot(fields[...], to_fields[: members * cols, lanes])
        weight = dot(weights[...], to_weights[:, lanes])
        product = field * weight
        for k in range(width):
            pick = slice(k * LANES, (k + 1) * LANES)
            own_values[:, first + k] = field[:, pick].reshape(rows, levels, LANES)
            own_products[:, first + k] = product[:, pick].reshape(rows, levels, LANES)


def inner_kernel(
    place, values, own_products, taper, left, right, to_sides, back, kappa,
    keep, send, edges, edge_values,
    x, packs, ordered,
):
    levels, rows, cols = taper.shape
    fine = x.shape[1] - 4
    members = LANES * fine // (cols + 2 * HALO)
    for i in range(rows // HALO):
        out = slice(i * HALO * levels, (i + 1) * HALO * levels)
        for side, ref in enumerate((left, right)):
            lanes = slice(side * LANES, (side + 1) * LANES)
            packs[out, lanes] = turned(ref[:, i * HALO : (i + 1) * HALO, :]).astype(BF16)
    for first in range(0, fine, 2):
        width = min(2, fine - first)
        beside = dot(packs[...], to_sides[:, first * LANES : (first + width) * LANES])
        for k in range(width):
            pick = slice(k * LANES, (k + 1) * LANES)
            x[:, 2 + first + k] = own_products[:, first + k] + beside[:, pick].reshape(rows, levels, LANES)
    upper, lower = place[1], 1 - place[1]
    for k in range(HALO):
        edge_values[upper, k] = values[k]
        edge_values[lower, k] = values[rows - 1 - k]

    linear, constant, scale = factors(kappa[...], 4 * members)

    def wrap(row):
        def target(c, value):
            x[row, c + 2] = value

        wrap_columns(row_of(x, row), target, fine)

    def wrap_first(row, _):
        wrap(row)
        return 0

    lax.fori_loop(0, rows, wrap_first, 0, unroll=True)

    for turn in range(PASSES):
        low = 2 * turn
        start, count = low + 2, rows - 4 * turn - 4
        for k in range(4):
            edges[upper, turn, k] = x[low + k]
            edges[lower, turn, k] = x[rows - 1 - low - k]

        v, _ = first_sweep(row_of(x, start - 2), row_of(x, start - 1), None, linear, fine)
        v, u = first_sweep(row_of(x, start - 1), row_of(x, start), v, linear, fine)
        v, u_next = first_sweep(row_of(x, start), row_of(x, start + 1), v, linear, fine)
        q, _ = second_sweep(None, u, u_next, None, constant, fine)
        u = u_next
        for i in range(start, start + count):
            v, u_next = first_sweep(row_of(x, i + 1), row_of(x, i + 2), v, linear, fine)
            q, y = second_sweep(row_of(x, i), u, u_next, q, constant, fine)
            u = u_next
            for c in range(fine):
                x[i, c + 2] = y[c]
            if turn < PASSES - 1:
                wrap(i)

    def last(i):
        first = i * HALO
        from_row = first + HALO
        product = jnp.concatenate(
            [
                (x[slice(from_row, from_row + HALO), c + 2] * values[slice(from_row, from_row + HALO), c]).reshape(HALO * levels, LANES)
                for c in range(fine)
            ],
            axis=1,
        )
        pick = slice(first, first + HALO)
        finish(
            product, back[...], scale,
            lambda lanes: taper[:, slice(from_row, from_row + HALO), lanes],
            lambda natural, lanes: to_owner(place, natural, ordered, pick, lanes, levels),
            levels,
        )

    for i in range((rows - 2 * HALO) // HALO):
        last(i)
    keep[...] = ordered[: levels // 2]
    send[...] = ordered[levels // 2 :]


def outer_kernel(
    place, taper, near, far, left, right, edges, edge_values, to_fields, back, kappa,
    keep, send,
    x, fields, ordered,
):
    levels, rows, cols = taper.shape
    fine = edge_values.shape[2]
    members = LANES * fine // (cols + 2 * HALO)
    linear, constant, scale = factors(kappa[...], 4 * members)
    inside = jnp.where(place[0] == 1, 0.0, 1.0).astype(F32)
    count, main = near.shape
    fields[:count, :main] = near[...]
    fields[:count, main:] = left[...] + right[...]
    fields[count:, :] = far[...]
    for first in range(0, fine, 2):
        width = min(2, fine - first)
        field = dot(fields[...], to_fields[:, first * LANES : (first + width) * LANES])
        for k in range(width):
            part = field[:, k * LANES : (k + 1) * LANES].reshape(2, HALO + NEAR, levels, LANES)
            for edge in range(2):
                for distance in range(HALO):
                    value = part[edge, distance]
                    if distance < NEAR:
                        value = value + part[edge, HALO + distance]
                    if edge == 1 and distance == 0:
                        value = value * inside
                    x[edge, HALO - 1 - distance, 2 + first + k] = value

    def wrap(edge, row):
        def target(c, value):
            x[edge, row, c + 2] = value

        wrap_columns(row_of(x, edge, row), target, fine)

    for row in range(HALO):
        for edge in range(2):
            wrap(edge, row)

    for turn in range(PASSES):
        low = 2 * turn
        for edge in range(2):
            def row_at(row):
                if row < low + HALO:
                    return row_of(x, edge, row)
                return row_of(edges, edge, turn, row - low - HALO)

            v = u = q = None
            for i in range(low, low + HALO + 3):
                v, u_next = first_sweep(row_at(i), row_at(i + 1), v, linear, fine)
                if u_next is None:
                    continue
                if edge == 1 and i == HALO - 1:
                    u_next = {c: part * inside for c, part in u_next.items()}
                if u is not None:
                    q, y = second_sweep(row_at(i - 1), u, u_next, q, constant, fine)
                    if y is not None:
                        for c in range(fine):
                            x[edge, i - 1, c + 2] = y[c] * inside if edge == 1 and i == HALO else y[c]
                u = u_next
            if turn < PASSES - 1:
                for row in range(low + 2, low + HALO + 2):
                    wrap(edge, row)

    for edge in range(2):
        order = range(HALO) if edge == 0 else range(HALO - 1, -1, -1)
        slot = place[1] if edge == 0 else 1 - place[1]
        product = jnp.concatenate(
            [
                jnp.concatenate([x[slot, HALO + k, c + 2] * edge_values[slot, k, c] for k in order], axis=0)
                for c in range(fine)
            ],
            axis=1,
        )
        own = slice(edge * (rows - HALO), edge * (rows - HALO) + HALO)
        pick = slice(edge * HALO, (edge + 1) * HALO)
        finish(
            product, back[...], scale,
            lambda lanes: taper[:, own, lanes],
            lambda natural, lanes: to_owner(place, natural, ordered, pick, lanes, levels),
            levels,
        )
    keep[...] = ordered[: levels // 2]
    send[...] = ordered[levels // 2 :]


def shifted(value, axis, step, wrap):
    count = lax.axis_size(axis)
    pairs = [(i, (i + step) % count) for i in range(count) if wrap or 0 <= i + step < count]
    return lax.ppermute(value, axis, pairs)


def over_core(keep, send):
    got = lax.ppermute(send, "mem", [(i, i ^ 1) for i in range(4)])
    return keep[:2] + got[:2], keep[2:] + got[2:]


def over_plane(here, there):
    return here + lax.ppermute(there, "mem", [(i, i ^ 2) for i in range(4)])


def local(perturbations, increment, taper_norm, kappa):
    members, levels, rows, cols = perturbations.shape
    fine = (cols + 2 * HALO) * members // LANES
    shape = jax.ShapeDtypeStruct
    tile = (levels, LANES)
    vmem = pl.BlockSpec(memory_space=pltpu.VMEM)
    smem = pl.BlockSpec(memory_space=pltpu.SMEM)
    hbm = pl.BlockSpec(memory_space=pltpu.HBM)

    def call(kernel, name, outs, ins, scratch=(), specs=None, cost=None):
        return pl.pallas_call(
            kernel,
            out_shape=tuple(outs),
            in_specs=specs or [vmem] * len(ins),
            out_specs=(vmem,) * len(outs),
            scratch_shapes=list(scratch),
            compiler_params=pltpu.CompilerParams(vmem_limit_bytes=20 * 1024 * 1024),
            cost_estimate=cost,
            name=name,
        )(*ins)

    def strip(blocks):
        return shape(((HALO + NEAR) * levels, members * cols + blocks * LANES), BF16)

    pack = shape((levels, rows, LANES), BF16)
    whole = shape((levels, rows, cols), F32)
    kappa = jnp.broadcast_to(kappa[:, None], tile)
    lat, mem = lax.axis_index("lat"), lax.axis_index("mem")
    count = lax.axis_size("lat")
    place = jnp.stack([
        ((lat == 0) | (lat == count - 1)).astype(jnp.int32),
        1 - lat % 2,
        mem % 2,
        mem // 2,
    ])

    to_near, to_left, to_right, p, g = call(
        start_kernel, "start",
        (strip(0), pack, pack, shape(perturbations.shape, BF16), whole),
        (place, *(pltpu.with_memory_space_constraint(a, pltpu.HBM) for a in (perturbations, increment, taper_norm))),
        (pltpu.VMEM(whole.shape, F32), pltpu.VMEM(whole.shape, F32), pltpu.SemaphoreType.DMA((rows // HALO, 3))),
        specs=[smem] + [hbm] * 3,
    )
    near = lax.ppermute(to_near, "lat", [(i, i ^ 1) for i in range(count)])
    left = shifted(to_right, "lon", 1, True)
    right = shifted(to_left, "lon", -1, True)

    values = shape((rows, fine, *tile), F32)
    own_values, own_products, to_fields, to_sides, back = call(
        prepare_kernel, "prepare",
        (
            values, values,
            shape((members * cols + LANES, fine * LANES), BF16),
            shape((2 * LANES, fine * LANES), BF16),
            shape((fine * LANES, cols), BF16),
        ),
        (p, g),
        (
            pltpu.VMEM((rows * levels, members * cols), BF16),
            pltpu.VMEM((rows * levels, 2 * cols), BF16),
            pltpu.VMEM((2 * cols, fine * LANES), BF16),
        ),
    )

    p, g, own_values = lax.optimization_barrier((p, g, own_values))
    (to_far,) = call(far_kernel, "far", (strip(1),), (place, p, g, left, right), specs=[smem] + [vmem] * 4)
    far = lax.ppermute(to_far, "lat", [(i, (i + 1 - 2 * (1 - i % 2)) % count) for i in range(count)])
    near, to_far = lax.optimization_barrier((near, to_far))
    side = shape(((HALO + NEAR) * levels, LANES), BF16)
    to_left, to_right = call(corners_kernel, "corners", (side, side), (near,))
    near_left = shifted(to_right, "lon", 1, True)
    near_right = shifted(to_left, "lon", -1, True)
    own_values, to_left = lax.optimization_barrier((own_values, to_left))

    part = shape((levels // 2, rows - 2 * HALO, cols), F32)
    keep, send, edges, edge_values = call(
        inner_kernel, "inner",
        (part, part, shape((2, PASSES, 4, fine + 4, *tile), F32), shape((2, HALO, fine, *tile), F32)),
        (place, own_values, own_products, taper_norm, left, right, to_sides, back, kappa),
        (
            pltpu.VMEM((rows, fine + 4, *tile), F32),
            pltpu.VMEM((rows * levels, 2 * LANES), BF16),
            pltpu.VMEM((levels, rows - 2 * HALO, cols), F32),
        ),
        specs=[smem] + [vmem] * 8,
        cost=pl.CostEstimate(flops=INNER_FLOPS, bytes_accessed=1 << 20, transcendentals=0),
    )
    middle = over_plane(*over_core(keep, send))
    part = shape((levels // 2, 2 * HALO, cols), F32)
    keep, send = call(
        outer_kernel, "outer",
        (part, part),
        (
            place, taper_norm, near, far, near_left, near_right, edges, edge_values,
            to_fields, back, kappa,
        ),
        (
            pltpu.VMEM((2, 2 * HALO, fine + 4, *tile), F32),
            pltpu.VMEM((2 * (HALO + NEAR) * levels, members * cols + LANES), BF16),
            pltpu.VMEM((levels, 2 * HALO, cols), F32),
        ),
        specs=[smem] + [vmem] * 10,
        cost=pl.CostEstimate(flops=OUTER_FLOPS, bytes_accessed=1 << 20, transcendentals=0),
    )
    outside = over_plane(*over_core(keep, send))
    return jnp.concatenate([outside[:, :HALO], middle, outside[:, HALO:]], axis=1)


def solution(mesh):
    return jax.shard_map(
        local,
        mesh=mesh,
        in_specs=(P("mem", None, "lat", "lon"), P(None, "lat", "lon"), P(None, "lat", "lon"), P()),
        out_specs=P("mem", "lat", "lon"),
        check_vma=False,
    )
```

```python
import jax
import jax.numpy as jnp
from jax import lax
from jax.experimental import pallas as pl
from jax.experimental.pallas import tpu as pltpu
from jax.sharding import PartitionSpec as P

PASSES = 8
HALO = 2 * PASSES
LANES = 128
NEAR = 4
INNER_FLOPS = 4 * 10**9
OUTER_FLOPS = 4 * 10**9
BF16 = jnp.bfloat16
F32 = jnp.float32


def roll(x, shift):
    shift = shift % LANES
    return pltpu.roll(x, shift, x.ndim - 1) if shift else x


def lane_of(shape):
    return lax.broadcasted_iota(jnp.int32, shape, len(shape) - 1)


def split(value):
    hi = value.astype(BF16)
    return hi, (value - hi.astype(F32)).astype(BF16)


def target_column(lane, first, members, cols):
    chunks = LANES // members
    fine = (cols + 2 * HALO) // chunks
    return fine * (lane & (chunks - 1)) + first - HALO, lane >> (chunks.bit_length() - 1)


def fill_selectors(wanted, to_fields, to_weights, to_sides, back, members, cols):
    fine = back.shape[0] // LANES
    nowhere = -4 * LANES

    def mark(hit):
        return jnp.where(hit, 1.0, 0.0).astype(BF16)

    for first in wanted:
        lanes = slice(first * LANES, (first + 1) * LANES)
        column, member = target_column(lax.broadcasted_iota(jnp.int32, (1, LANES), 1), first, members, cols)
        marked = mark(lax.broadcasted_iota(jnp.int32, (cols, LANES), 0) == column)
        for m in range(members):
            to_fields[m * cols : (m + 1) * cols, lanes] = marked * mark(member == m)
        for part in range(2):
            to_weights[part * cols : (part + 1) * cols, lanes] = marked
        for ref, base, count, offsets in (
            (to_fields, members * cols, LANES, (0,)), (to_sides, 0, 2 * LANES, (0, LANES // 2)),
        ):
            row = lax.broadcasted_iota(jnp.int32, (count, LANES), 0)
            after = column - cols + count // 2
            at = jnp.where(column < 0, column + HALO, jnp.where(column >= cols, after, nowhere)) + HALO * member
            hit = row == at
            for offset in offsets[1:]:
                hit = hit | (row == at + offset)
            ref[base : base + count, lanes] = mark(hit)
        shape = (LANES, cols)
        column, _ = target_column(lax.broadcasted_iota(jnp.int32, shape, 0), first, members, cols)
        back[lanes, :] = mark(lax.broadcasted_iota(jnp.int32, shape, 1) == column)


def facing(value):
    return jnp.swapaxes(value.astype(F32), 0, 1)


def write_strip(out, p, g, pick, order):
    members, levels, _, cols = p.shape

    def put(pair, lanes, field, first=0):
        rows = slice((first + 2 * pair) * levels, (first + 2 * pair + 2) * levels)
        both = jnp.concatenate([field[order[2 * pair]], field[order[2 * pair + 1]]], axis=0)
        out[rows, lanes] = both.astype(BF16)

    for half in range(2):
        lanes = slice(half * LANES, (half + 1) * LANES)
        weight = g[:, pick, lanes]
        for m in range(members):
            to = slice(m * cols + half * LANES, m * cols + (half + 1) * LANES)
            product = facing(p[m, :, pick, lanes].astype(F32) * weight)
            rest = product - product.astype(BF16).astype(F32)
            for pair in range(HALO // 2):
                put(pair, to, product)
            for pair in range(NEAR // 2):
                put(pair, to, rest, HALO)


def write_sides(out, lanes, left, right, pick, order):
    levels = left.shape[0]
    left, right = facing(left[:, pick, :]), facing(right[:, pick, :])
    lane = lane_of(left.shape)
    half = LANES // 2
    product = jnp.where(lane < half, left, roll(right, half))
    rest = jnp.where(lane < half, roll(left, half), right)
    for count, first, field in ((HALO, 0, product), (NEAR, HALO, rest)):
        for pair in range(count // 2):
            rows = slice((first + 2 * pair) * levels, (first + 2 * pair + 2) * levels)
            both = jnp.concatenate([field[order[2 * pair]], field[order[2 * pair + 1]]], axis=0)
            out[rows, lanes] = both.astype(BF16)


def start_kernel(place, p_hbm, increment_hbm, taper_hbm, to_near, to_left, to_right, p, g, taper, increment, sems):
    members, levels, rows, cols = p.shape
    copies = []
    for i in (0, rows // HALO - 1, *range(1, rows // HALO - 1)):
        pick = slice(i * HALO, (i + 1) * HALO)
        copies.append((pick, [
            pltpu.make_async_copy(p_hbm.at[:, :, pick, :], p.at[:, :, pick, :], sems.at[i, 0]),
            pltpu.make_async_copy(increment_hbm.at[:, pick, :], increment.at[:, pick, :], sems.at[i, 1]),
            pltpu.make_async_copy(taper_hbm.at[:, pick, :], taper.at[:, pick, :], sems.at[i, 2]),
        ]))
    for _, group in copies:
        for copy in group:
            copy.start()

    def packed(pick, column, shift):
        products = [p[m, :, pick, column].astype(F32) * g[:, pick, column] for m in range(members)]
        products += [product - product.astype(BF16).astype(F32) for product in products]
        lane = lane_of(products[0].shape)
        total = jnp.zeros_like(products[0])
        for e, product in enumerate(products):
            inside = (lane >= HALO * e) & (lane < HALO * (e + 1))
            total = jnp.where(inside, roll(product, shift + HALO * e), total)
        return total.astype(BF16)

    for k, (pick, group) in enumerate(copies):
        for copy in group:
            copy.wait()
        g[:, pick, :] = increment[:, pick, :] * taper[:, pick, :]
        if k < 2:
            order = range(HALO) if k == 0 else range(HALO - 1, -1, -1)

            @pl.when(place[1] == k)
            def _():
                write_strip(to_near, p, g, pick, order)
        to_left[:, pick, :] = packed(pick, slice(0, LANES), 0)
        to_right[:, pick, :] = packed(pick, slice(cols - LANES, cols), HALO)


def far_kernel(place, p, g, left, right, to_far, to_near_sides):
    members, _, rows, cols = p.shape
    for k in range(2):
        pick = slice(k * (rows - HALO), k * (rows - HALO) + HALO)
        order = range(HALO) if k == 0 else range(HALO - 1, -1, -1)

        @pl.when(place[1] != k)
        def _():
            write_strip(to_far, p, g, pick, order)
            write_sides(to_far, slice(members * cols, members * cols + LANES), left, right, pick, order)

        @pl.when(place[1] == k)
        def _():
            write_sides(to_near_sides, slice(0, LANES), left, right, pick, order)


def turned(value):
    levels, rows, lanes = value.shape
    return jnp.swapaxes(value.astype(F32), 0, 1).reshape(rows * levels, lanes)


def factors(kappa, count):
    denominator = 1.0 + 4.0 * kappa
    scale = kappa / denominator
    for _ in range(4):
        scale = scale * scale
    return 1.0 / kappa, denominator / (kappa * kappa), scale / (count - 1)


def row_of(ref, *where):
    return lambda c: ref[(*where, c + 2)]


def first_sweep(x, x_next, v, linear, fine):
    v_next = {c: x(c) + x_next(c + 1) for c in range(-2, fine + 1)}
    if v is None:
        return v_next, None
    u = {c: linear * x(c) + v[c] + v_next[c - 1] for c in range(-1, fine + 1)}
    return v_next, u


def second_sweep(x, u, u_next, q, constant, fine):
    q_next = {c: u[c] + u_next[c + 1] for c in range(-1, fine)}
    if q is None:
        return q_next, None
    return q_next, [constant * x(c) + q[c] + q_next[c - 1] for c in range(fine)]


def wrap_columns(source, target, fine):
    for c in (0, 1):
        target(fine + c, roll(source(c), -1))
        target(c - 2, roll(source(fine - 2 + c), 1))


def finish(sums, back, scale, taper_of, write, levels):
    hi, lo = split(sums)
    total = jnp.dot(hi, back, preferred_element_type=F32) + jnp.dot(lo, back, preferred_element_type=F32)
    count = total.shape[0] // levels
    for half in range(total.shape[1] // LANES):
        lanes = slice(half * LANES, (half + 1) * LANES)
        part = total[:, lanes].reshape(count, levels, LANES) * scale
        natural = jnp.swapaxes(part, 0, 1) * taper_of(lanes)
        write(natural, lanes)


def to_owner(place, natural, ordered, pick, lanes, levels):
    core, plane = place[2], place[3]
    for level in range(levels):
        other_core = jnp.where(core == level // 2 % 2, 0, 1)
        other_plane = jnp.where(plane == level // 4, 0, 1)
        ordered[levels // 2 * other_core + 2 * other_plane + level % 2, pick, lanes] = natural[level]


def dot(a, b):
    return jnp.dot(a, b, preferred_element_type=F32)


def prepare_kernel(p, g, own_values, own_products, to_fields, to_sides, back, fields, weights, to_weights):
    members, levels, rows, cols = p.shape
    fine = back.shape[0] // LANES

    def fill(first):
        wanted = range(first, min(first + 2, fine))
        fill_selectors(wanted, to_fields, to_weights, to_sides, back, members, cols)

    fill(0)
    for i in range(rows // HALO):
        pick = slice(i * HALO, (i + 1) * HALO)
        out = slice(i * HALO * levels, (i + 1) * HALO * levels)
        for half in range(cols // LANES):
            lanes = slice(half * LANES, (half + 1) * LANES)
            for m in range(members):
                to = slice(m * cols + half * LANES, m * cols + (half + 1) * LANES)
                fields[out, to] = turned(p[m, :, pick, lanes]).astype(BF16)
            hi, lo = split(turned(g[:, pick, lanes]))
            weights[out, lanes] = hi
            weights[out, cols + half * LANES : cols + (half + 1) * LANES] = lo
    for first in range(0, fine, 2):
        width = min(2, fine - first)
        lanes = slice(first * LANES, (first + width) * LANES)
        fill(first + 2)
        field = dot(fields[...], to_fields[: members * cols, lanes])
        weight = dot(weights[...], to_weights[:, lanes])
        product = field * weight
        for k in range(width):
            pick = slice(k * LANES, (k + 1) * LANES)
            own_values[:, first + k] = field[:, pick].reshape(rows, levels, LANES)
            own_products[:, first + k] = product[:, pick].reshape(rows, levels, LANES)


def inner_kernel(
    place, values, own_products, taper, left, right, to_sides, back, kappa,
    keep, send, edges, edge_values,
    x, packs, ordered,
):
    levels, rows, cols = taper.shape
    fine = x.shape[1] - 4
    members = LANES * fine // (cols + 2 * HALO)
    for i in range(rows // HALO):
        out = slice(i * HALO * levels, (i + 1) * HALO * levels)
        for side, ref in enumerate((left, right)):
            lanes = slice(side * LANES, (side + 1) * LANES)
            packs[out, lanes] = turned(ref[:, i * HALO : (i + 1) * HALO, :]).astype(BF16)
    for first in range(0, fine, 2):
        width = min(2, fine - first)
        beside = dot(packs[...], to_sides[:, first * LANES : (first + width) * LANES])
        for k in range(width):
            pick = slice(k * LANES, (k + 1) * LANES)
            x[:, 2 + first + k] = own_products[:, first + k] + beside[:, pick].reshape(rows, levels, LANES)
    upper, lower = place[1], 1 - place[1]
    for k in range(HALO):
        edge_values[upper, k] = values[k]
        edge_values[lower, k] = values[rows - 1 - k]

    linear, constant, scale = factors(kappa[...], 4 * members)

    def wrap(row):
        def target(c, value):
            x[row, c + 2] = value

        wrap_columns(row_of(x, row), target, fine)

    def wrap_first(row, _):
        wrap(row)
        return 0

    lax.fori_loop(0, rows, wrap_first, 0, unroll=True)

    for turn in range(PASSES):
        low = 2 * turn
        start, count = low + 2, rows - 4 * turn - 4
        for k in range(4):
            edges[upper, turn, k] = x[low + k]
            edges[lower, turn, k] = x[rows - 1 - low - k]

        v, _ = first_sweep(row_of(x, start - 2), row_of(x, start - 1), None, linear, fine)
        v, u = first_sweep(row_of(x, start - 1), row_of(x, start), v, linear, fine)
        v, u_next = first_sweep(row_of(x, start), row_of(x, start + 1), v, linear, fine)
        q, _ = second_sweep(None, u, u_next, None, constant, fine)
        u = u_next
        for i in range(start, start + count):
            v, u_next = first_sweep(row_of(x, i + 1), row_of(x, i + 2), v, linear, fine)
            q, y = second_sweep(row_of(x, i), u, u_next, q, constant, fine)
            u = u_next
            for c in range(fine):
                x[i, c + 2] = y[c]
            if turn < PASSES - 1:
                wrap(i)

    def last(i):
        first = i * HALO
        from_row = first + HALO
        product = jnp.concatenate(
            [
                (x[slice(from_row, from_row + HALO), c + 2] * values[slice(from_row, from_row + HALO), c]).reshape(HALO * levels, LANES)
                for c in range(fine)
            ],
            axis=1,
        )
        pick = slice(first, first + HALO)
        finish(
            product, back[...], scale,
            lambda lanes: taper[:, slice(from_row, from_row + HALO), lanes],
            lambda natural, lanes: to_owner(place, natural, ordered, pick, lanes, levels),
            levels,
        )

    for i in range((rows - 2 * HALO) // HALO):
        last(i)
    keep[...] = ordered[: levels // 2]
    send[...] = ordered[levels // 2 :]


def outer_kernel(
    place, taper, near, far, near_sides, edges, edge_values, to_fields, back, kappa,
    keep, send,
    x, fields, ordered,
):
    levels, rows, cols = taper.shape
    fine = edge_values.shape[2]
    members = LANES * fine // (cols + 2 * HALO)
    linear, constant, scale = factors(kappa[...], 4 * members)
    inside = jnp.where(place[0] == 1, 0.0, 1.0).astype(F32)
    count, main = near.shape
    fields[:count, :main] = near[...]
    fields[:count, main:] = near_sides[...]
    fields[count:, :] = far[...]
    for first in range(0, fine, 2):
        width = min(2, fine - first)
        field = dot(fields[...], to_fields[:, first * LANES : (first + width) * LANES])
        for k in range(width):
            part = field[:, k * LANES : (k + 1) * LANES].reshape(2, HALO + NEAR, levels, LANES)
            for edge in range(2):
                for distance in range(HALO):
                    value = part[edge, distance]
                    if distance < NEAR:
                        value = value + part[edge, HALO + distance]
                    if edge == 1 and distance == 0:
                        value = value * inside
                    x[edge, HALO - 1 - distance, 2 + first + k] = value

    def wrap(edge, row):
        def target(c, value):
            x[edge, row, c + 2] = value

        wrap_columns(row_of(x, edge, row), target, fine)

    for row in range(HALO):
        for edge in range(2):
            wrap(edge, row)

    for turn in range(PASSES):
        low = 2 * turn
        for edge in range(2):
            def row_at(row):
                if row < low + HALO:
                    return row_of(x, edge, row)
                return row_of(edges, edge, turn, row - low - HALO)

            v = u = q = None
            for i in range(low, low + HALO + 3):
                v, u_next = first_sweep(row_at(i), row_at(i + 1), v, linear, fine)
                if u_next is None:
                    continue
                if edge == 1 and i == HALO - 1:
                    u_next = {c: part * inside for c, part in u_next.items()}
                if u is not None:
                    q, y = second_sweep(row_at(i - 1), u, u_next, q, constant, fine)
                    if y is not None:
                        for c in range(fine):
                            x[edge, i - 1, c + 2] = y[c] * inside if edge == 1 and i == HALO else y[c]
                u = u_next
            if turn < PASSES - 1:
                for row in range(low + 2, low + HALO + 2):
                    wrap(edge, row)

    for edge in range(2):
        order = range(HALO) if edge == 0 else range(HALO - 1, -1, -1)
        slot = place[1] if edge == 0 else 1 - place[1]
        product = jnp.concatenate(
            [
                jnp.concatenate([x[slot, HALO + k, c + 2] * edge_values[slot, k, c] for k in order], axis=0)
                for c in range(fine)
            ],
            axis=1,
        )
        own = slice(edge * (rows - HALO), edge * (rows - HALO) + HALO)
        pick = slice(edge * HALO, (edge + 1) * HALO)
        finish(
            product, back[...], scale,
            lambda lanes: taper[:, own, lanes],
            lambda natural, lanes: to_owner(place, natural, ordered, pick, lanes, levels),
            levels,
        )
    keep[...] = ordered[: levels // 2]
    send[...] = ordered[levels // 2 :]


def shifted(value, axis, step, wrap):
    count = lax.axis_size(axis)
    pairs = [(i, (i + step) % count) for i in range(count) if wrap or 0 <= i + step < count]
    return lax.ppermute(value, axis, pairs)


def over_core(keep, send):
    got = lax.ppermute(send, "mem", [(i, i ^ 1) for i in range(4)])
    return keep[:2] + got[:2], keep[2:] + got[2:]


def over_plane(here, there):
    return here + lax.ppermute(there, "mem", [(i, i ^ 2) for i in range(4)])


def local(perturbations, increment, taper_norm, kappa):
    members, levels, rows, cols = perturbations.shape
    fine = (cols + 2 * HALO) * members // LANES
    shape = jax.ShapeDtypeStruct
    tile = (levels, LANES)
    vmem = pl.BlockSpec(memory_space=pltpu.VMEM)
    smem = pl.BlockSpec(memory_space=pltpu.SMEM)
    hbm = pl.BlockSpec(memory_space=pltpu.HBM)

    def call(kernel, name, outs, ins, scratch=(), specs=None, cost=None):
        return pl.pallas_call(
            kernel,
            out_shape=tuple(outs),
            in_specs=specs or [vmem] * len(ins),
            out_specs=(vmem,) * len(outs),
            scratch_shapes=list(scratch),
            compiler_params=pltpu.CompilerParams(vmem_limit_bytes=20 * 1024 * 1024),
            cost_estimate=cost,
            name=name,
        )(*ins)

    def strip(blocks):
        return shape(((HALO + NEAR) * levels, members * cols + blocks * LANES), BF16)

    pack = shape((levels, rows, LANES), BF16)
    whole = shape((levels, rows, cols), F32)
    kappa = jnp.broadcast_to(kappa[:, None], tile)
    lat, mem = lax.axis_index("lat"), lax.axis_index("mem")
    count = lax.axis_size("lat")
    place = jnp.stack([
        ((lat == 0) | (lat == count - 1)).astype(jnp.int32),
        1 - lat % 2,
        mem % 2,
        mem // 2,
    ])

    to_near, to_left, to_right, p, g = call(
        start_kernel, "start",
        (strip(0), pack, pack, shape(perturbations.shape, BF16), whole),
        (place, *(pltpu.with_memory_space_constraint(a, pltpu.HBM) for a in (perturbations, increment, taper_norm))),
        (pltpu.VMEM(whole.shape, F32), pltpu.VMEM(whole.shape, F32), pltpu.SemaphoreType.DMA((rows // HALO, 3))),
        specs=[smem] + [hbm] * 3,
    )
    near = lax.ppermute(to_near, "lat", [(i, i ^ 1) for i in range(count)])
    left = shifted(to_right, "lon", 1, True)
    right = shifted(to_left, "lon", -1, True)

    values = shape((rows, fine, *tile), F32)
    own_values, own_products, to_fields, to_sides, back = call(
        prepare_kernel, "prepare",
        (
            values, values,
            shape((members * cols + LANES, fine * LANES), BF16),
            shape((2 * LANES, fine * LANES), BF16),
            shape((fine * LANES, cols), BF16),
        ),
        (p, g),
        (
            pltpu.VMEM((rows * levels, members * cols), BF16),
            pltpu.VMEM((rows * levels, 2 * cols), BF16),
            pltpu.VMEM((2 * cols, fine * LANES), BF16),
        ),
    )

    p, g, own_values = lax.optimization_barrier((p, g, own_values))
    side = shape(((HALO + NEAR) * levels, LANES), BF16)
    to_far, to_near_sides = call(
        far_kernel, "far", (strip(1), side), (place, p, g, left, right), specs=[smem] + [vmem] * 4
    )
    far = lax.ppermute(to_far, "lat", [(i, (i + 1 - 2 * (1 - i % 2)) % count) for i in range(count)])
    near_sides = lax.ppermute(to_near_sides, "lat", [(i, i ^ 1) for i in range(count)])
    own_values, to_far = lax.optimization_barrier((own_values, to_far))

    part = shape((levels // 2, rows - 2 * HALO, cols), F32)
    keep, send, edges, edge_values = call(
        inner_kernel, "inner",
        (part, part, shape((2, PASSES, 4, fine + 4, *tile), F32), shape((2, HALO, fine, *tile), F32)),
        (place, own_values, own_products, taper_norm, left, right, to_sides, back, kappa),
        (
            pltpu.VMEM((rows, fine + 4, *tile), F32),
            pltpu.VMEM((rows * levels, 2 * LANES), BF16),
            pltpu.VMEM((levels, rows - 2 * HALO, cols), F32),
        ),
        specs=[smem] + [vmem] * 8,
        cost=pl.CostEstimate(flops=INNER_FLOPS, bytes_accessed=1 << 20, transcendentals=0),
    )
    middle = over_plane(*over_core(keep, send))
    part = shape((levels // 2, 2 * HALO, cols), F32)
    keep, send = call(
        outer_kernel, "outer",
        (part, part),
        (
            place, taper_norm, near, far, near_sides, edges, edge_values,
            to_fields, back, kappa,
        ),
        (
            pltpu.VMEM((2, 2 * HALO, fine + 4, *tile), F32),
            pltpu.VMEM((2 * (HALO + NEAR) * levels, members * cols + LANES), BF16),
            pltpu.VMEM((levels, 2 * HALO, cols), F32),
        ),
        specs=[smem] + [vmem] * 9,
        cost=pl.CostEstimate(flops=OUTER_FLOPS, bytes_accessed=1 << 20, transcendentals=0),
    )
    outside = over_plane(*over_core(keep, send))
    return jnp.concatenate([outside[:, :HALO], middle, outside[:, HALO:]], axis=1)


def solution(mesh):
    return jax.shard_map(
        local,
        mesh=mesh,
        in_specs=(P("mem", None, "lat", "lon"), P(None, "lat", "lon"), P(None, "lat", "lon"), P()),
        out_specs=P("mem", "lat", "lon"),
        check_vma=False,
    )
```

```python
import jax
import jax.numpy as jnp
from jax import lax
from jax.experimental import pallas as pl
from jax.experimental.pallas import tpu as pltpu
from jax.sharding import PartitionSpec as P

PASSES = 8
HALO = 2 * PASSES
LANES = 128
NEAR = 4
INNER_FLOPS = 4 * 10**9
OUTER_FLOPS = 4 * 10**9
BF16 = jnp.bfloat16
F32 = jnp.float32


def roll(x, shift):
    shift = shift % LANES
    return pltpu.roll(x, shift, x.ndim - 1) if shift else x


def lane_of(shape):
    return lax.broadcasted_iota(jnp.int32, shape, len(shape) - 1)


def split(value):
    hi = value.astype(BF16)
    return hi, (value - hi.astype(F32)).astype(BF16)


def target_column(lane, first, members, cols):
    chunks = LANES // members
    fine = (cols + 2 * HALO) // chunks
    return fine * (lane & (chunks - 1)) + first - HALO, lane >> (chunks.bit_length() - 1)


def fill_selectors(wanted, to_fields, to_weights, to_sides, back, members, cols):
    fine = back.shape[0] // LANES
    nowhere = -4 * LANES

    def mark(hit):
        return jnp.where(hit, 1.0, 0.0).astype(BF16)

    for first in wanted:
        lanes = slice(first * LANES, (first + 1) * LANES)
        column, member = target_column(lax.broadcasted_iota(jnp.int32, (1, LANES), 1), first, members, cols)
        marked = mark(lax.broadcasted_iota(jnp.int32, (cols, LANES), 0) == column)
        for m in range(members):
            to_fields[m * cols : (m + 1) * cols, lanes] = marked * mark(member == m)
        for part in range(2):
            to_weights[part * cols : (part + 1) * cols, lanes] = marked
        for ref, base, count, offsets in (
            (to_fields, members * cols, LANES, (0,)), (to_sides, 0, 2 * LANES, (0, LANES // 2)),
        ):
            row = lax.broadcasted_iota(jnp.int32, (count, LANES), 0)
            after = column - cols + count // 2
            at = jnp.where(column < 0, column + HALO, jnp.where(column >= cols, after, nowhere)) + HALO * member
            hit = row == at
            for offset in offsets[1:]:
                hit = hit | (row == at + offset)
            ref[base : base + count, lanes] = mark(hit)
        shape = (LANES, cols)
        column, _ = target_column(lax.broadcasted_iota(jnp.int32, shape, 0), first, members, cols)
        back[lanes, :] = mark(lax.broadcasted_iota(jnp.int32, shape, 1) == column)


def facing(value):
    return jnp.swapaxes(value.astype(F32), 0, 1)


def write_strip(out, p, g, pick, order):
    members, levels, _, cols = p.shape

    def put(pair, lanes, field, first=0):
        rows = slice((first + 2 * pair) * levels, (first + 2 * pair + 2) * levels)
        both = jnp.concatenate([field[order[2 * pair]], field[order[2 * pair + 1]]], axis=0)
        out[rows, lanes] = both.astype(BF16)

    for half in range(2):
        lanes = slice(half * LANES, (half + 1) * LANES)
        weight = g[:, pick, lanes]
        for m in range(members):
            to = slice(m * cols + half * LANES, m * cols + (half + 1) * LANES)
            product = facing(p[m, :, pick, lanes].astype(F32) * weight)
            rest = product - product.astype(BF16).astype(F32)
            for pair in range(HALO // 2):
                put(pair, to, product)
            for pair in range(NEAR // 2):
                put(pair, to, rest, HALO)


def write_sides(out, lanes, left, right, pick, order):
    levels = left.shape[0]
    left, right = facing(left[:, pick, :]), facing(right[:, pick, :])
    lane = lane_of(left.shape)
    half = LANES // 2
    product = jnp.where(lane < half, left, roll(right, half))
    rest = jnp.where(lane < half, roll(left, half), right)
    for count, first, field in ((HALO, 0, product), (NEAR, HALO, rest)):
        for pair in range(count // 2):
            rows = slice((first + 2 * pair) * levels, (first + 2 * pair + 2) * levels)
            both = jnp.concatenate([field[order[2 * pair]], field[order[2 * pair + 1]]], axis=0)
            out[rows, lanes] = both.astype(BF16)


def start_kernel(place, p_hbm, increment_hbm, taper_hbm, to_near, to_left, to_right, p, g, taper, increment, sems):
    members, levels, rows, cols = p.shape
    copies = []
    for i in (0, rows // HALO - 1, *range(1, rows // HALO - 1)):
        pick = slice(i * HALO, (i + 1) * HALO)
        copies.append((pick, [
            pltpu.make_async_copy(p_hbm.at[:, :, pick, :], p.at[:, :, pick, :], sems.at[i, 0]),
            pltpu.make_async_copy(increment_hbm.at[:, pick, :], increment.at[:, pick, :], sems.at[i, 1]),
            pltpu.make_async_copy(taper_hbm.at[:, pick, :], taper.at[:, pick, :], sems.at[i, 2]),
        ]))
    for _, group in copies:
        for copy in group:
            copy.start()

    def packed(pick, column, shift):
        products = [p[m, :, pick, column].astype(F32) * g[:, pick, column] for m in range(members)]
        products += [product - product.astype(BF16).astype(F32) for product in products]
        lane = lane_of(products[0].shape)
        total = jnp.zeros_like(products[0])
        for e, product in enumerate(products):
            inside = (lane >= HALO * e) & (lane < HALO * (e + 1))
            total = jnp.where(inside, roll(product, shift + HALO * e), total)
        return total.astype(BF16)

    for k, (pick, group) in enumerate(copies):
        for copy in group:
            copy.wait()
        g[:, pick, :] = increment[:, pick, :] * taper[:, pick, :]
        if k < 2:
            order = range(HALO) if k == 0 else range(HALO - 1, -1, -1)

            @pl.when(place[1] == k)
            def _():
                write_strip(to_near, p, g, pick, order)
        to_left[:, pick, :] = packed(pick, slice(0, LANES), 0)
        to_right[:, pick, :] = packed(pick, slice(cols - LANES, cols), HALO)


def far_kernel(place, p, g, left, right, to_far):
    members, _, rows, cols = p.shape
    for k in range(2):
        pick = slice(k * (rows - HALO), k * (rows - HALO) + HALO)
        order = range(HALO) if k == 0 else range(HALO - 1, -1, -1)

        @pl.when(place[1] != k)
        def _():
            write_strip(to_far, p, g, pick, order)
            write_sides(to_far, slice(members * cols, members * cols + LANES), left, right, pick, order)


def near_sides_kernel(place, left, right, to_near_sides):
    rows = left.shape[1]
    for k in range(2):
        pick = slice(k * (rows - HALO), k * (rows - HALO) + HALO)
        order = range(HALO) if k == 0 else range(HALO - 1, -1, -1)

        @pl.when(place[1] == k)
        def _():
            write_sides(to_near_sides, slice(0, LANES), left, right, pick, order)


def turned(value):
    levels, rows, lanes = value.shape
    return jnp.swapaxes(value.astype(F32), 0, 1).reshape(rows * levels, lanes)


def factors(kappa, count):
    denominator = 1.0 + 4.0 * kappa
    scale = kappa / denominator
    for _ in range(4):
        scale = scale * scale
    return 1.0 / kappa, denominator / (kappa * kappa), scale / (count - 1)


def row_of(ref, *where):
    return lambda c: ref[(*where, c + 2)]


def first_sweep(x, x_next, v, linear, fine):
    v_next = {c: x(c) + x_next(c + 1) for c in range(-2, fine + 1)}
    if v is None:
        return v_next, None
    u = {c: linear * x(c) + v[c] + v_next[c - 1] for c in range(-1, fine + 1)}
    return v_next, u


def second_sweep(x, u, u_next, q, constant, fine):
    q_next = {c: u[c] + u_next[c + 1] for c in range(-1, fine)}
    if q is None:
        return q_next, None
    return q_next, [constant * x(c) + q[c] + q_next[c - 1] for c in range(fine)]


def wrap_columns(source, target, fine):
    for c in (0, 1):
        target(fine + c, roll(source(c), -1))
        target(c - 2, roll(source(fine - 2 + c), 1))


def finish(sums, back, scale, taper_of, write, levels):
    hi, lo = split(sums)
    total = jnp.dot(hi, back, preferred_element_type=F32) + jnp.dot(lo, back, preferred_element_type=F32)
    count = total.shape[0] // levels
    for half in range(total.shape[1] // LANES):
        lanes = slice(half * LANES, (half + 1) * LANES)
        part = total[:, lanes].reshape(count, levels, LANES) * scale
        natural = jnp.swapaxes(part, 0, 1) * taper_of(lanes)
        write(natural, lanes)


def to_owner(place, natural, ordered, pick, lanes, levels):
    core, plane = place[2], place[3]
    for level in range(levels):
        other_core = jnp.where(core == level // 2 % 2, 0, 1)
        other_plane = jnp.where(plane == level // 4, 0, 1)
        ordered[levels // 2 * other_core + 2 * other_plane + level % 2, pick, lanes] = natural[level]


def dot(a, b):
    return jnp.dot(a, b, preferred_element_type=F32)


def prepare_kernel(p, g, own_values, own_products, to_fields, to_sides, back, fields, weights, to_weights):
    members, levels, rows, cols = p.shape
    fine = back.shape[0] // LANES

    def fill(first):
        wanted = range(first, min(first + 2, fine))
        fill_selectors(wanted, to_fields, to_weights, to_sides, back, members, cols)

    fill(0)
    for i in range(rows // HALO):
        pick = slice(i * HALO, (i + 1) * HALO)
        out = slice(i * HALO * levels, (i + 1) * HALO * levels)
        for half in range(cols // LANES):
            lanes = slice(half * LANES, (half + 1) * LANES)
            for m in range(members):
                to = slice(m * cols + half * LANES, m * cols + (half + 1) * LANES)
                fields[out, to] = turned(p[m, :, pick, lanes]).astype(BF16)
            hi, lo = split(turned(g[:, pick, lanes]))
            weights[out, lanes] = hi
            weights[out, cols + half * LANES : cols + (half + 1) * LANES] = lo
    for first in range(0, fine, 2):
        width = min(2, fine - first)
        lanes = slice(first * LANES, (first + width) * LANES)
        fill(first + 2)
        field = dot(fields[...], to_fields[: members * cols, lanes])
        weight = dot(weights[...], to_weights[:, lanes])
        product = field * weight
        for k in range(width):
            pick = slice(k * LANES, (k + 1) * LANES)
            own_values[:, first + k] = field[:, pick].reshape(rows, levels, LANES)
            own_products[:, first + k] = product[:, pick].reshape(rows, levels, LANES)


def inner_kernel(
    place, values, own_products, taper, left, right, to_sides, back, kappa,
    keep, send, edges, edge_values,
    x, packs, ordered,
):
    levels, rows, cols = taper.shape
    fine = x.shape[1] - 4
    members = LANES * fine // (cols + 2 * HALO)
    for i in range(rows // HALO):
        out = slice(i * HALO * levels, (i + 1) * HALO * levels)
        for side, ref in enumerate((left, right)):
            lanes = slice(side * LANES, (side + 1) * LANES)
            packs[out, lanes] = turned(ref[:, i * HALO : (i + 1) * HALO, :]).astype(BF16)
    for first in range(0, fine, 2):
        width = min(2, fine - first)
        beside = dot(packs[...], to_sides[:, first * LANES : (first + width) * LANES])
        for k in range(width):
            pick = slice(k * LANES, (k + 1) * LANES)
            x[:, 2 + first + k] = own_products[:, first + k] + beside[:, pick].reshape(rows, levels, LANES)
    upper, lower = place[1], 1 - place[1]
    for k in range(HALO):
        edge_values[upper, k] = values[k]
        edge_values[lower, k] = values[rows - 1 - k]

    linear, constant, scale = factors(kappa[...], 4 * members)

    def wrap(row):
        def target(c, value):
            x[row, c + 2] = value

        wrap_columns(row_of(x, row), target, fine)

    def wrap_first(row, _):
        wrap(row)
        return 0

    lax.fori_loop(0, rows, wrap_first, 0, unroll=True)

    for turn in range(PASSES):
        low = 2 * turn
        start, count = low + 2, rows - 4 * turn - 4
        for k in range(4):
            edges[upper, turn, k] = x[low + k]
            edges[lower, turn, k] = x[rows - 1 - low - k]

        v, _ = first_sweep(row_of(x, start - 2), row_of(x, start - 1), None, linear, fine)
        v, u = first_sweep(row_of(x, start - 1), row_of(x, start), v, linear, fine)
        v, u_next = first_sweep(row_of(x, start), row_of(x, start + 1), v, linear, fine)
        q, _ = second_sweep(None, u, u_next, None, constant, fine)
        u = u_next
        for i in range(start, start + count):
            v, u_next = first_sweep(row_of(x, i + 1), row_of(x, i + 2), v, linear, fine)
            q, y = second_sweep(row_of(x, i), u, u_next, q, constant, fine)
            u = u_next
            for c in range(fine):
                x[i, c + 2] = y[c]
            if turn < PASSES - 1:
                wrap(i)

    def last(i):
        first = i * HALO
        from_row = first + HALO
        product = jnp.concatenate(
            [
                (x[slice(from_row, from_row + HALO), c + 2] * values[slice(from_row, from_row + HALO), c]).reshape(HALO * levels, LANES)
                for c in range(fine)
            ],
            axis=1,
        )
        pick = slice(first, first + HALO)
        finish(
            product, back[...], scale,
            lambda lanes: taper[:, slice(from_row, from_row + HALO), lanes],
            lambda natural, lanes: to_owner(place, natural, ordered, pick, lanes, levels),
            levels,
        )

    for i in range((rows - 2 * HALO) // HALO):
        last(i)
    keep[...] = ordered[: levels // 2]
    send[...] = ordered[levels // 2 :]


def outer_kernel(
    place, taper, near, far, near_sides, edges, edge_values, to_fields, back, kappa,
    keep, send,
    x, fields, ordered,
):
    levels, rows, cols = taper.shape
    fine = edge_values.shape[2]
    members = LANES * fine // (cols + 2 * HALO)
    linear, constant, scale = factors(kappa[...], 4 * members)
    inside = jnp.where(place[0] == 1, 0.0, 1.0).astype(F32)
    count, main = near.shape
    fields[:count, :main] = near[...]
    fields[:count, main:] = near_sides[...]
    fields[count:, :] = far[...]
    for first in range(0, fine, 2):
        width = min(2, fine - first)
        field = dot(fields[...], to_fields[:, first * LANES : (first + width) * LANES])
        for k in range(width):
            part = field[:, k * LANES : (k + 1) * LANES].reshape(2, HALO + NEAR, levels, LANES)
            for edge in range(2):
                for distance in range(HALO):
                    value = part[edge, distance]
                    if distance < NEAR:
                        value = value + part[edge, HALO + distance]
                    if edge == 1 and distance == 0:
                        value = value * inside
                    x[edge, HALO - 1 - distance, 2 + first + k] = value

    def wrap(edge, row):
        def target(c, value):
            x[edge, row, c + 2] = value

        wrap_columns(row_of(x, edge, row), target, fine)

    for row in range(HALO):
        for edge in range(2):
            wrap(edge, row)

    for turn in range(PASSES):
        low = 2 * turn
        for edge in range(2):
            def row_at(row):
                if row < low + HALO:
                    return row_of(x, edge, row)
                return row_of(edges, edge, turn, row - low - HALO)

            v = u = q = None
            for i in range(low, low + HALO + 3):
                v, u_next = first_sweep(row_at(i), row_at(i + 1), v, linear, fine)
                if u_next is None:
                    continue
                if edge == 1 and i == HALO - 1:
                    u_next = {c: part * inside for c, part in u_next.items()}
                if u is not None:
                    q, y = second_sweep(row_at(i - 1), u, u_next, q, constant, fine)
                    if y is not None:
                        for c in range(fine):
                            x[edge, i - 1, c + 2] = y[c] * inside if edge == 1 and i == HALO else y[c]
                u = u_next
            if turn < PASSES - 1:
                for row in range(low + 2, low + HALO + 2):
                    wrap(edge, row)

    for edge in range(2):
        order = range(HALO) if edge == 0 else range(HALO - 1, -1, -1)
        slot = place[1] if edge == 0 else 1 - place[1]
        product = jnp.concatenate(
            [
                jnp.concatenate([x[slot, HALO + k, c + 2] * edge_values[slot, k, c] for k in order], axis=0)
                for c in range(fine)
            ],
            axis=1,
        )
        own = slice(edge * (rows - HALO), edge * (rows - HALO) + HALO)
        pick = slice(edge * HALO, (edge + 1) * HALO)
        finish(
            product, back[...], scale,
            lambda lanes: taper[:, own, lanes],
            lambda natural, lanes: to_owner(place, natural, ordered, pick, lanes, levels),
            levels,
        )
    keep[...] = ordered[: levels // 2]
    send[...] = ordered[levels // 2 :]


def shifted(value, axis, step, wrap):
    count = lax.axis_size(axis)
    pairs = [(i, (i + step) % count) for i in range(count) if wrap or 0 <= i + step < count]
    return lax.ppermute(value, axis, pairs)


def over_core(keep, send):
    got = lax.ppermute(send, "mem", [(i, i ^ 1) for i in range(4)])
    return keep[:2] + got[:2], keep[2:] + got[2:]


def over_plane(here, there):
    return here + lax.ppermute(there, "mem", [(i, i ^ 2) for i in range(4)])


def local(perturbations, increment, taper_norm, kappa):
    members, levels, rows, cols = perturbations.shape
    fine = (cols + 2 * HALO) * members // LANES
    shape = jax.ShapeDtypeStruct
    tile = (levels, LANES)
    vmem = pl.BlockSpec(memory_space=pltpu.VMEM)
    smem = pl.BlockSpec(memory_space=pltpu.SMEM)
    hbm = pl.BlockSpec(memory_space=pltpu.HBM)

    def call(kernel, name, outs, ins, scratch=(), specs=None, cost=None):
        return pl.pallas_call(
            kernel,
            out_shape=tuple(outs),
            in_specs=specs or [vmem] * len(ins),
            out_specs=(vmem,) * len(outs),
            scratch_shapes=list(scratch),
            compiler_params=pltpu.CompilerParams(vmem_limit_bytes=20 * 1024 * 1024),
            cost_estimate=cost,
            name=name,
        )(*ins)

    def strip(blocks):
        return shape(((HALO + NEAR) * levels, members * cols + blocks * LANES), BF16)

    pack = shape((levels, rows, LANES), BF16)
    whole = shape((levels, rows, cols), F32)
    kappa = jnp.broadcast_to(kappa[:, None], tile)
    lat, mem = lax.axis_index("lat"), lax.axis_index("mem")
    count = lax.axis_size("lat")
    place = jnp.stack([
        ((lat == 0) | (lat == count - 1)).astype(jnp.int32),
        1 - lat % 2,
        mem % 2,
        mem // 2,
    ])

    to_near, to_left, to_right, p, g = call(
        start_kernel, "start",
        (strip(0), pack, pack, shape(perturbations.shape, BF16), whole),
        (place, *(pltpu.with_memory_space_constraint(a, pltpu.HBM) for a in (perturbations, increment, taper_norm))),
        (pltpu.VMEM(whole.shape, F32), pltpu.VMEM(whole.shape, F32), pltpu.SemaphoreType.DMA((rows // HALO, 3))),
        specs=[smem] + [hbm] * 3,
    )
    near = lax.ppermute(to_near, "lat", [(i, i ^ 1) for i in range(count)])
    left = shifted(to_right, "lon", 1, True)
    right = shifted(to_left, "lon", -1, True)

    values = shape((rows, fine, *tile), F32)
    own_values, own_products, to_fields, to_sides, back = call(
        prepare_kernel, "prepare",
        (
            values, values,
            shape((members * cols + LANES, fine * LANES), BF16),
            shape((2 * LANES, fine * LANES), BF16),
            shape((fine * LANES, cols), BF16),
        ),
        (p, g),
        (
            pltpu.VMEM((rows * levels, members * cols), BF16),
            pltpu.VMEM((rows * levels, 2 * cols), BF16),
            pltpu.VMEM((2 * cols, fine * LANES), BF16),
        ),
    )

    p, g, own_values = lax.optimization_barrier((p, g, own_values))
    side = shape(((HALO + NEAR) * levels, LANES), BF16)
    (to_far,) = call(far_kernel, "far", (strip(1),), (place, p, g, left, right), specs=[smem] + [vmem] * 4)
    far = lax.ppermute(to_far, "lat", [(i, (i + 1 - 2 * (1 - i % 2)) % count) for i in range(count)])
    left, right, to_far = lax.optimization_barrier((left, right, to_far))
    (to_near_sides,) = call(
        near_sides_kernel, "near_sides", (side,), (place, left, right), specs=[smem] + [vmem] * 2
    )
    near_sides = lax.ppermute(to_near_sides, "lat", [(i, i ^ 1) for i in range(count)])
    own_values, near, to_near_sides = lax.optimization_barrier((own_values, near, to_near_sides))

    part = shape((levels // 2, rows - 2 * HALO, cols), F32)
    keep, send, edges, edge_values = call(
        inner_kernel, "inner",
        (part, part, shape((2, PASSES, 4, fine + 4, *tile), F32), shape((2, HALO, fine, *tile), F32)),
        (place, own_values, own_products, taper_norm, left, right, to_sides, back, kappa),
        (
            pltpu.VMEM((rows, fine + 4, *tile), F32),
            pltpu.VMEM((rows * levels, 2 * LANES), BF16),
            pltpu.VMEM((levels, rows - 2 * HALO, cols), F32),
        ),
        specs=[smem] + [vmem] * 8,
        cost=pl.CostEstimate(flops=INNER_FLOPS, bytes_accessed=1 << 20, transcendentals=0),
    )
    middle = over_plane(*over_core(keep, send))
    part = shape((levels // 2, 2 * HALO, cols), F32)
    keep, send = call(
        outer_kernel, "outer",
        (part, part),
        (
            place, taper_norm, near, far, near_sides, edges, edge_values,
            to_fields, back, kappa,
        ),
        (
            pltpu.VMEM((2, 2 * HALO, fine + 4, *tile), F32),
            pltpu.VMEM((2 * (HALO + NEAR) * levels, members * cols + LANES), BF16),
            pltpu.VMEM((levels, 2 * HALO, cols), F32),
        ),
        specs=[smem] + [vmem] * 9,
        cost=pl.CostEstimate(flops=OUTER_FLOPS, bytes_accessed=1 << 20, transcendentals=0),
    )
    outside = over_plane(*over_core(keep, send))
    return jnp.concatenate([outside[:, :HALO], middle, outside[:, HALO:]], axis=1)


def solution(mesh):
    return jax.shard_map(
        local,
        mesh=mesh,
        in_specs=(P("mem", None, "lat", "lon"), P(None, "lat", "lon"), P(None, "lat", "lon"), P()),
        out_specs=P("mem", "lat", "lon"),
        check_vma=False,
    )
```

```python
import jax
import jax.numpy as jnp
from jax import lax
from jax.experimental import pallas as pl
from jax.experimental.pallas import tpu as pltpu
from jax.sharding import PartitionSpec as P

PASSES = 8
HALO = 2 * PASSES
LANES = 128
NEAR = 4
INNER_FLOPS = 4 * 10**9
OUTER_FLOPS = 4 * 10**9
BF16 = jnp.bfloat16
F32 = jnp.float32


def roll(x, shift):
    shift = shift % LANES
    return pltpu.roll(x, shift, x.ndim - 1) if shift else x


def lane_of(shape):
    return lax.broadcasted_iota(jnp.int32, shape, len(shape) - 1)


def split(value):
    hi = value.astype(BF16)
    return hi, (value - hi.astype(F32)).astype(BF16)


def target_column(lane, first, members, cols):
    chunks = LANES // members
    fine = (cols + 2 * HALO) // chunks
    return fine * (lane & (chunks - 1)) + first - HALO, lane >> (chunks.bit_length() - 1)


def fill_selectors(wanted, to_fields, to_weights, to_sides, back, members, cols):
    fine = back.shape[0] // LANES
    nowhere = -4 * LANES

    def mark(hit):
        return jnp.where(hit, 1.0, 0.0).astype(BF16)

    for first in wanted:
        lanes = slice(first * LANES, (first + 1) * LANES)
        column, member = target_column(lax.broadcasted_iota(jnp.int32, (1, LANES), 1), first, members, cols)
        marked = mark(lax.broadcasted_iota(jnp.int32, (cols, LANES), 0) == column)
        for m in range(members):
            to_fields[m * cols : (m + 1) * cols, lanes] = marked * mark(member == m)
        for part in range(2):
            to_weights[part * cols : (part + 1) * cols, lanes] = marked
        for ref, base, count, offsets in (
            (to_fields, members * cols, LANES, (0,)), (to_sides, 0, 2 * LANES, (0, LANES // 2)),
        ):
            row = lax.broadcasted_iota(jnp.int32, (count, LANES), 0)
            after = column - cols + count // 2
            at = jnp.where(column < 0, column + HALO, jnp.where(column >= cols, after, nowhere)) + HALO * member
            hit = row == at
            for offset in offsets[1:]:
                hit = hit | (row == at + offset)
            ref[base : base + count, lanes] = mark(hit)
        shape = (LANES, cols)
        column, _ = target_column(lax.broadcasted_iota(jnp.int32, shape, 0), first, members, cols)
        back[lanes, :] = mark(lax.broadcasted_iota(jnp.int32, shape, 1) == column)


def facing(value):
    return jnp.swapaxes(value.astype(F32), 0, 1)


def write_strip(out, p, g, pick, order, sides=None):
    members, levels, _, cols = p.shape

    def put(pair, lanes, field, first=0):
        rows = slice((first + 2 * pair) * levels, (first + 2 * pair + 2) * levels)
        both = jnp.concatenate([field[order[2 * pair]], field[order[2 * pair + 1]]], axis=0)
        out[rows, lanes] = both.astype(BF16)

    for half in range(2):
        lanes = slice(half * LANES, (half + 1) * LANES)
        weight = g[:, pick, lanes]
        for m in range(members):
            to = slice(m * cols + half * LANES, m * cols + (half + 1) * LANES)
            product = facing(p[m, :, pick, lanes].astype(F32) * weight)
            rest = product - product.astype(BF16).astype(F32)
            for pair in range(HALO // 2):
                put(pair, to, product)
            for pair in range(NEAR // 2):
                put(pair, to, rest, HALO)
    if sides is not None:
        left, right = (facing(side[:, pick, :]) for side in sides)
        lane = lane_of(left.shape)
        half = LANES // 2
        to = slice(members * cols, members * cols + LANES)
        product = jnp.where(lane < half, left, roll(right, half))
        rest = jnp.where(lane < half, roll(left, half), right)
        for pair in range(HALO // 2):
            put(pair, to, product)
        for pair in range(NEAR // 2):
            put(pair, to, rest, HALO)


def start_kernel(
    place, p_hbm, increment_hbm, taper_hbm,
    to_near, to_left, to_right, p, g, to_fields, to_weights, to_sides, back,
    taper, increment, sems,
):
    members, levels, rows, cols = p.shape
    copies = []
    for i in (0, rows // HALO - 1, *range(1, rows // HALO - 1)):
        pick = slice(i * HALO, (i + 1) * HALO)
        copies.append((pick, [
            pltpu.make_async_copy(p_hbm.at[:, :, pick, :], p.at[:, :, pick, :], sems.at[i, 0]),
            pltpu.make_async_copy(increment_hbm.at[:, pick, :], increment.at[:, pick, :], sems.at[i, 1]),
            pltpu.make_async_copy(taper_hbm.at[:, pick, :], taper.at[:, pick, :], sems.at[i, 2]),
        ]))
    for _, group in copies:
        for copy in group:
            copy.start()
    fill_selectors(range(back.shape[0] // LANES), to_fields, to_weights, to_sides, back, members, cols)

    def packed(pick, column, shift):
        products = [p[m, :, pick, column].astype(F32) * g[:, pick, column] for m in range(members)]
        products += [product - product.astype(BF16).astype(F32) for product in products]
        lane = lane_of(products[0].shape)
        total = jnp.zeros_like(products[0])
        for e, product in enumerate(products):
            inside = (lane >= HALO * e) & (lane < HALO * (e + 1))
            total = jnp.where(inside, roll(product, shift + HALO * e), total)
        return total.astype(BF16)

    for k, (pick, group) in enumerate(copies):
        for copy in group:
            copy.wait()
        g[:, pick, :] = increment[:, pick, :] * taper[:, pick, :]
        if k < 2:
            order = range(HALO) if k == 0 else range(HALO - 1, -1, -1)

            @pl.when(place[1] == k)
            def _():
                write_strip(to_near, p, g, pick, order)
        to_left[:, pick, :] = packed(pick, slice(0, LANES), 0)
        to_right[:, pick, :] = packed(pick, slice(cols - LANES, cols), HALO)


def far_kernel(place, p, g, left, right, to_far):
    rows = p.shape[2]
    for k in range(2):
        pick = slice(k * (rows - HALO), k * (rows - HALO) + HALO)
        order = range(HALO) if k == 0 else range(HALO - 1, -1, -1)

        @pl.when(place[1] != k)
        def _():
            write_strip(to_far, p, g, pick, order, (left, right))


def corners_kernel(strip, to_left, to_right):
    count, main = strip.shape
    members = main // (2 * LANES)
    for first in range(0, count, 16):
        rows = slice(first, first + 16)
        lane = lane_of((16, LANES))
        for ref, half, base, shift in ((to_left, 0, LANES // 2, 0), (to_right, 1, 0, HALO)):
            total = jnp.zeros((16, LANES), F32)
            for m in range(members):
                field = strip[rows, (2 * m + half) * LANES : (2 * m + half + 1) * LANES].astype(F32)
                at = base + HALO * m
                total = jnp.where((lane >= at) & (lane < at + HALO), roll(field, shift + at), total)
            ref[rows, :] = total.astype(BF16)


def turned(value):
    levels, rows, lanes = value.shape
    return jnp.swapaxes(value.astype(F32), 0, 1).reshape(rows * levels, lanes)


def factors(kappa, count):
    denominator = 1.0 + 4.0 * kappa
    scale = kappa / denominator
    for _ in range(4):
        scale = scale * scale
    return 1.0 / kappa, denominator / (kappa * kappa), scale / (count - 1)


def row_of(ref, *where):
    return lambda c: ref[(*where, c + 2)]


def first_sweep(x, x_next, v, linear, fine):
    v_next = {c: x(c) + x_next(c + 1) for c in range(-2, fine + 1)}
    if v is None:
        return v_next, None
    u = {c: linear * x(c) + v[c] + v_next[c - 1] for c in range(-1, fine + 1)}
    return v_next, u


def second_sweep(x, u, u_next, q, constant, fine):
    q_next = {c: u[c] + u_next[c + 1] for c in range(-1, fine)}
    if q is None:
        return q_next, None
    return q_next, [constant * x(c) + q[c] + q_next[c - 1] for c in range(fine)]


def wrap_columns(source, target, fine):
    for c in (0, 1):
        target(fine + c, roll(source(c), -1))
        target(c - 2, roll(source(fine - 2 + c), 1))


def finish(sums, back, scale, taper_of, write, levels):
    hi, lo = split(sums)
    total = jnp.dot(hi, back, preferred_element_type=F32) + jnp.dot(lo, back, preferred_element_type=F32)
    count = total.shape[0] // levels
    for half in range(total.shape[1] // LANES):
        lanes = slice(half * LANES, (half + 1) * LANES)
        part = total[:, lanes].reshape(count, levels, LANES) * scale
        natural = jnp.swapaxes(part, 0, 1) * taper_of(lanes)
        write(natural, lanes)


def to_owner(place, natural, ordered, pick, lanes, levels):
    core, plane = place[2], place[3]
    for level in range(levels):
        other_core = jnp.where(core == level // 2 % 2, 0, 1)
        other_plane = jnp.where(plane == level // 4, 0, 1)
        ordered[levels // 2 * other_core + 2 * other_plane + level % 2, pick, lanes] = natural[level]


def dot(a, b):
    return jnp.dot(a, b, preferred_element_type=F32)


def prepare_kernel(p, g, to_fields, to_weights, own_values, own_products, fields, weights):
    members, levels, rows, cols = p.shape
    fine = to_fields.shape[1] // LANES
    for i in range(rows // HALO):
        pick = slice(i * HALO, (i + 1) * HALO)
        out = slice(i * HALO * levels, (i + 1) * HALO * levels)
        for half in range(cols // LANES):
            lanes = slice(half * LANES, (half + 1) * LANES)
            for m in range(members):
                to = slice(m * cols + half * LANES, m * cols + (half + 1) * LANES)
                fields[out, to] = turned(p[m, :, pick, lanes]).astype(BF16)
            hi, lo = split(turned(g[:, pick, lanes]))
            weights[out, lanes] = hi
            weights[out, cols + half * LANES : cols + (half + 1) * LANES] = lo
    for first in range(0, fine, 2):
        width = min(2, fine - first)
        lanes = slice(first * LANES, (first + width) * LANES)
        field = dot(fields[...], to_fields[: members * cols, lanes])
        weight = dot(weights[...], to_weights[:, lanes])
        product = field * weight
        for k in range(width):
            pick = slice(k * LANES, (k + 1) * LANES)
            own_values[:, first + k] = field[:, pick].reshape(rows, levels, LANES)
            own_products[:, first + k] = product[:, pick].reshape(rows, levels, LANES)


def inner_kernel(
    place, values, own_products, taper, left, right, to_sides, back, kappa,
    keep, send, edges, edge_values,
    x, packs, ordered,
):
    levels, rows, cols = taper.shape
    fine = x.shape[1] - 4
    members = LANES * fine // (cols + 2 * HALO)
    for i in range(rows // HALO):
        out = slice(i * HALO * levels, (i + 1) * HALO * levels)
        for side, ref in enumerate((left, right)):
            lanes = slice(side * LANES, (side + 1) * LANES)
            packs[out, lanes] = turned(ref[:, i * HALO : (i + 1) * HALO, :]).astype(BF16)
    for first in range(0, fine, 2):
        width = min(2, fine - first)
        beside = dot(packs[...], to_sides[:, first * LANES : (first + width) * LANES])
        for k in range(width):
            pick = slice(k * LANES, (k + 1) * LANES)
            x[:, 2 + first + k] = own_products[:, first + k] + beside[:, pick].reshape(rows, levels, LANES)
    upper, lower = place[1], 1 - place[1]
    for k in range(HALO):
        edge_values[upper, k] = values[k]
        edge_values[lower, k] = values[rows - 1 - k]

    linear, constant, scale = factors(kappa[...], 4 * members)

    def wrap(row):
        def target(c, value):
            x[row, c + 2] = value

        wrap_columns(row_of(x, row), target, fine)

    def wrap_first(row, _):
        wrap(row)
        return 0

    lax.fori_loop(0, rows, wrap_first, 0, unroll=True)

    for turn in range(PASSES):
        low = 2 * turn
        start, count = low + 2, rows - 4 * turn - 4
        for k in range(4):
            edges[upper, turn, k] = x[low + k]
            edges[lower, turn, k] = x[rows - 1 - low - k]

        v, _ = first_sweep(row_of(x, start - 2), row_of(x, start - 1), None, linear, fine)
        v, u = first_sweep(row_of(x, start - 1), row_of(x, start), v, linear, fine)
        v, u_next = first_sweep(row_of(x, start), row_of(x, start + 1), v, linear, fine)
        q, _ = second_sweep(None, u, u_next, None, constant, fine)
        u = u_next
        for i in range(start, start + count):
            v, u_next = first_sweep(row_of(x, i + 1), row_of(x, i + 2), v, linear, fine)
            q, y = second_sweep(row_of(x, i), u, u_next, q, constant, fine)
            u = u_next
            for c in range(fine):
                x[i, c + 2] = y[c]
            if turn < PASSES - 1:
                wrap(i)

    def last(i):
        first = i * HALO
        from_row = first + HALO
        product = jnp.concatenate(
            [
                (x[slice(from_row, from_row + HALO), c + 2] * values[slice(from_row, from_row + HALO), c]).reshape(HALO * levels, LANES)
                for c in range(fine)
            ],
            axis=1,
        )
        pick = slice(first, first + HALO)
        finish(
            product, back[...], scale,
            lambda lanes: taper[:, slice(from_row, from_row + HALO), lanes],
            lambda natural, lanes: to_owner(place, natural, ordered, pick, lanes, levels),
            levels,
        )

    for i in range((rows - 2 * HALO) // HALO):
        last(i)
    keep[...] = ordered[: levels // 2]
    send[...] = ordered[levels // 2 :]


def outer_kernel(
    place, taper, near, far, left, right, edges, edge_values, to_fields, back, kappa,
    keep, send,
    x, fields, ordered,
):
    levels, rows, cols = taper.shape
    fine = edge_values.shape[2]
    members = LANES * fine // (cols + 2 * HALO)
    linear, constant, scale = factors(kappa[...], 4 * members)
    inside = jnp.where(place[0] == 1, 0.0, 1.0).astype(F32)
    count, main = near.shape
    fields[:count, :main] = near[...]
    fields[:count, main:] = left[...] + right[...]
    fields[count:, :] = far[...]
    for first in range(0, fine, 2):
        width = min(2, fine - first)
        field = dot(fields[...], to_fields[:, first * LANES : (first + width) * LANES])
        for k in range(width):
            part = field[:, k * LANES : (k + 1) * LANES].reshape(2, HALO + NEAR, levels, LANES)
            for edge in range(2):
                for distance in range(HALO):
                    value = part[edge, distance]
                    if distance < NEAR:
                        value = value + part[edge, HALO + distance]
                    if edge == 1 and distance == 0:
                        value = value * inside
                    x[edge, HALO - 1 - distance, 2 + first + k] = value

    def wrap(edge, row):
        def target(c, value):
            x[edge, row, c + 2] = value

        wrap_columns(row_of(x, edge, row), target, fine)

    for row in range(HALO):
        for edge in range(2):
            wrap(edge, row)

    for turn in range(PASSES):
        low = 2 * turn
        for edge in range(2):
            def row_at(row):
                if row < low + HALO:
                    return row_of(x, edge, row)
                return row_of(edges, edge, turn, row - low - HALO)

            v = u = q = None
            for i in range(low, low + HALO + 3):
                v, u_next = first_sweep(row_at(i), row_at(i + 1), v, linear, fine)
                if u_next is None:
                    continue
                if edge == 1 and i == HALO - 1:
                    u_next = {c: part * inside for c, part in u_next.items()}
                if u is not None:
                    q, y = second_sweep(row_at(i - 1), u, u_next, q, constant, fine)
                    if y is not None:
                        for c in range(fine):
                            x[edge, i - 1, c + 2] = y[c] * inside if edge == 1 and i == HALO else y[c]
                u = u_next
            if turn < PASSES - 1:
                for row in range(low + 2, low + HALO + 2):
                    wrap(edge, row)

    for edge in range(2):
        order = range(HALO) if edge == 0 else range(HALO - 1, -1, -1)
        slot = place[1] if edge == 0 else 1 - place[1]
        product = jnp.concatenate(
            [
                jnp.concatenate([x[slot, HALO + k, c + 2] * edge_values[slot, k, c] for k in order], axis=0)
                for c in range(fine)
            ],
            axis=1,
        )
        own = slice(edge * (rows - HALO), edge * (rows - HALO) + HALO)
        pick = slice(edge * HALO, (edge + 1) * HALO)
        finish(
            product, back[...], scale,
            lambda lanes: taper[:, own, lanes],
            lambda natural, lanes: to_owner(place, natural, ordered, pick, lanes, levels),
            levels,
        )
    keep[...] = ordered[: levels // 2]
    send[...] = ordered[levels // 2 :]


def shifted(value, axis, step, wrap):
    count = lax.axis_size(axis)
    pairs = [(i, (i + step) % count) for i in range(count) if wrap or 0 <= i + step < count]
    return lax.ppermute(value, axis, pairs)


def over_core(keep, send):
    got = lax.ppermute(send, "mem", [(i, i ^ 1) for i in range(4)])
    return keep[:2] + got[:2], keep[2:] + got[2:]


def over_plane(here, there):
    return here + lax.ppermute(there, "mem", [(i, i ^ 2) for i in range(4)])


def local(perturbations, increment, taper_norm, kappa):
    members, levels, rows, cols = perturbations.shape
    fine = (cols + 2 * HALO) * members // LANES
    shape = jax.ShapeDtypeStruct
    tile = (levels, LANES)
    vmem = pl.BlockSpec(memory_space=pltpu.VMEM)
    smem = pl.BlockSpec(memory_space=pltpu.SMEM)
    hbm = pl.BlockSpec(memory_space=pltpu.HBM)

    def call(kernel, name, outs, ins, scratch=(), specs=None, cost=None):
        return pl.pallas_call(
            kernel,
            out_shape=tuple(outs),
            in_specs=specs or [vmem] * len(ins),
            out_specs=(vmem,) * len(outs),
            scratch_shapes=list(scratch),
            compiler_params=pltpu.CompilerParams(vmem_limit_bytes=20 * 1024 * 1024),
            cost_estimate=cost,
            name=name,
        )(*ins)

    def strip(blocks):
        return shape(((HALO + NEAR) * levels, members * cols + blocks * LANES), BF16)

    pack = shape((levels, rows, LANES), BF16)
    whole = shape((levels, rows, cols), F32)
    kappa = jnp.broadcast_to(kappa[:, None], tile)
    lat, mem = lax.axis_index("lat"), lax.axis_index("mem")
    count = lax.axis_size("lat")
    place = jnp.stack([
        ((lat == 0) | (lat == count - 1)).astype(jnp.int32),
        1 - lat % 2,
        mem % 2,
        mem // 2,
    ])

    to_near, to_left, to_right, p, g, to_fields, to_weights, to_sides, back = call(
        start_kernel, "start",
        (
            strip(0), pack, pack, shape(perturbations.shape, BF16), whole,
            shape((members * cols + LANES, fine * LANES), BF16),
            shape((2 * cols, fine * LANES), BF16),
            shape((2 * LANES, fine * LANES), BF16),
            shape((fine * LANES, cols), BF16),
        ),
        (place, *(pltpu.with_memory_space_constraint(a, pltpu.HBM) for a in (perturbations, increment, taper_norm))),
        (pltpu.VMEM(whole.shape, F32), pltpu.VMEM(whole.shape, F32), pltpu.SemaphoreType.DMA((rows // HALO, 3))),
        specs=[smem] + [hbm] * 3,
    )
    near = lax.ppermute(to_near, "lat", [(i, i ^ 1) for i in range(count)])
    left = shifted(to_right, "lon", 1, True)
    right = shifted(to_left, "lon", -1, True)

    values = shape((rows, fine, *tile), F32)
    own_values, own_products = call(
        prepare_kernel, "prepare",
        (values, values),
        (p, g, to_fields, to_weights),
        (pltpu.VMEM((rows * levels, members * cols), BF16), pltpu.VMEM((rows * levels, 2 * cols), BF16)),
    )
    p, g, own_values = lax.optimization_barrier((p, g, own_values))
    (to_far,) = call(far_kernel, "far", (strip(1),), (place, p, g, left, right), specs=[smem] + [vmem] * 4)
    far = lax.ppermute(to_far, "lat", [(i, (i + 1 - 2 * (1 - i % 2)) % count) for i in range(count)])
    near, to_far = lax.optimization_barrier((near, to_far))
    side = shape(((HALO + NEAR) * levels, LANES), BF16)
    to_left, to_right = call(corners_kernel, "corners", (side, side), (near,))
    near_left = shifted(to_right, "lon", 1, True)
    near_right = shifted(to_left, "lon", -1, True)
    own_values, to_left = lax.optimization_barrier((own_values, to_left))

    part = shape((levels // 2, rows - 2 * HALO, cols), F32)
    keep, send, edges, edge_values = call(
        inner_kernel, "inner",
        (part, part, shape((2, PASSES, 4, fine + 4, *tile), F32), shape((2, HALO, fine, *tile), F32)),
        (place, own_values, own_products, taper_norm, left, right, to_sides, back, kappa),
        (
            pltpu.VMEM((rows, fine + 4, *tile), F32),
            pltpu.VMEM((rows * levels, 2 * LANES), BF16),
            pltpu.VMEM((levels, rows - 2 * HALO, cols), F32),
        ),
        specs=[smem] + [vmem] * 8,
        cost=pl.CostEstimate(flops=INNER_FLOPS, bytes_accessed=1 << 20, transcendentals=0),
    )
    middle = over_plane(*over_core(keep, send))
    part = shape((levels // 2, 2 * HALO, cols), F32)
    keep, send = call(
        outer_kernel, "outer",
        (part, part),
        (
            place, taper_norm, near, far, near_left, near_right, edges, edge_values,
            to_fields, back, kappa,
        ),
        (
            pltpu.VMEM((2, 2 * HALO, fine + 4, *tile), F32),
            pltpu.VMEM((2 * (HALO + NEAR) * levels, members * cols + LANES), BF16),
            pltpu.VMEM((levels, 2 * HALO, cols), F32),
        ),
        specs=[smem] + [vmem] * 10,
        cost=pl.CostEstimate(flops=OUTER_FLOPS, bytes_accessed=1 << 20, transcendentals=0),
    )
    outside = over_plane(*over_core(keep, send))
    return jnp.concatenate([outside[:, :HALO], middle, outside[:, HALO:]], axis=1)


def solution(mesh):
    return jax.shard_map(
        local,
        mesh=mesh,
        in_specs=(P("mem", None, "lat", "lon"), P(None, "lat", "lon"), P(None, "lat", "lon"), P()),
        out_specs=P("mem", "lat", "lon"),
        check_vma=False,
    )
```
